32 devices in a mesh: slab: 8 (over z, y), walk: 4 (over x, core).
Axes of the slice: x: 2, y: 2, z: 4, core: 2. Of those that a mesh axis runs over, the one named last changes fastest.
Arguments:
- bias_grid: float32 [32, 512, 512], P('slab', 'walk'), may hold values from 0 to 12, as said below
- hill_slab: int32 [64, 64, 1], P(('slab', 'walk')), may hold values from 0 to 7; in each aligned block of 128 rows (0 to 127, 128 to 255, ..., all dimensions but the last counted through in order) at most 64 rows name the same one
- hill_row: int32 [64, 64], P(('slab', 'walk')), may hold values from 0 to 3
- hill_col: int32 [64, 64], P(('slab', 'walk')), may hold values from 0 to 511
- hill_depth: int32 [64, 64], P(('slab', 'walk')), may hold values from 0 to 511
- hill_level: int32 [64, 64], P(('slab', 'walk')), may hold values from 0 to 7
- hill_count: int32 [64], P(('slab', 'walk')), may hold values from 1 to 64
- height_levels: float32 [8], replicated, may hold values from 0.5 to 2
Outputs:
- new_bias: float32 [32, 512, 512], P('slab', 'walk')
- free_energy: float32 [32, 512, 512], P('slab', 'walk')
The draws below stay inside these ranges and needn't reach their ends.
Inputs may be any that keep to these rules, and one draw needn't show every extreme that they name: `bias_grid`: the bias is not negative. `hill_slab`: among the hills of one device's walkers (128 hills in a row of the flattened walkers and hills), no slab is named more than 64 times, and in some such blocks one slab is named exactly 64 times.
All inputs are finite; a program needn't handle non-finite values.
Results may differ from the reference program's by a relative error of at most 0.000082.
Values sent between devices are 32-bit elements; how exact they have to be, the bound alone decides.
A program may use at most 64 MiB of HBM per device.

```python
import math
import jax
import jax.numpy as jnp
import numpy as np
from jax import lax

ROWS_DEV = 4
DEPTH = 512
HILLS = 64
WALKERS_DEV = 2
LEVELS = 8
REACH = 8
CAP = 64
GRID_ROWS = 32
GRID_COLS = 512
WALKERS = 64
N_SLAB = 8


def draw_bias_grid(key, part):
    rough_key = jax.random.fold_in(key, 11)
    row_key = jax.random.fold_in(key, 12)
    col_key = jax.random.fold_in(key, 13)
    depth_key = jax.random.fold_in(key, 14)
    rough_cells = jax.random.uniform(rough_key, (GRID_ROWS, GRID_COLS, DEPTH), jnp.float32)
    row_scale = jnp.exp(jax.random.uniform(row_key, (GRID_ROWS, 1, 1), jnp.float32, math.log(0.5), math.log(4.0)))
    col_scale = jnp.exp(jax.random.uniform(col_key, (1, GRID_COLS, 1), jnp.float32, math.log(0.8), math.log(2.0)))
    depth_scale = jnp.exp(jax.random.uniform(depth_key, (1, 1, DEPTH), jnp.float32, math.log(0.8), math.log(1.25)))
    rough_part = rough_cells * row_scale * col_scale * depth_scale
    return rough_part


def with_ends(values, stream_key, low, top_value):
    longest = values.shape.index(max(values.shape))
    spots = []
    for shift in (0, 1):
        where = [jax.random.randint(jax.random.fold_in(stream_key, axis), (), 0, length) for axis, length in enumerate(values.shape)]
        where[longest] = (where[longest] + shift) % values.shape[longest]
        spots.append(tuple(where))
    return values.at[spots[0]].set(low).at[spots[1]].set(top_value)


def shared_out(own_key, own, number, rows, number_of, top, bound, slope):
    sequence = jax.random.permutation(own_key, number_of)
    heavy_load, usual = shares(number_of, rows * top, bound, slope, True), shares(number_of, rows * top, bound, slope, False)
    places = jnp.arange(number_of)

    def named(sizes, offset_by):
        used = int((sizes > 0).sum())
        fixed = max(1, used // 4)
        moved = fixed + (places - fixed + offset_by * (used - fixed)) % max(1, number_of - fixed)
        return jnp.zeros((number_of,), jnp.int32).at[sequence[jnp.where(places < fixed, places, moved)]].set(jnp.asarray(sizes, jnp.int32))

    sizes = jnp.where(number % 4 == 0, named(heavy_load, number // 4), named(usual, number - number // 4 - 1))
    mixed = jax.random.permutation(jax.random.fold_in(own, 3), number_of)
    source_of, taker = mixed[0:number_of // 2 * 2:2], mixed[1:number_of // 2 * 2:2]
    slack = jnp.minimum(sizes[source_of] - 1, bound - sizes[taker]) // 2
    slack = jnp.where((source_of == sequence[0]) | (taker == sequence[0]) | (sizes[taker] == 0), 0, jnp.maximum(slack, 0))
    moved = jax.random.randint(jax.random.fold_in(own, 4), (number_of // 2,), 0, 1 << 20) % (slack + 1)
    sizes = sizes.at[source_of].add(-moved).at[taker].add(moved)
    members = jnp.searchsorted(jnp.cumsum(sizes), jnp.arange(rows * top), side="right").astype(jnp.int32)
    table = members.reshape(top, rows).T
    table = table[jax.random.permutation(jax.random.fold_in(own, 1), rows)]
    offset_by = jax.random.randint(jax.random.fold_in(own, 2), (rows, 1), 0, top)
    return jnp.take_along_axis(table, (jnp.arange(top)[None, :] + offset_by) % top, axis=1)


def shares(count, total, bound, skew, full):
    portions = [(1 << 20) // math.isqrt(rank ** skew) + 1 for rank in range(1, count + 1)]
    largest = bound if full else min(bound, max(-(-total // count), total * portions[0] // sum(portions)))
    least = 1 if total - largest >= count - 1 else 0
    counts, surplus = [largest] + [least] * (count - 1), total - largest - least * (count - 1)
    while surplus > 0:
        free = [i for i in range(1, count) if counts[i] < largest] or [i for i in range(1, count) if counts[i] < bound]
        whole, budget = sum([portions[i] for i in free]), surplus
        for i in free:
            extra = min(bound - counts[i], max(1, budget * portions[i] // whole), surplus)
            counts[i] = counts[i] + extra
            surplus = surplus - extra
    return np.array(counts)


def setup_inputs(seed: int = 0) -> dict:
    streams_of = jax.random.split(jax.random.key(seed), 9)
    bias_grid = draw_bias_grid(jax.random.fold_in(streams_of[8], 71), 0)
    hill_slab_keys = jax.random.split(jax.random.fold_in(streams_of[1], 1), WALKERS * HILLS // (WALKERS_DEV * HILLS))
    hill_slab_turns = jax.random.permutation(jax.random.fold_in(streams_of[1], 3), WALKERS * HILLS // (WALKERS_DEV * HILLS))
    hill_slab = jax.vmap(lambda own, number: shared_out(jax.random.fold_in(streams_of[1], 2), own, number, WALKERS_DEV * HILLS, N_SLAB, 1, CAP, 2))(hill_slab_keys, hill_slab_turns).reshape((WALKERS, HILLS, 1))
    hill_row = with_ends(jax.random.randint(streams_of[2], (WALKERS, HILLS), 0, ROWS_DEV), jax.random.fold_in(streams_of[2], 1), 0, ROWS_DEV - 1).astype(jnp.int32)
    hill_col = with_ends(jax.random.randint(streams_of[3], (WALKERS, HILLS), 0, GRID_COLS), jax.random.fold_in(streams_of[3], 1), 0, GRID_COLS - 1).astype(jnp.int32)
    hill_depth = with_ends(jax.random.randint(streams_of[4], (WALKERS, HILLS), 0, DEPTH), jax.random.fold_in(streams_of[4], 1), 0, DEPTH - 1).astype(jnp.int32)
    hill_level = with_ends(jax.random.randint(streams_of[5], (WALKERS, HILLS), 0, LEVELS), jax.random.fold_in(streams_of[5], 1), 0, LEVELS - 1).astype(jnp.int32)
    hill_count = with_ends(jax.random.randint(streams_of[6], (WALKERS,), 1, HILLS + 1), jax.random.fold_in(streams_of[6], 1), 1, HILLS).astype(jnp.int32)
    height_levels = jnp.clip(jnp.exp(jax.random.uniform(streams_of[7], (LEVELS,), jnp.float32, math.log(0.5), math.log(2.0))), 0.5, 2.0)
    return dict(bias_grid=bias_grid, hill_slab=hill_slab, hill_row=hill_row, hill_col=hill_col, hill_depth=hill_depth, hill_level=hill_level, hill_count=hill_count, height_levels=height_levels)


BASE_HEIGHT = 1.2
TEMPER = 4.0
SIGMA_SHARE = 0.3125
FREE_SCALE = 10.0 / 9.0


def fold_axis(padded, radius, extent, axis):
    inner = lax.slice_in_dim(padded, radius, radius + extent, axis=axis)
    low_part = lax.slice_in_dim(padded, 0, radius, axis=axis)
    high_part = lax.slice_in_dim(padded, radius + extent, 2 * radius + extent, axis=axis)
    head = lax.slice_in_dim(inner, 0, radius, axis=axis) + high_part
    middle = lax.slice_in_dim(inner, radius, extent - radius, axis=axis)
    tail = lax.slice_in_dim(inner, extent - radius, extent, axis=axis) + low_part
    return jnp.concatenate([head, middle, tail], axis=axis)


def reference(bias_grid, hill_slab, hill_row, hill_col, hill_depth, hill_level, hill_count, height_levels):
    grid_rows, grid_cols, grid_depth = bias_grid.shape
    radius = REACH
    centre_row = (hill_slab[:, :, 0] * ROWS_DEV + hill_row).reshape(-1).astype(jnp.int32)
    centre_col = hill_col.reshape(-1).astype(jnp.int32)
    centre_depth = hill_depth.reshape(-1).astype(jnp.int32)
    is_live = (jnp.arange(HILLS, dtype=jnp.int32)[None, :] < hill_count[:, None]).reshape(-1)
    level_match = hill_level.reshape(-1)[:, None] == jnp.arange(LEVELS, dtype=jnp.int32)[None, :]
    base_height = jnp.sum(jnp.where(level_match, height_levels[None, :], 0.0), axis=1)
    base_height = jnp.where(is_live, BASE_HEIGHT * base_height, 0.0)
    height = base_height * jnp.exp(-bias_grid[centre_row, centre_col, centre_depth] / TEMPER)
    spread = SIGMA_SHARE * radius
    distance = (jnp.arange(2 * radius, dtype=jnp.int32) - radius).astype(jnp.float32)
    profile = jnp.exp(-(distance * distance) / (2.0 * spread * spread))

    def add_hill(padded, hill):
        weight, row_at, col_at, depth_at = hill
        patch = (weight * profile)[:, None, None] * profile[None, :, None] * profile[None, None, :]
        current = lax.dynamic_slice(padded, (row_at, col_at, depth_at), (2 * radius, 2 * radius, 2 * radius))
        return lax.dynamic_update_slice(padded, current + patch, (row_at, col_at, depth_at)), None

    start = jnp.zeros((grid_rows + 2 * radius, grid_cols + 2 * radius, grid_depth + 2 * radius), jnp.float32)
    padded, unused = lax.scan(add_hill, start, (height, centre_row, centre_col, centre_depth))
    folded = fold_axis(padded, radius, grid_rows, 0)
    folded = fold_axis(folded, radius, grid_cols, 1)
    deposit = fold_axis(folded, radius, grid_depth, 2)
    new_bias = bias_grid + deposit
    highest = jnp.max(new_bias)
    free_energy = FREE_SCALE * (highest - new_bias)
    return new_bias, free_energy
```

```python
import functools
import math

import jax
import jax.numpy as jnp
from jax import lax
from jax.experimental import pallas as pl
from jax.experimental.pallas import tpu as pltpu
from jax.sharding import PartitionSpec as P

BASE_HEIGHT = 1.2
TEMPER = 4.0
SIGMA_SHARE = 0.3125
FREE_SCALE = 10.0 / 9.0


def from_behind(block, axis, distance):
    devices = range(lax.axis_size(axis))
    route = [((i - distance) % len(devices), i) for i in devices]
    return lax.ppermute(block, axis, route)


def gaussian(position, centre, extent, radius):
    offset = jnp.mod(position - centre + extent // 2, extent) - extent // 2
    inside = (offset >= -radius) & (offset < radius)
    spread = SIGMA_SHARE * radius
    distance = offset.astype(jnp.float32)
    return jnp.where(inside, jnp.exp(-(distance * distance) / (2.0 * spread * spread)), 0.0)


def deposit(row_ids, col_ids, depth_ids, hill_lists, grid_rows, grid_cols, grid_depth, radius):
    slot_total = hill_lists.shape[1]
    block_size = math.gcd(slot_total, 256)
    row_count = row_ids.shape[0]
    col_count = col_ids.shape[0]
    depth_count = depth_ids.shape[0]

    def one_block(carry_sum, index):
        portion = lax.dynamic_slice_in_dim(hill_lists, index * block_size, block_size, 1)
        row_gauss = (
            gaussian(row_ids[:, None], portion[1].astype(jnp.int32)[None, :], grid_rows, radius)
            * portion[0][None, :]
        )
        col_gauss = gaussian(
            col_ids[:, None], portion[2].astype(jnp.int32)[None, :], grid_cols, radius
        )
        depth_gauss = gaussian(
            depth_ids[None, :], portion[3].astype(jnp.int32)[:, None], grid_depth, radius
        )
        plane_gauss = (row_gauss[:, None, :] * col_gauss[None, :, :]).reshape(
            row_count * col_count, block_size
        )
        added = jnp.dot(
            plane_gauss,
            depth_gauss,
            precision=lax.Precision.HIGHEST,
            preferred_element_type=jnp.float32,
        )
        return (carry_sum + added, None)

    start = jnp.zeros((row_count * col_count, depth_count), jnp.float32)
    result, unused = lax.scan(one_block, start, jnp.arange(slot_total // block_size))
    return result.reshape(row_count, col_count, depth_count)


def by_collectives(
    bias_grid, hill_slab, hill_row, hill_col, hill_depth, hill_level, hill_count, height_levels
):
    rows_dev, cols_dev, depth_bins = bias_grid.shape
    slab_count = lax.axis_size("slab")
    walk_count = lax.axis_size("walk")
    radius = 2 * rows_dev
    grid_rows = rows_dev * slab_count
    grid_cols = cols_dev * walk_count
    walkers_dev, hill_slots = hill_row.shape
    sent_rows = walkers_dev * hill_slots
    capacity = max(2, 4 * sent_rows // slab_count)
    target = hill_slab[:, :, 0].reshape(-1)
    centre_row = target * rows_dev + hill_row.reshape(-1)
    is_live = (
        lax.broadcasted_iota(jnp.int32, (walkers_dev, hill_slots), 1) < hill_count[:, None]
    ).reshape(-1)
    level_match = hill_level.reshape(-1)[:, None] == lax.broadcasted_iota(
        jnp.int32, (1, height_levels.shape[0]), 1
    )
    base_height = jnp.sum(jnp.where(level_match, height_levels[None, :], 0.0), axis=1)
    base_height = jnp.where(is_live, BASE_HEIGHT * base_height, 0.0)
    same_slab = target[:, None] == target[None, :]
    earlier = lax.broadcasted_iota(jnp.int32, (sent_rows, sent_rows), 1) < lax.broadcasted_iota(
        jnp.int32, (sent_rows, sent_rows), 0
    )
    slot_rank = jnp.sum((same_slab & earlier).astype(jnp.int32), axis=1)
    slot_place = target * capacity + slot_rank
    placing = (
        slot_place[:, None] == lax.broadcasted_iota(jnp.int32, (1, slab_count * capacity), 1)
    ).astype(jnp.float32)
    fields = jnp.stack(
        [
            base_height,
            centre_row.astype(jnp.float32),
            hill_col.reshape(-1).astype(jnp.float32),
            hill_depth.reshape(-1).astype(jnp.float32),
        ]
    )
    outgoing = jnp.dot(
        fields, placing, precision=lax.Precision.HIGHEST, preferred_element_type=jnp.float32
    )
    outgoing = outgoing.reshape(4, slab_count, capacity)
    arrived = lax.all_to_all(outgoing, "slab", split_axis=1, concat_axis=1, tiled=True).reshape(
        4, slab_count * capacity
    )
    shared = lax.all_gather(arrived, "walk", axis=1, tiled=True)
    slab_index = lax.axis_index("slab")
    walk_index = lax.axis_index("walk")
    local_row = jnp.clip(shared[1].astype(jnp.int32) - slab_index * rows_dev, 0, rows_dev - 1)
    local_col = shared[2].astype(jnp.int32) - walk_index * cols_dev
    local_depth = jnp.clip(shared[3].astype(jnp.int32), 0, depth_bins - 1)
    owned = (local_col >= 0) & (local_col < cols_dev)
    flat_place = (
        local_row * cols_dev + jnp.clip(local_col, 0, cols_dev - 1)
    ) * depth_bins + local_depth
    picked = bias_grid.reshape(-1)[flat_place]
    centre_value = lax.psum(jnp.where(owned, picked, 0.0), "walk")
    height = shared[0] * jnp.exp(-centre_value / TEMPER)
    hill_lists = jnp.stack([height, shared[1], shared[2], shared[3]])
    col_ids = walk_index * cols_dev + lax.broadcasted_iota(jnp.int32, (cols_dev,), 0)
    depth_ids = lax.broadcasted_iota(jnp.int32, (depth_bins,), 0)
    collected = [hill_lists]
    for offset in (-2, -1, 1, 2):
        collected.append(from_behind(hill_lists, "slab", offset))
    row_ids = slab_index * rows_dev + lax.broadcasted_iota(jnp.int32, (rows_dev,), 0)
    added = deposit(
        row_ids,
        col_ids,
        depth_ids,
        jnp.concatenate(collected, axis=1),
        grid_rows,
        grid_cols,
        depth_bins,
        radius,
    )
    new_bias = bias_grid + added
    highest = lax.pmax(jnp.max(new_bias), ("slab", "walk"))
    free_energy = FREE_SCALE * (highest - new_bias)
    return (new_bias, free_energy)


LANES = 128
F32 = jnp.float32
BF16 = jnp.bfloat16
MESH = pl.DeviceIdType.MESH
NT = (((1,), (1,)), ((), ()))


def wrapped(offset, extent):
    offset = jnp.where(offset >= extent // 2, offset - extent, offset)
    return jnp.where(offset < -(extent // 2), offset + extent, offset)


def profile(offset, radius):
    spread = SIGMA_SHARE * radius
    value = jnp.exp(-(offset * offset) / (2.0 * spread * spread))
    return jnp.where((offset >= -radius) & (offset < radius), value, 0.0)


def halves(value):
    high = value.astype(BF16)
    return high, (value - high.astype(F32)).astype(BF16)


def iota(shape, dim):
    return lax.broadcasted_iota(jnp.int32, shape, dim).astype(F32)


def whole_iota(shape, dim):
    return lax.broadcasted_iota(jnp.int32, shape, dim)


OFFSETS = [(i, j) for i in (-2, -1, 0, 1, 2) for j in (-1, 0, 1)]
HERE = OFFSETS.index((0, 0))


def mesh_steps(slabs, walks):
    devices = slabs * walks
    me = lax.axis_index("slab") * walks + lax.axis_index("walk")

    def place(step):
        other = lax.rem(me + step, devices)
        return (other // walks, lax.rem(other, walks))

    steps = sorted(range(1, devices), key=lambda step: -min(step, devices - step))
    return place, steps


def greet(place, steps):
    barrier = pltpu.get_barrier_semaphore()
    for step in steps:
        pl.semaphore_signal(barrier, inc=1, device_id=place(step), device_id_type=MESH)
    return barrier


def to_all(source, target, send, recv, place, steps):
    return [
        pltpu.make_async_remote_copy(
            source, target, send.at[step], recv.at[step],
            device_id=place(step), device_id_type=MESH,
        )
        for step in steps
    ]


def to_near(source, tables, send, recv, slabs, walks):
    slab, walk = lax.axis_index("slab"), lax.axis_index("walk")
    copies = []
    for n, (i, j) in sorted(enumerate(OFFSETS), key=lambda item: -abs(item[1][0])):
        if n == HERE:
            continue
        device = (lax.rem(slab - i + slabs, slabs), lax.rem(walk - j + walks, walks))
        copies.append(
            pltpu.make_async_remote_copy(
                source, tables.at[n], send.at[n], recv.at[n],
                device_id=device, device_id_type=MESH,
            )
        )
    return copies


def owner_of(at_row, at_col, rows, cols, slabs, walks):
    slab_of = jnp.floor(at_row / rows) - lax.axis_index("slab").astype(F32)
    walk_of = jnp.floor(at_col / cols) - lax.axis_index("walk").astype(F32)
    slab_of = jnp.where(slab_of < -2, slab_of + slabs, slab_of)
    slab_of = jnp.where(slab_of > 2, slab_of - slabs, slab_of)
    walk_of = jnp.where(walk_of < -1, walk_of + walks, walk_of)
    walk_of = jnp.where(walk_of > 1, walk_of - walks, walk_of)
    inside = (jnp.abs(slab_of) <= 2) & (jnp.abs(walk_of) <= 1)
    return jnp.where(inside, (slab_of + 2) * 3 + walk_of + 1, -1.0)


def lane_tops(value):
    most = jnp.max(value, axis=0, keepdims=True)
    top = most[:, 0:LANES]
    for i in range(1, value.shape[1] // LANES):
        top = jnp.maximum(top, most[:, i * LANES : (i + 1) * LANES])
    return top


def as_column(row):
    return jnp.broadcast_to(row, (LANES, LANES)).T


def squeeze(mask, rank):
    lane = whole_iota(mask.shape, 1)
    code = (lane - rank.astype(jnp.int32)) * LANES + lane + LANES * LANES
    code = jnp.where(mask, code, 0)
    step = 1
    while step < LANES:
        came = pltpu.roll(code, LANES - step, axis=1)
        bit = step * LANES
        stays = jnp.where((code & bit) != 0, 0, code)
        code = jnp.where((came & bit) != 0, came, stays)
        step *= 2
    return code & (LANES - 1)


def window_kernel(
    slabs, walks, rows, cols, own_blocks, close_blocks,
    bias_in, slab_in, row_in, col_in, depth_in, level_in, count_in, table_in,
    new_ref, top_ref, bias_ref, hills_ref, flag_ref,
    slab_ref, row_ref, col_ref, depth_ref, level_ref, count_ref, table_ref, in_sems,
    mine, hills, bias_high, bias_low, picked, tables, chosen,
    left_high, left_low, right_high, right_low, near, peak, peaks,
    a_send, a_recv, b_send, b_recv, c_send, c_recv,
):
    devices = slabs * walks
    cells, depth = bias_ref.shape
    radius = 2 * rows
    grid_rows, grid_cols = slabs * rows, walks * cols
    slab = lax.axis_index("slab")
    walk = lax.axis_index("walk")
    me = slab * walks + walk
    first_row = (slab * rows).astype(F32)
    first_col = (walk * cols).astype(F32)
    place, steps = mesh_steps(slabs, walks)
    barrier = greet(place, steps)

    inputs = (
        (slab_in, slab_ref), (row_in, row_ref), (col_in, col_ref), (depth_in, depth_ref),
        (level_in, level_ref), (count_in, count_ref), (table_in, table_ref), (bias_in, bias_ref),
    )
    fetches = [
        pltpu.make_async_copy(there, here, in_sems.at[i])
        for i, (there, here) in enumerate(inputs)
    ]
    for fetch in fetches:
        fetch.start()
    for fetch in fetches[:-1]:
        fetch.wait()

    def in_row(ref):
        value = ref[...].astype(F32)
        return jnp.concatenate([value[i : i + 1] for i in range(value.shape[0])], axis=1)

    slots = row_ref.shape[1]
    lane = iota((1, LANES), 1)
    live = jnp.zeros((1, LANES), F32)
    for i in range(row_ref.shape[0]):
        inside = (lane >= i * slots) & (lane < i * slots + count_ref[i].astype(F32))
        live = jnp.where(inside, 1.0, live)
    level = in_row(level_ref)
    base = jnp.zeros((1, LANES), F32)
    for i in range(table_ref.shape[0]):
        base = jnp.where((level == i) & (live > 0), BASE_HEIGHT * table_ref[i], base)
    fields = (base, in_row(slab_ref) * rows + in_row(row_ref), in_row(col_ref), in_row(depth_ref))
    for i, field in enumerate(fields):
        mine[i : i + 1, :] = field
        hills[me, i : i + 1, :] = field

    pl.semaphore_wait(barrier, devices - 1)
    sent = pl.ds(0, len(fields))
    a_copies = to_all(mine.at[sent], hills.at[me, sent], a_send, a_recv, place, steps)
    for copy in a_copies:
        copy.start()

    fetches[-1].wait()
    high, low = halves(bias_ref[...])
    bias_high[...] = high
    bias_low[...] = low
    counting = jnp.concatenate(
        [
            jnp.where(iota((LANES, LANES), 0) < iota((LANES, LANES), 1), 1.0, 0.0),
            jnp.ones((LANES, LANES), F32),
        ],
        axis=1,
    ).astype(BF16)
    before = jnp.where(
        iota((devices, devices), 1) < iota((devices, devices), 0), 1.0, 0.0
    ).astype(BF16)
    lanes = whole_iota((devices, LANES), 1)

    for copy in a_copies:
        copy.wait_recv()

    all_base, all_row, all_col, all_depth = [hills[:, i, :] for i in range(4)]
    there = all_base > 0
    owner = jnp.where(there, owner_of(all_row, all_col, rows, cols, slabs, walks), -1.0)

    def ranks(masks):
        ones = [jnp.where(mask, 1.0, 0.0).astype(BF16) for mask in masks]
        both = jnp.dot(jnp.concatenate(ones, axis=0), counting, preferred_element_type=F32)
        ranked = [both[i * devices : (i + 1) * devices, :LANES] for i in range(len(masks))]
        counts = [both[i * devices : (i + 1) * devices, LANES:] for i in range(len(masks))]
        starts = jnp.dot(
            before, jnp.concatenate(counts, axis=1).astype(BF16), preferred_element_type=F32
        )
        starts = [starts[:, i * LANES : (i + 1) * LANES] for i in range(len(masks))]
        return ranked, counts, starts

    def gathering(mask, rank, count, start):
        start = start.astype(jnp.int32)
        moved = lanes - start
        index = jnp.take_along_axis(squeeze(mask, rank), moved & (LANES - 1), axis=1)

        def gather(values, blocks):
            taken = [jnp.take_along_axis(value, index, axis=1) for value in values]
            result = []
            for block in range(blocks):
                spot = moved + block * LANES
                valid = (spot >= 0) & (spot < count.astype(jnp.int32))
                result.append(
                    [jnp.sum(jnp.where(valid, t, 0.0), axis=0, keepdims=True) for t in taken]
                )
            return result

        return gather

    own_mask = owner == HERE
    (own_rank,), (own_count,), (own_start,) = ranks([own_mask])
    own_cell = (all_row - first_row) * cols + all_col - first_col
    own_lists = gathering(own_mask, own_rank, own_count, own_start)(
        [own_cell * depth + all_depth], own_blocks
    )
    own_code = jnp.concatenate([block[0] for block in own_lists], axis=1).astype(jnp.int32)
    own_width = own_blocks * LANES
    select = jnp.where(
        whole_iota((depth, own_width), 0) == (own_code & (depth - 1)), 1.0, 0.0
    ).astype(BF16)
    lines = jnp.dot(bias_high[...], select, preferred_element_type=F32)
    lines = lines + jnp.dot(bias_low[...], select, preferred_element_type=F32)
    wanted = own_code >> (depth.bit_length() - 1)
    hit = whole_iota((cells, own_width), 0) == wanted
    value = jnp.sum(jnp.where(hit, lines, 0.0), axis=0, keepdims=True)
    value = jnp.exp(-value / TEMPER)
    for block in range(own_blocks):
        picked[block : block + 1, :] = value[:, block * LANES : (block + 1) * LANES]

    b_copies = to_near(picked, tables, b_send, b_recv, slabs, walks)
    for copy in b_copies:
        copy.start()

    def past(away, extent, limit):
        away = away + (radius - 1)
        away = jnp.where(away < 0, away + extent, away)
        away = jnp.where(away >= extent, away - extent, away)
        return away < limit

    close = (
        there
        & past(all_row - first_row, grid_rows, rows + 2 * radius - 1)
        & past(all_col - first_col, grid_cols, cols + 2 * radius - 1)
    )
    masks = [owner == n for n in range(len(OFFSETS))] + [close]
    rank_list, count_list, start_list = ranks(masks)
    spot = jnp.zeros((devices, LANES), F32)
    for n in range(len(OFFSETS)):
        code = rank_list[n] + start_list[n] + n * own_width
        spot = jnp.where(masks[n], code, spot)
    over = jnp.maximum(
        own_start + own_count - own_width,
        start_list[-1] + count_list[-1] - close_blocks * LANES,
    )
    over = jnp.max(over, axis=(0, 1), keepdims=True)
    close_lists = gathering(close, rank_list[-1], count_list[-1], start_list[-1])(
        [all_base, all_row, all_col, all_depth, spot], close_blocks
    )
    depth_lane = iota((LANES, LANES), 1)
    col_id = iota((cols, LANES), 0)
    for block, parts in enumerate(close_lists):
        span = slice(block * LANES, (block + 1) * LANES)
        for i in (0, 1, 4):
            chosen[i, block : block + 1, :] = parts[i]
        at = as_column(parts[3])
        for i in range(depth // LANES):
            part = profile(wrapped(depth_lane + i * LANES - at, depth), radius)
            high, low = halves(part)
            right_high[span, i * LANES : (i + 1) * LANES] = high
            right_low[span, i * LANES : (i + 1) * LANES] = low
        near[:, span] = profile(wrapped(col_id + first_col - parts[2], grid_cols), radius)
    hills_ref[...] = hills[...]

    at_base, at_row = chosen[0], chosen[1]
    at_spot = chosen[4].astype(jnp.int32)
    at_lane = at_spot & (LANES - 1)
    at_table = at_spot >> (LANES.bit_length() - 1)
    row_parts = [
        at_base * profile(wrapped(first_row + r - at_row, grid_rows), radius) for r in range(rows)
    ]

    for copy in b_copies:
        copy.wait_recv()
    factor = jnp.zeros((close_blocks, LANES), F32)
    for n in range(len(OFFSETS)):
        for block in range(own_blocks):
            table = picked if n == HERE else tables.at[n]
            line = jnp.broadcast_to(table[block : block + 1, :], factor.shape)
            value = jnp.take_along_axis(line, at_lane, axis=1)
            factor = jnp.where(at_table == n * own_blocks + block, value, factor)
    row_parts = [factor * part for part in row_parts]
    for r in range(rows):
        for block in range(close_blocks):
            span = slice(block * LANES, (block + 1) * LANES)
            high, low = halves(near[:, span] * row_parts[r][block : block + 1])
            left_high[r * cols : (r + 1) * cols, span] = high
            left_low[r * cols : (r + 1) * cols, span] = low

    added = jnp.dot(left_high[...], right_high[...], preferred_element_type=F32)
    added += jnp.dot(left_low[...], right_high[...], preferred_element_type=F32)
    added += jnp.dot(left_high[...], right_low[...], preferred_element_type=F32)
    value = bias_ref[...] + added
    new_ref[...] = value
    top = jnp.where(over > 0, jnp.inf, lane_tops(value))
    peak[...] = top
    peaks[me] = top
    c_copies = to_all(peak, peaks.at[me], c_send, c_recv, place, steps)
    for copy in c_copies:
        copy.start()
    for copy in c_copies:
        copy.wait_recv()
    highest = jnp.max(peaks[...])
    top_ref[...] = jnp.broadcast_to(highest, top_ref.shape)
    flag_ref[0] = jnp.where(highest == jnp.inf, 1, 0)
    for copy in a_copies + b_copies + c_copies:
        copy.wait_send()


def by_kernel(own_blocks, close_blocks, slabs, walks, arrays):
    bias_grid, hill_slab, hill_row, hill_col, hill_depth, hill_level, hill_count, table = arrays
    rows, cols, depth = bias_grid.shape
    devices = slabs * walks
    total = close_blocks * LANES
    cells = rows * cols
    walkers = hill_row.shape
    vmem = pl.BlockSpec(memory_space=pltpu.VMEM)
    smem = pl.BlockSpec(memory_space=pltpu.SMEM)
    hbm = pl.BlockSpec(memory_space=pltpu.HBM)
    return pl.pallas_call(
        functools.partial(window_kernel, slabs, walks, rows, cols, own_blocks, close_blocks),
        out_shape=(
            jax.ShapeDtypeStruct((cells, depth), F32),
            jax.ShapeDtypeStruct((8, LANES), F32),
            jax.ShapeDtypeStruct((cells, depth), F32),
            jax.ShapeDtypeStruct((devices, 4, LANES), F32),
            jax.ShapeDtypeStruct((1,), jnp.int32),
        ),
        in_specs=[hbm] * 8,
        out_specs=(vmem, vmem, vmem, vmem, smem),
        scratch_shapes=[
            pltpu.VMEM(walkers, jnp.int32),
            pltpu.VMEM(walkers, jnp.int32),
            pltpu.VMEM(walkers, jnp.int32),
            pltpu.VMEM(walkers, jnp.int32),
            pltpu.VMEM(walkers, jnp.int32),
            pltpu.SMEM(hill_count.shape, jnp.int32),
            pltpu.SMEM(table.shape, F32),
            pltpu.SemaphoreType.DMA((8,)),
            pltpu.VMEM((4, LANES), F32),
            pltpu.VMEM((devices, 4, LANES), F32),
            pltpu.VMEM((cells, depth), BF16),
            pltpu.VMEM((cells, depth), BF16),
            pltpu.VMEM((own_blocks, LANES), F32),
            pltpu.VMEM((len(OFFSETS), own_blocks, LANES), F32),
            pltpu.VMEM((5, close_blocks, LANES), F32),
            pltpu.VMEM((cells, total), BF16),
            pltpu.VMEM((cells, total), BF16),
            pltpu.VMEM((total, depth), BF16),
            pltpu.VMEM((total, depth), BF16),
            pltpu.VMEM((cols, total), F32),
            pltpu.VMEM((1, LANES), F32),
            pltpu.VMEM((devices, 1, LANES), F32),
            pltpu.SemaphoreType.DMA((devices,)),
            pltpu.SemaphoreType.DMA((devices,)),
            pltpu.SemaphoreType.DMA((len(OFFSETS),)),
            pltpu.SemaphoreType.DMA((len(OFFSETS),)),
            pltpu.SemaphoreType.DMA((devices,)),
            pltpu.SemaphoreType.DMA((devices,)),
        ],
        compiler_params=pltpu.CompilerParams(
            collective_id=0, has_side_effects=True, vmem_limit_bytes=58 * 2**20
        ),
    )(
        bias_grid.reshape(cells, depth),
        hill_slab.reshape(hill_row.shape),
        hill_row,
        hill_col,
        hill_depth,
        hill_level,
        hill_count,
        table,
    )


def full_kernel(
    slabs, walks, rows, cols,
    bias_ref, hills_ref, new_ref, top_ref,
    bias_high, bias_low, picked, tables, peak, peaks,
    b_send, b_recv, c_send, c_recv,
):
    devices = slabs * walks
    cells, depth = bias_ref.shape
    radius = 2 * rows
    grid_rows, grid_cols = slabs * rows, walks * cols
    slab = lax.axis_index("slab")
    walk = lax.axis_index("walk")
    me = slab * walks + walk
    first_row = (slab * rows).astype(F32)
    first_col = (walk * cols).astype(F32)
    place, steps = mesh_steps(slabs, walks)
    barrier = greet(place, steps)
    high, low = halves(bias_ref[...])
    bias_high[...] = high
    bias_low[...] = low

    def pick(sender, carry):
        part = hills_ref[sender]
        cell = (part[1:2] - first_row) * cols + part[2:3] - first_col
        owner = owner_of(part[1:2], part[2:3], rows, cols, slabs, walks)
        cell = jnp.where(owner == HERE, cell, -1.0)
        select = jnp.where(iota((depth, LANES), 0) == part[3:4], 1.0, 0.0).astype(BF16)
        lines = jnp.dot(bias_high[...], select, preferred_element_type=F32)
        lines = lines + jnp.dot(bias_low[...], select, preferred_element_type=F32)
        hit = iota((cells, LANES), 0) == cell
        value = jnp.sum(jnp.where(hit, lines, 0.0), axis=0, keepdims=True)
        picked[pl.ds(sender, 1), :] = jnp.exp(-value / TEMPER)
        return carry

    lax.fori_loop(0, devices, pick, 0)
    pl.semaphore_wait(barrier, devices - 1)
    b_copies = to_near(picked, tables, b_send, b_recv, slabs, walks)
    for copy in b_copies:
        copy.start()
    tables[HERE] = picked[...]
    for copy in b_copies:
        copy.wait_recv()
    new_ref[...] = bias_ref[...]

    def add(sender, carry):
        part = hills_ref[sender]
        owner = owner_of(part[1:2], part[2:3], rows, cols, slabs, walks)
        height = jnp.zeros((1, LANES), F32)
        for n in range(len(OFFSETS)):
            height = jnp.where(owner == n, part[0:1] * tables[n, pl.ds(sender, 1), :], height)
        at = as_column(part[3:4])[:, 0:1]
        right = profile(wrapped(iota((LANES, depth), 1) - at, depth), radius)
        right_high, right_low = halves(right)
        col_offset = iota((cols, LANES), 0) + first_col - part[2:3]
        near = profile(wrapped(col_offset, grid_cols), radius)
        for r in range(rows):
            along = profile(wrapped(first_row + r - part[1:2], grid_rows), radius)
            left_high, left_low = halves(near * (height * along))
            added = jnp.dot(left_high, right_high, preferred_element_type=F32)
            added += jnp.dot(left_low, right_high, preferred_element_type=F32)
            added += jnp.dot(left_high, right_low, preferred_element_type=F32)
            new_ref[r * cols : (r + 1) * cols, :] += added
        return carry

    lax.fori_loop(0, devices, add, 0)
    top = lane_tops(new_ref[...])
    peak[...] = top
    peaks[me] = top
    c_copies = to_all(peak, peaks.at[me], c_send, c_recv, place, steps)
    for copy in c_copies:
        copy.start()
    for copy in c_copies:
        copy.wait_recv()
    top_ref[...] = jnp.broadcast_to(jnp.max(peaks[...]), top_ref.shape)
    for copy in b_copies + c_copies:
        copy.wait_send()


def by_full_kernel(rows, slabs, walks, bias, hills):
    cells, depth = bias.shape
    devices = slabs * walks
    vmem = pl.BlockSpec(memory_space=pltpu.VMEM)
    return pl.pallas_call(
        functools.partial(full_kernel, slabs, walks, rows, cells // rows),
        out_shape=(
            jax.ShapeDtypeStruct((cells, depth), F32),
            jax.ShapeDtypeStruct((8, LANES), F32),
        ),
        in_specs=[vmem] * 2,
        out_specs=(vmem, vmem),
        scratch_shapes=[
            pltpu.VMEM((cells, depth), BF16),
            pltpu.VMEM((cells, depth), BF16),
            pltpu.VMEM((devices, LANES), F32),
            pltpu.VMEM((len(OFFSETS), devices, LANES), F32),
            pltpu.VMEM((1, LANES), F32),
            pltpu.VMEM((devices, 1, LANES), F32),
            pltpu.SemaphoreType.DMA((len(OFFSETS),)),
            pltpu.SemaphoreType.DMA((len(OFFSETS),)),
            pltpu.SemaphoreType.DMA((devices,)),
            pltpu.SemaphoreType.DMA((devices,)),
        ],
        compiler_params=pltpu.CompilerParams(
            collective_id=1, has_side_effects=True, vmem_limit_bytes=20 * 2**20
        ),
    )(bias, hills)


def output_kernel(new_ref, top_ref, new_out, free_out, free_ref, sems):
    parts = 4
    span = new_ref.shape[0] // parts
    first = pltpu.make_async_copy(new_ref, new_out, sems.at[0])
    first.start()
    copies = [first]
    for i in range(parts):
        rows = pl.ds(i * span, span)
        free_ref[rows, :] = FREE_SCALE * (top_ref[0:1, 0:1] - new_ref[rows, :])
        copy = pltpu.make_async_copy(free_ref.at[rows], free_out.at[rows], sems.at[1 + i])
        copy.start()
        copies.append(copy)
    for copy in copies:
        copy.wait()


def outputs(new_bias, top):
    hbm = pl.BlockSpec(memory_space=pltpu.HBM)
    return pl.pallas_call(
        output_kernel,
        out_shape=(jax.ShapeDtypeStruct(new_bias.shape, F32),) * 2,
        in_specs=[pl.BlockSpec(memory_space=pltpu.VMEM)] * 2,
        out_specs=(hbm, hbm),
        scratch_shapes=[pltpu.VMEM(new_bias.shape, F32), pltpu.SemaphoreType.DMA((5,))],
        compiler_params=pltpu.CompilerParams(vmem_limit_bytes=4 * 2**20),
    )(new_bias, top)


def per_device(*arrays):
    bias_grid = arrays[0]
    shape = bias_grid.shape
    slabs, walks = lax.axis_size("slab"), lax.axis_size("walk")
    devices = slabs * walks
    fits = (
        arrays[2].size == LANES
        and slabs >= 5
        and walks >= 3
        and devices <= 64
        and devices % 8 == 0
        and shape[1] % LANES == 0
        and shape[1] >= 2 * shape[0]
        and shape[2] % LANES == 0
        and max(walks * shape[1], shape[2]) <= 4096
        and shape[2] & (shape[2] - 1) == 0
        and shape[0] * shape[1] * shape[2] <= 2**24
    )
    if not fits:
        return by_collectives(*arrays)

    def finish(new_bias, top):
        new_out, free_out = outputs(new_bias, top)
        return new_out.reshape(shape), free_out.reshape(shape)

    new_bias, top, bias, hills, flag = by_kernel(3, 5, slabs, walks, arrays)
    return lax.cond(
        flag.reshape(()),
        lambda: finish(*by_full_kernel(shape[0], slabs, walks, bias, hills)),
        lambda: finish(new_bias, top),
    )


def solution(mesh):
    in_specs = (
        P("slab", "walk", None),
        P(("slab", "walk"), None, None),
        P(("slab", "walk"), None),
        P(("slab", "walk"), None),
        P(("slab", "walk"), None),
        P(("slab", "walk"), None),
        P(("slab", "walk")),
        P(),
    )
    out_specs = (P("slab", "walk", None), P("slab", "walk", None))
    return jax.shard_map(
        per_device, mesh=mesh, in_specs=in_specs, out_specs=out_specs, check_vma=False
    )
```

```python
import functools
import math

import jax
import jax.numpy as jnp
from jax import lax
from jax.experimental import pallas as pl
from jax.experimental.pallas import tpu as pltpu
from jax.sharding import PartitionSpec as P

BASE_HEIGHT = 1.2
TEMPER = 4.0
SIGMA_SHARE = 0.3125
FREE_SCALE = 10.0 / 9.0


def from_behind(block, axis, distance):
    devices = range(lax.axis_size(axis))
    route = [((i - distance) % len(devices), i) for i in devices]
    return lax.ppermute(block, axis, route)


def gaussian(position, centre, extent, radius):
    offset = jnp.mod(position - centre + extent // 2, extent) - extent // 2
    inside = (offset >= -radius) & (offset < radius)
    spread = SIGMA_SHARE * radius
    distance = offset.astype(jnp.float32)
    return jnp.where(inside, jnp.exp(-(distance * distance) / (2.0 * spread * spread)), 0.0)


def deposit(row_ids, col_ids, depth_ids, hill_lists, grid_rows, grid_cols, grid_depth, radius):
    slot_total = hill_lists.shape[1]
    block_size = math.gcd(slot_total, 256)
    row_count = row_ids.shape[0]
    col_count = col_ids.shape[0]
    depth_count = depth_ids.shape[0]

    def one_block(carry_sum, index):
        portion = lax.dynamic_slice_in_dim(hill_lists, index * block_size, block_size, 1)
        row_gauss = (
            gaussian(row_ids[:, None], portion[1].astype(jnp.int32)[None, :], grid_rows, radius)
            * portion[0][None, :]
        )
        col_gauss = gaussian(
            col_ids[:, None], portion[2].astype(jnp.int32)[None, :], grid_cols, radius
        )
        depth_gauss = gaussian(
            depth_ids[None, :], portion[3].astype(jnp.int32)[:, None], grid_depth, radius
        )
        plane_gauss = (row_gauss[:, None, :] * col_gauss[None, :, :]).reshape(
            row_count * col_count, block_size
        )
        added = jnp.dot(
            plane_gauss,
            depth_gauss,
            precision=lax.Precision.HIGHEST,
            preferred_element_type=jnp.float32,
        )
        return (carry_sum + added, None)

    start = jnp.zeros((row_count * col_count, depth_count), jnp.float32)
    result, unused = lax.scan(one_block, start, jnp.arange(slot_total // block_size))
    return result.reshape(row_count, col_count, depth_count)


def by_collectives(
    bias_grid, hill_slab, hill_row, hill_col, hill_depth, hill_level, hill_count, height_levels
):
    rows_dev, cols_dev, depth_bins = bias_grid.shape
    slab_count = lax.axis_size("slab")
    walk_count = lax.axis_size("walk")
    radius = 2 * rows_dev
    grid_rows = rows_dev * slab_count
    grid_cols = cols_dev * walk_count
    walkers_dev, hill_slots = hill_row.shape
    sent_rows = walkers_dev * hill_slots
    capacity = max(2, 4 * sent_rows // slab_count)
    target = hill_slab[:, :, 0].reshape(-1)
    centre_row = target * rows_dev + hill_row.reshape(-1)
    is_live = (
        lax.broadcasted_iota(jnp.int32, (walkers_dev, hill_slots), 1) < hill_count[:, None]
    ).reshape(-1)
    level_match = hill_level.reshape(-1)[:, None] == lax.broadcasted_iota(
        jnp.int32, (1, height_levels.shape[0]), 1
    )
    base_height = jnp.sum(jnp.where(level_match, height_levels[None, :], 0.0), axis=1)
    base_height = jnp.where(is_live, BASE_HEIGHT * base_height, 0.0)
    same_slab = target[:, None] == target[None, :]
    earlier = lax.broadcasted_iota(jnp.int32, (sent_rows, sent_rows), 1) < lax.broadcasted_iota(
        jnp.int32, (sent_rows, sent_rows), 0
    )
    slot_rank = jnp.sum((same_slab & earlier).astype(jnp.int32), axis=1)
    slot_place = target * capacity + slot_rank
    placing = (
        slot_place[:, None] == lax.broadcasted_iota(jnp.int32, (1, slab_count * capacity), 1)
    ).astype(jnp.float32)
    fields = jnp.stack(
        [
            base_height,
            centre_row.astype(jnp.float32),
            hill_col.reshape(-1).astype(jnp.float32),
            hill_depth.reshape(-1).astype(jnp.float32),
        ]
    )
    outgoing = jnp.dot(
        fields, placing, precision=lax.Precision.HIGHEST, preferred_element_type=jnp.float32
    )
    outgoing = outgoing.reshape(4, slab_count, capacity)
    arrived = lax.all_to_all(outgoing, "slab", split_axis=1, concat_axis=1, tiled=True).reshape(
        4, slab_count * capacity
    )
    shared = lax.all_gather(arrived, "walk", axis=1, tiled=True)
    slab_index = lax.axis_index("slab")
    walk_index = lax.axis_index("walk")
    local_row = jnp.clip(shared[1].astype(jnp.int32) - slab_index * rows_dev, 0, rows_dev - 1)
    local_col = shared[2].astype(jnp.int32) - walk_index * cols_dev
    local_depth = jnp.clip(shared[3].astype(jnp.int32), 0, depth_bins - 1)
    owned = (local_col >= 0) & (local_col < cols_dev)
    flat_place = (
        local_row * cols_dev + jnp.clip(local_col, 0, cols_dev - 1)
    ) * depth_bins + local_depth
    picked = bias_grid.reshape(-1)[flat_place]
    centre_value = lax.psum(jnp.where(owned, picked, 0.0), "walk")
    height = shared[0] * jnp.exp(-centre_value / TEMPER)
    hill_lists = jnp.stack([height, shared[1], shared[2], shared[3]])
    col_ids = walk_index * cols_dev + lax.broadcasted_iota(jnp.int32, (cols_dev,), 0)
    depth_ids = lax.broadcasted_iota(jnp.int32, (depth_bins,), 0)
    collected = [hill_lists]
    for offset in (-2, -1, 1, 2):
        collected.append(from_behind(hill_lists, "slab", offset))
    row_ids = slab_index * rows_dev + lax.broadcasted_iota(jnp.int32, (rows_dev,), 0)
    added = deposit(
        row_ids,
        col_ids,
        depth_ids,
        jnp.concatenate(collected, axis=1),
        grid_rows,
        grid_cols,
        depth_bins,
        radius,
    )
    new_bias = bias_grid + added
    highest = lax.pmax(jnp.max(new_bias), ("slab", "walk"))
    free_energy = FREE_SCALE * (highest - new_bias)
    return (new_bias, free_energy)


LANES = 128
F32 = jnp.float32
BF16 = jnp.bfloat16
MESH = pl.DeviceIdType.MESH
NT = (((1,), (1,)), ((), ()))


def wrapped(offset, extent):
    offset = jnp.where(offset >= extent // 2, offset - extent, offset)
    return jnp.where(offset < -(extent // 2), offset + extent, offset)


def profile(offset, radius):
    spread = SIGMA_SHARE * radius
    value = jnp.exp(-(offset * offset) / (2.0 * spread * spread))
    return jnp.where((offset >= -radius) & (offset < radius), value, 0.0)


def halves(value):
    high = value.astype(BF16)
    return high, (value - high.astype(F32)).astype(BF16)


def iota(shape, dim):
    return lax.broadcasted_iota(jnp.int32, shape, dim).astype(F32)


def whole_iota(shape, dim):
    return lax.broadcasted_iota(jnp.int32, shape, dim)


OFFSETS = [(i, j) for i in (-2, -1, 0, 1, 2) for j in (-1, 0, 1)]
HERE = OFFSETS.index((0, 0))


def flipped(index, extent):
    values = [index]
    bit = 1
    while bit < extent:
        turn = bit * (1 - 2 * lax.rem(index // bit, 2))
        values += [value + turn for value in values]
        bit *= 2
    return values


def mesh_steps(slabs, walks):
    slab_at = flipped(lax.axis_index("slab"), slabs)
    walk_at = flipped(lax.axis_index("walk"), walks)

    def place(step):
        return (slab_at[step // walks], walk_at[step % walks])

    return place, range(slabs * walks - 1, 0, -1)


def greet(place, steps):
    barrier = pltpu.get_barrier_semaphore()
    for step in steps:
        pl.semaphore_signal(barrier, inc=1, device_id=place(step), device_id_type=MESH)
    return barrier


def to_all(source, target, send, recv, place, steps):
    return [
        pltpu.make_async_remote_copy(
            source, target, send.at[step], recv.at[step],
            device_id=place(step), device_id_type=MESH,
        )
        for step in steps
    ]


def to_near(source, tables, send, recv, slabs, walks):
    slab, walk = lax.axis_index("slab"), lax.axis_index("walk")
    copies = []
    for n, (i, j) in sorted(enumerate(OFFSETS), key=lambda item: -abs(item[1][0])):
        if n == HERE:
            continue
        device = (lax.rem(slab - i + slabs, slabs), lax.rem(walk - j + walks, walks))
        copies.append(
            pltpu.make_async_remote_copy(
                source, tables.at[n], send.at[n], recv.at[n],
                device_id=device, device_id_type=MESH,
            )
        )
    return copies


def owner_of(at_row, at_col, rows, cols, slabs, walks):
    slab_of = jnp.floor(at_row / rows) - lax.axis_index("slab").astype(F32)
    walk_of = jnp.floor(at_col / cols) - lax.axis_index("walk").astype(F32)
    slab_of = jnp.where(slab_of < -2, slab_of + slabs, slab_of)
    slab_of = jnp.where(slab_of > 2, slab_of - slabs, slab_of)
    walk_of = jnp.where(walk_of < -1, walk_of + walks, walk_of)
    walk_of = jnp.where(walk_of > 1, walk_of - walks, walk_of)
    inside = (jnp.abs(slab_of) <= 2) & (jnp.abs(walk_of) <= 1)
    return jnp.where(inside, (slab_of + 2) * 3 + walk_of + 1, -1.0)


def lane_tops(value):
    most = jnp.max(value, axis=0, keepdims=True)
    top = most[:, 0:LANES]
    for i in range(1, value.shape[1] // LANES):
        top = jnp.maximum(top, most[:, i * LANES : (i + 1) * LANES])
    return top


def as_column(row):
    return jnp.broadcast_to(row, (LANES, LANES)).T


def squeeze(mask, rank):
    lane = whole_iota(mask.shape, 1)
    code = (lane - rank.astype(jnp.int32)) * LANES + lane + LANES * LANES
    code = jnp.where(mask, code, 0)
    step = 1
    while step < LANES:
        came = pltpu.roll(code, LANES - step, axis=1)
        bit = step * LANES
        stays = jnp.where((code & bit) != 0, 0, code)
        code = jnp.where((came & bit) != 0, came, stays)
        step *= 2
    return code & (LANES - 1)


def window_kernel(
    slabs, walks, rows, cols, own_blocks, close_blocks,
    bias_in, slab_in, row_in, col_in, depth_in, level_in, count_in, table_in,
    new_ref, top_ref, bias_ref, hills_ref, flag_ref,
    slab_ref, row_ref, col_ref, depth_ref, level_ref, count_ref, table_ref, in_sems,
    mine, hills, bias_parts, picked, tables, chosen, left, right, near, peak, peaks,
    a_send, a_recv, b_send, b_recv, c_send, c_recv,
):
    devices = slabs * walks
    cells, depth = bias_ref.shape
    radius = 2 * rows
    grid_rows, grid_cols = slabs * rows, walks * cols
    slab = lax.axis_index("slab")
    walk = lax.axis_index("walk")
    me = slab * walks + walk
    first_row = (slab * rows).astype(F32)
    first_col = (walk * cols).astype(F32)
    place, steps = mesh_steps(slabs, walks)
    barrier = greet(place, steps)

    inputs = (
        (slab_in, slab_ref), (row_in, row_ref), (col_in, col_ref), (depth_in, depth_ref),
        (level_in, level_ref), (count_in, count_ref), (table_in, table_ref), (bias_in, bias_ref),
    )
    fetches = [
        pltpu.make_async_copy(there, here, in_sems.at[i])
        for i, (there, here) in enumerate(inputs)
    ]
    for fetch in fetches:
        fetch.start()
    for fetch in fetches[:-1]:
        fetch.wait()

    def in_row(ref):
        value = ref[...].astype(F32)
        return jnp.concatenate([value[i : i + 1] for i in range(value.shape[0])], axis=1)

    slots = row_ref.shape[1]
    lane = iota((1, LANES), 1)
    live = jnp.zeros((1, LANES), F32)
    for i in range(row_ref.shape[0]):
        inside = (lane >= i * slots) & (lane < i * slots + count_ref[i].astype(F32))
        live = jnp.where(inside, 1.0, live)
    target, centre_col, centre_depth = in_row(slab_ref), in_row(col_ref), in_row(depth_ref)
    key = target * walks + jnp.floor(centre_col / cols)
    key = jnp.where(live > 0, key, float(devices)) * LANES + lane
    keys = as_column(key)
    ahead = jnp.sum(jnp.where(keys < key, 1.0, 0.0), axis=0, keepdims=True)
    starts = jnp.sum(jnp.where(keys < lane * LANES, 1.0, 0.0), axis=0, keepdims=True)
    col_high = jnp.floor(centre_col / 16.0)
    depth_high = jnp.floor(centre_depth / 16.0)
    unsorted = jnp.concatenate(
        [
            jnp.where(live > 0, in_row(level_ref) + 1.0, 0.0),
            target * rows + in_row(row_ref),
            col_high,
            centre_col - 16.0 * col_high,
            depth_high,
            centre_depth - 16.0 * depth_high,
            live,
            live,
        ],
        axis=0,
    ).astype(BF16)
    order = jnp.where(iota((LANES, LANES), 0) == ahead, 1.0, 0.0).astype(BF16)
    ordered = lax.dot_general(unsorted, order, NT, preferred_element_type=F32)
    level = ordered[0:1]
    base = jnp.zeros((1, LANES), F32)
    for i in range(table_ref.shape[0]):
        base = jnp.where(level == i + 1, BASE_HEIGHT * table_ref[i], base)
    fields = (
        base,
        ordered[1:2],
        ordered[2:3] * 16.0 + ordered[3:4],
        ordered[4:5] * 16.0 + ordered[5:6],
        starts,
    )
    for i, field in enumerate(fields):
        mine[i : i + 1, :] = field
        hills[me, i : i + 1, :] = field

    pl.semaphore_wait(barrier, devices - 1)
    sent = pl.ds(0, len(fields))
    a_copies = to_all(mine.at[sent], hills.at[me, sent], a_send, a_recv, place, steps)
    for copy in a_copies:
        copy.start()

    fetches[-1].wait()
    high, low = halves(bias_ref[...])
    bias_parts[:, :depth] = high
    bias_parts[:, depth:] = low
    counting = jnp.concatenate(
        [
            jnp.where(iota((LANES, LANES), 0) < iota((LANES, LANES), 1), 1.0, 0.0),
            jnp.ones((LANES, LANES), F32),
        ],
        axis=1,
    ).astype(BF16)
    before = jnp.where(
        iota((devices, devices), 1) < iota((devices, devices), 0), 1.0, 0.0
    ).astype(BF16)
    lanes = whole_iota((devices, LANES), 1)

    for copy in a_copies:
        copy.wait_recv()

    all_base, all_row, all_col, all_depth, starts = [hills[:, i, :] for i in range(5)]
    there = all_base > 0
    owner = jnp.where(there, owner_of(all_row, all_col, rows, cols, slabs, walks), -1.0)

    counts = pltpu.roll(starts, LANES - 1, axis=1) - starts
    reached = jnp.dot(before, counts.astype(BF16), preferred_element_type=F32)

    def listed(values, index, moved, count, blocks):
        taken = [jnp.take_along_axis(value, index, axis=1) for value in values]
        result = []
        for block in range(blocks):
            spot = moved + block * LANES
            valid = (spot >= 0) & (spot < count)
            result.append([jnp.sum(jnp.where(valid, t, 0.0), axis=0, keepdims=True) for t in taken])
        return result

    here = jnp.full((devices, LANES), me, jnp.int32)
    own_start = jnp.take_along_axis(starts, here, axis=1).astype(jnp.int32)
    own_count = jnp.take_along_axis(counts, here, axis=1).astype(jnp.int32)
    own_reached = jnp.take_along_axis(reached, here, axis=1).astype(jnp.int32)
    own_cell = (all_row - first_row) * cols + all_col - first_col
    moved = lanes - own_reached
    own_lists = listed(
        [own_cell * depth + all_depth], (own_start + moved) & (LANES - 1), moved, own_count,
        own_blocks,
    )
    own_code = jnp.concatenate([block[0] for block in own_lists], axis=1).astype(jnp.int32)
    own_width = own_blocks * LANES
    select = jnp.where(
        whole_iota((depth, own_width), 0) == (own_code & (depth - 1)), 1.0, 0.0
    ).astype(BF16)
    lines = jnp.dot(
        bias_parts[...], jnp.concatenate([select, select], axis=0), preferred_element_type=F32
    )
    wanted = own_code >> (depth.bit_length() - 1)
    hit = whole_iota((cells, own_width), 0) == wanted
    value = jnp.sum(jnp.where(hit, lines, 0.0), axis=0, keepdims=True)
    value = jnp.exp(-value / TEMPER)
    for block in range(own_blocks):
        picked[block : block + 1, :] = value[:, block * LANES : (block + 1) * LANES]

    b_copies = to_near(picked, tables, b_send, b_recv, slabs, walks)
    for copy in b_copies:
        copy.start()

    def past(away, extent, limit):
        away = away + (radius - 1)
        away = jnp.where(away < 0, away + extent, away)
        away = jnp.where(away >= extent, away - extent, away)
        return away < limit

    close = (
        there
        & past(all_row - first_row, grid_rows, rows + 2 * radius - 1)
        & past(all_col - first_col, grid_cols, cols + 2 * radius - 1)
    )
    close_one = jnp.where(close, 1.0, 0.0).astype(BF16)
    both = jnp.dot(close_one, counting, preferred_element_type=F32)
    rank, close_count = both[:, :LANES], both[:, LANES:]
    close_reached = jnp.dot(before, close_count.astype(BF16), preferred_element_type=F32)
    owner_index = jnp.floor(all_row / rows) * walks + jnp.floor(all_col / cols)
    shift = jnp.take_along_axis(reached - starts, owner_index.astype(jnp.int32), axis=1)
    spot = lanes.astype(F32) + shift + owner * own_width
    over = jnp.maximum(
        own_reached + own_count - own_width,
        (close_reached + close_count).astype(jnp.int32) - close_blocks * LANES,
    ).astype(F32)
    over = jnp.max(over, axis=(0, 1), keepdims=True)
    moved = lanes - close_reached.astype(jnp.int32)
    index = jnp.take_along_axis(squeeze(close, rank), moved & (LANES - 1), axis=1)
    close_lists = listed(
        [all_base, all_row, all_col, all_depth, spot], index, moved,
        close_count.astype(jnp.int32), close_blocks,
    )
    total = close_blocks * LANES
    depth_lane = iota((LANES, LANES), 1)
    col_id = iota((cols, LANES), 0)
    for block, parts in enumerate(close_lists):
        span = slice(block * LANES, (block + 1) * LANES)
        for i in (0, 1, 4):
            chosen[i, block : block + 1, :] = parts[i]
        at = as_column(parts[3])
        for i in range(depth // LANES):
            part = profile(wrapped(depth_lane + i * LANES - at, depth), radius)
            high, low = halves(part)
            for j, half in enumerate((high, high, low)):
                rows_at = slice(j * total + block * LANES, j * total + (block + 1) * LANES)
                right[rows_at, i * LANES : (i + 1) * LANES] = half
        near[:, span] = profile(wrapped(col_id + first_col - parts[2], grid_cols), radius)
    hills_ref[...] = hills[:, 0:4, :]

    at_base, at_row = chosen[0], chosen[1]
    at_spot = chosen[4].astype(jnp.int32)
    at_lane = at_spot & (LANES - 1)
    at_table = at_spot >> (LANES.bit_length() - 1)
    row_parts = [
        at_base * profile(wrapped(first_row + r - at_row, grid_rows), radius) for r in range(rows)
    ]

    for copy in b_copies:
        copy.wait_recv()
    factor = jnp.zeros((close_blocks, LANES), F32)
    for n in range(len(OFFSETS)):
        for block in range(own_blocks):
            table = picked if n == HERE else tables.at[n]
            line = jnp.broadcast_to(table[block : block + 1, :], factor.shape)
            value = jnp.take_along_axis(line, at_lane, axis=1)
            factor = jnp.where(at_table == n * own_blocks + block, value, factor)
    row_parts = [factor * part for part in row_parts]
    for r in range(rows):
        for block in range(close_blocks):
            span = slice(block * LANES, (block + 1) * LANES)
            high, low = halves(near[:, span] * row_parts[r][block : block + 1])
            for j, half in enumerate((high, low, high)):
                lanes_at = slice(j * total + block * LANES, j * total + (block + 1) * LANES)
                left[r * cols : (r + 1) * cols, lanes_at] = half

    added = jnp.dot(left[...], right[...], preferred_element_type=F32)
    value = bias_ref[...] + added
    new_ref[...] = value
    top = jnp.where(over > 0, jnp.inf, lane_tops(value))
    peak[...] = top
    peaks[me] = top
    c_copies = to_all(peak, peaks.at[me], c_send, c_recv, place, steps)
    for copy in c_copies:
        copy.start()
    for copy in c_copies:
        copy.wait_recv()
    highest = jnp.max(peaks[...])
    top_ref[...] = jnp.broadcast_to(highest, top_ref.shape)
    flag_ref[0] = jnp.where(highest == jnp.inf, 1, 0)
    for copy in a_copies + b_copies + c_copies:
        copy.wait_send()


def by_kernel(own_blocks, close_blocks, slabs, walks, arrays):
    bias_grid, hill_slab, hill_row, hill_col, hill_depth, hill_level, hill_count, table = arrays
    rows, cols, depth = bias_grid.shape
    devices = slabs * walks
    total = close_blocks * LANES
    cells = rows * cols
    walkers = hill_row.shape
    vmem = pl.BlockSpec(memory_space=pltpu.VMEM)
    smem = pl.BlockSpec(memory_space=pltpu.SMEM)
    hbm = pl.BlockSpec(memory_space=pltpu.HBM)
    return pl.pallas_call(
        functools.partial(window_kernel, slabs, walks, rows, cols, own_blocks, close_blocks),
        out_shape=(
            jax.ShapeDtypeStruct((cells, depth), F32),
            jax.ShapeDtypeStruct((8, LANES), F32),
            jax.ShapeDtypeStruct((cells, depth), F32),
            jax.ShapeDtypeStruct((devices, 4, LANES), F32),
            jax.ShapeDtypeStruct((1,), jnp.int32),
        ),
        in_specs=[hbm] * 8,
        out_specs=(vmem, vmem, vmem, vmem, smem),
        scratch_shapes=[
            pltpu.VMEM(walkers, jnp.int32),
            pltpu.VMEM(walkers, jnp.int32),
            pltpu.VMEM(walkers, jnp.int32),
            pltpu.VMEM(walkers, jnp.int32),
            pltpu.VMEM(walkers, jnp.int32),
            pltpu.SMEM(hill_count.shape, jnp.int32),
            pltpu.SMEM(table.shape, F32),
            pltpu.SemaphoreType.DMA((8,)),
            pltpu.VMEM((8, LANES), F32),
            pltpu.VMEM((devices, 8, LANES), F32),
            pltpu.VMEM((cells, 2 * depth), BF16),
            pltpu.VMEM((own_blocks, LANES), F32),
            pltpu.VMEM((len(OFFSETS), own_blocks, LANES), F32),
            pltpu.VMEM((5, close_blocks, LANES), F32),
            pltpu.VMEM((cells, 3 * total), BF16),
            pltpu.VMEM((3 * total, depth), BF16),
            pltpu.VMEM((cols, total), F32),
            pltpu.VMEM((1, LANES), F32),
            pltpu.VMEM((devices, 1, LANES), F32),
            pltpu.SemaphoreType.DMA((devices,)),
            pltpu.SemaphoreType.DMA((devices,)),
            pltpu.SemaphoreType.DMA((len(OFFSETS),)),
            pltpu.SemaphoreType.DMA((len(OFFSETS),)),
            pltpu.SemaphoreType.DMA((devices,)),
            pltpu.SemaphoreType.DMA((devices,)),
        ],
        compiler_params=pltpu.CompilerParams(
            collective_id=0, has_side_effects=True, vmem_limit_bytes=58 * 2**20
        ),
    )(
        bias_grid.reshape(cells, depth),
        hill_slab.reshape(hill_row.shape),
        hill_row,
        hill_col,
        hill_depth,
        hill_level,
        hill_count,
        table,
    )


def full_kernel(
    slabs, walks, rows, cols,
    bias_ref, hills_ref, new_ref, top_ref,
    bias_high, bias_low, picked, tables, peak, peaks,
    b_send, b_recv, c_send, c_recv,
):
    devices = slabs * walks
    cells, depth = bias_ref.shape
    radius = 2 * rows
    grid_rows, grid_cols = slabs * rows, walks * cols
    slab = lax.axis_index("slab")
    walk = lax.axis_index("walk")
    me = slab * walks + walk
    first_row = (slab * rows).astype(F32)
    first_col = (walk * cols).astype(F32)
    place, steps = mesh_steps(slabs, walks)
    barrier = greet(place, steps)
    high, low = halves(bias_ref[...])
    bias_high[...] = high
    bias_low[...] = low

    def pick(sender, carry):
        part = hills_ref[sender]
        cell = (part[1:2] - first_row) * cols + part[2:3] - first_col
        owner = owner_of(part[1:2], part[2:3], rows, cols, slabs, walks)
        cell = jnp.where(owner == HERE, cell, -1.0)
        select = jnp.where(iota((depth, LANES), 0) == part[3:4], 1.0, 0.0).astype(BF16)
        lines = jnp.dot(bias_high[...], select, preferred_element_type=F32)
        lines = lines + jnp.dot(bias_low[...], select, preferred_element_type=F32)
        hit = iota((cells, LANES), 0) == cell
        value = jnp.sum(jnp.where(hit, lines, 0.0), axis=0, keepdims=True)
        picked[pl.ds(sender, 1), :] = jnp.exp(-value / TEMPER)
        return carry

    lax.fori_loop(0, devices, pick, 0)
    pl.semaphore_wait(barrier, devices - 1)
    b_copies = to_near(picked, tables, b_send, b_recv, slabs, walks)
    for copy in b_copies:
        copy.start()
    tables[HERE] = picked[...]
    for copy in b_copies:
        copy.wait_recv()
    new_ref[...] = bias_ref[...]

    def add(sender, carry):
        part = hills_ref[sender]
        owner = owner_of(part[1:2], part[2:3], rows, cols, slabs, walks)
        height = jnp.zeros((1, LANES), F32)
        for n in range(len(OFFSETS)):
            height = jnp.where(owner == n, part[0:1] * tables[n, pl.ds(sender, 1), :], height)
        at = as_column(part[3:4])[:, 0:1]
        right = profile(wrapped(iota((LANES, depth), 1) - at, depth), radius)
        right_high, right_low = halves(right)
        col_offset = iota((cols, LANES), 0) + first_col - part[2:3]
        near = profile(wrapped(col_offset, grid_cols), radius)
        for r in range(rows):
            along = profile(wrapped(first_row + r - part[1:2], grid_rows), radius)
            left_high, left_low = halves(near * (height * along))
            added = jnp.dot(left_high, right_high, preferred_element_type=F32)
            added += jnp.dot(left_low, right_high, preferred_element_type=F32)
            added += jnp.dot(left_high, right_low, preferred_element_type=F32)
            new_ref[r * cols : (r + 1) * cols, :] += added
        return carry

    lax.fori_loop(0, devices, add, 0)
    top = lane_tops(new_ref[...])
    peak[...] = top
    peaks[me] = top
    c_copies = to_all(peak, peaks.at[me], c_send, c_recv, place, steps)
    for copy in c_copies:
        copy.start()
    for copy in c_copies:
        copy.wait_recv()
    top_ref[...] = jnp.broadcast_to(jnp.max(peaks[...]), top_ref.shape)
    for copy in b_copies + c_copies:
        copy.wait_send()


def by_full_kernel(rows, slabs, walks, bias, hills):
    cells, depth = bias.shape
    devices = slabs * walks
    vmem = pl.BlockSpec(memory_space=pltpu.VMEM)
    return pl.pallas_call(
        functools.partial(full_kernel, slabs, walks, rows, cells // rows),
        out_shape=(
            jax.ShapeDtypeStruct((cells, depth), F32),
            jax.ShapeDtypeStruct((8, LANES), F32),
        ),
        in_specs=[vmem] * 2,
        out_specs=(vmem, vmem),
        scratch_shapes=[
            pltpu.VMEM((cells, depth), BF16),
            pltpu.VMEM((cells, depth), BF16),
            pltpu.VMEM((devices, LANES), F32),
            pltpu.VMEM((len(OFFSETS), devices, LANES), F32),
            pltpu.VMEM((1, LANES), F32),
            pltpu.VMEM((devices, 1, LANES), F32),
            pltpu.SemaphoreType.DMA((len(OFFSETS),)),
            pltpu.SemaphoreType.DMA((len(OFFSETS),)),
            pltpu.SemaphoreType.DMA((devices,)),
            pltpu.SemaphoreType.DMA((devices,)),
        ],
        compiler_params=pltpu.CompilerParams(
            collective_id=1, has_side_effects=True, vmem_limit_bytes=20 * 2**20
        ),
    )(bias, hills)


def output_kernel(new_ref, top_ref, new_out, free_out, free_ref, sems):
    parts = 4
    span = new_ref.shape[0] // parts
    first = pltpu.make_async_copy(new_ref, new_out, sems.at[0])
    first.start()
    copies = [first]
    for i in range(parts):
        rows = pl.ds(i * span, span)
        free_ref[rows, :] = FREE_SCALE * (top_ref[0:1, 0:1] - new_ref[rows, :])
        copy = pltpu.make_async_copy(free_ref.at[rows], free_out.at[rows], sems.at[1 + i])
        copy.start()
        copies.append(copy)
    for copy in copies:
        copy.wait()


def outputs(new_bias, top):
    hbm = pl.BlockSpec(memory_space=pltpu.HBM)
    return pl.pallas_call(
        output_kernel,
        out_shape=(jax.ShapeDtypeStruct(new_bias.shape, F32),) * 2,
        in_specs=[pl.BlockSpec(memory_space=pltpu.VMEM)] * 2,
        out_specs=(hbm, hbm),
        scratch_shapes=[pltpu.VMEM(new_bias.shape, F32), pltpu.SemaphoreType.DMA((5,))],
        compiler_params=pltpu.CompilerParams(vmem_limit_bytes=4 * 2**20),
    )(new_bias, top)


def per_device(*arrays):
    bias_grid = arrays[0]
    shape = bias_grid.shape
    slabs, walks = lax.axis_size("slab"), lax.axis_size("walk")
    devices = slabs * walks
    fits = (
        arrays[2].size == LANES
        and slabs >= 5
        and walks >= 3
        and devices <= 64
        and devices % 8 == 0
        and shape[1] % LANES == 0
        and shape[1] >= 2 * shape[0]
        and shape[2] % LANES == 0
        and max(walks * shape[1], shape[2]) <= 4096
        and max(slabs * shape[0], arrays[7].size) <= 255
        and all(size & (size - 1) == 0 for size in (slabs, walks, shape[2]))
        and shape[0] * shape[1] * shape[2] <= 2**24
    )
    if not fits:
        return by_collectives(*arrays)

    def finish(new_bias, top):
        new_out, free_out = outputs(new_bias, top)
        return new_out.reshape(shape), free_out.reshape(shape)

    new_bias, top, bias, hills, flag = by_kernel(3, 5, slabs, walks, arrays)
    return lax.cond(
        flag.reshape(()),
        lambda: finish(*by_full_kernel(shape[0], slabs, walks, bias, hills)),
        lambda: finish(new_bias, top),
    )


def solution(mesh):
    in_specs = (
        P("slab", "walk", None),
        P(("slab", "walk"), None, None),
        P(("slab", "walk"), None),
        P(("slab", "walk"), None),
        P(("slab", "walk"), None),
        P(("slab", "walk"), None),
        P(("slab", "walk")),
        P(),
    )
    out_specs = (P("slab", "walk", None), P("slab", "walk", None))
    return jax.shard_map(
        per_device, mesh=mesh, in_specs=in_specs, out_specs=out_specs, check_vma=False
    )
```

```python
import functools
import math

import jax
import jax.numpy as jnp
from jax import lax
from jax.experimental import pallas as pl
from jax.experimental.pallas import tpu as pltpu
from jax.sharding import PartitionSpec as P

BASE_HEIGHT = 1.2
TEMPER = 4.0
SIGMA_SHARE = 0.3125
FREE_SCALE = 10.0 / 9.0


def from_behind(block, axis, distance):
    devices = range(lax.axis_size(axis))
    route = [((i - distance) % len(devices), i) for i in devices]
    return lax.ppermute(block, axis, route)


def gaussian(position, centre, extent, radius):
    offset = jnp.mod(position - centre + extent // 2, extent) - extent // 2
    inside = (offset >= -radius) & (offset < radius)
    spread = SIGMA_SHARE * radius
    distance = offset.astype(jnp.float32)
    return jnp.where(inside, jnp.exp(-(distance * distance) / (2.0 * spread * spread)), 0.0)


def deposit(row_ids, col_ids, depth_ids, hill_lists, grid_rows, grid_cols, grid_depth, radius):
    slot_total = hill_lists.shape[1]
    block_size = math.gcd(slot_total, 256)
    row_count = row_ids.shape[0]
    col_count = col_ids.shape[0]
    depth_count = depth_ids.shape[0]

    def one_block(carry_sum, index):
        portion = lax.dynamic_slice_in_dim(hill_lists, index * block_size, block_size, 1)
        row_gauss = (
            gaussian(row_ids[:, None], portion[1].astype(jnp.int32)[None, :], grid_rows, radius)
            * portion[0][None, :]
        )
        col_gauss = gaussian(
            col_ids[:, None], portion[2].astype(jnp.int32)[None, :], grid_cols, radius
        )
        depth_gauss = gaussian(
            depth_ids[None, :], portion[3].astype(jnp.int32)[:, None], grid_depth, radius
        )
        plane_gauss = (row_gauss[:, None, :] * col_gauss[None, :, :]).reshape(
            row_count * col_count, block_size
        )
        added = jnp.dot(
            plane_gauss,
            depth_gauss,
            precision=lax.Precision.HIGHEST,
            preferred_element_type=jnp.float32,
        )
        return (carry_sum + added, None)

    start = jnp.zeros((row_count * col_count, depth_count), jnp.float32)
    result, unused = lax.scan(one_block, start, jnp.arange(slot_total // block_size))
    return result.reshape(row_count, col_count, depth_count)


def by_collectives(
    bias_grid, hill_slab, hill_row, hill_col, hill_depth, hill_level, hill_count, height_levels
):
    rows_dev, cols_dev, depth_bins = bias_grid.shape
    slab_count = lax.axis_size("slab")
    walk_count = lax.axis_size("walk")
    radius = 2 * rows_dev
    grid_rows = rows_dev * slab_count
    grid_cols = cols_dev * walk_count
    walkers_dev, hill_slots = hill_row.shape
    sent_rows = walkers_dev * hill_slots
    capacity = max(2, 4 * sent_rows // slab_count)
    target = hill_slab[:, :, 0].reshape(-1)
    centre_row = target * rows_dev + hill_row.reshape(-1)
    is_live = (
        lax.broadcasted_iota(jnp.int32, (walkers_dev, hill_slots), 1) < hill_count[:, None]
    ).reshape(-1)
    level_match = hill_level.reshape(-1)[:, None] == lax.broadcasted_iota(
        jnp.int32, (1, height_levels.shape[0]), 1
    )
    base_height = jnp.sum(jnp.where(level_match, height_levels[None, :], 0.0), axis=1)
    base_height = jnp.where(is_live, BASE_HEIGHT * base_height, 0.0)
    same_slab = target[:, None] == target[None, :]
    earlier = lax.broadcasted_iota(jnp.int32, (sent_rows, sent_rows), 1) < lax.broadcasted_iota(
        jnp.int32, (sent_rows, sent_rows), 0
    )
    slot_rank = jnp.sum((same_slab & earlier).astype(jnp.int32), axis=1)
    slot_place = target * capacity + slot_rank
    placing = (
        slot_place[:, None] == lax.broadcasted_iota(jnp.int32, (1, slab_count * capacity), 1)
    ).astype(jnp.float32)
    fields = jnp.stack(
        [
            base_height,
            centre_row.astype(jnp.float32),
            hill_col.reshape(-1).astype(jnp.float32),
            hill_depth.reshape(-1).astype(jnp.float32),
        ]
    )
    outgoing = jnp.dot(
        fields, placing, precision=lax.Precision.HIGHEST, preferred_element_type=jnp.float32
    )
    outgoing = outgoing.reshape(4, slab_count, capacity)
    arrived = lax.all_to_all(outgoing, "slab", split_axis=1, concat_axis=1, tiled=True).reshape(
        4, slab_count * capacity
    )
    shared = lax.all_gather(arrived, "walk", axis=1, tiled=True)
    slab_index = lax.axis_index("slab")
    walk_index = lax.axis_index("walk")
    local_row = jnp.clip(shared[1].astype(jnp.int32) - slab_index * rows_dev, 0, rows_dev - 1)
    local_col = shared[2].astype(jnp.int32) - walk_index * cols_dev
    local_depth = jnp.clip(shared[3].astype(jnp.int32), 0, depth_bins - 1)
    owned = (local_col >= 0) & (local_col < cols_dev)
    flat_place = (
        local_row * cols_dev + jnp.clip(local_col, 0, cols_dev - 1)
    ) * depth_bins + local_depth
    picked = bias_grid.reshape(-1)[flat_place]
    centre_value = lax.psum(jnp.where(owned, picked, 0.0), "walk")
    height = shared[0] * jnp.exp(-centre_value / TEMPER)
    hill_lists = jnp.stack([height, shared[1], shared[2], shared[3]])
    col_ids = walk_index * cols_dev + lax.broadcasted_iota(jnp.int32, (cols_dev,), 0)
    depth_ids = lax.broadcasted_iota(jnp.int32, (depth_bins,), 0)
    collected = [hill_lists]
    for offset in (-2, -1, 1, 2):
        collected.append(from_behind(hill_lists, "slab", offset))
    row_ids = slab_index * rows_dev + lax.broadcasted_iota(jnp.int32, (rows_dev,), 0)
    added = deposit(
        row_ids,
        col_ids,
        depth_ids,
        jnp.concatenate(collected, axis=1),
        grid_rows,
        grid_cols,
        depth_bins,
        radius,
    )
    new_bias = bias_grid + added
    highest = lax.pmax(jnp.max(new_bias), ("slab", "walk"))
    free_energy = FREE_SCALE * (highest - new_bias)
    return (new_bias, free_energy)


LANES = 128
F32 = jnp.float32
BF16 = jnp.bfloat16
MESH = pl.DeviceIdType.MESH
NT = (((1,), (1,)), ((), ()))


def wrapped(offset, extent):
    offset = jnp.where(offset >= extent // 2, offset - extent, offset)
    return jnp.where(offset < -(extent // 2), offset + extent, offset)


def profile(offset, radius):
    spread = SIGMA_SHARE * radius
    value = jnp.exp(-(offset * offset) / (2.0 * spread * spread))
    return jnp.where((offset >= -radius) & (offset < radius), value, 0.0)


def halves(value):
    high = value.astype(BF16)
    return high, (value - high.astype(F32)).astype(BF16)


def iota(shape, dim):
    return lax.broadcasted_iota(jnp.int32, shape, dim).astype(F32)


def whole_iota(shape, dim):
    return lax.broadcasted_iota(jnp.int32, shape, dim)


OFFSETS = [(i, j) for i in (-2, -1, 0, 1, 2) for j in (-1, 0, 1)]
HERE = OFFSETS.index((0, 0))


def flipped(index, extent):
    values = [index]
    bit = 1
    while bit < extent:
        turn = bit * (1 - 2 * lax.rem(index // bit, 2))
        values += [value + turn for value in values]
        bit *= 2
    return values


def mesh_steps(slabs, walks):
    slab_at = flipped(lax.axis_index("slab"), slabs)
    walk_at = flipped(lax.axis_index("walk"), walks)

    def place(step):
        return (slab_at[step // walks], walk_at[step % walks])

    return place, range(slabs * walks - 1, 0, -1)


def greet(place, steps):
    barrier = pltpu.get_barrier_semaphore()
    for step in steps:
        pl.semaphore_signal(barrier, inc=1, device_id=place(step), device_id_type=MESH)
    return barrier


def to_all(source, target, send, recv, place, steps):
    return [
        pltpu.make_async_remote_copy(
            source, target, send.at[0], recv.at[0],
            device_id=place(step), device_id_type=MESH,
        )
        for step in steps
    ]


def to_near(source, tables, send, recv, slabs, walks):
    slab, walk = lax.axis_index("slab"), lax.axis_index("walk")
    copies = []
    for n, (i, j) in sorted(enumerate(OFFSETS), key=lambda item: -abs(item[1][0])):
        if n == HERE:
            continue
        device = (lax.rem(slab - i + slabs, slabs), lax.rem(walk - j + walks, walks))
        copies.append(
            pltpu.make_async_remote_copy(
                source, tables.at[n], send.at[0], recv.at[0],
                device_id=device, device_id_type=MESH,
            )
        )
    return copies


def arrival(landing, send, recv, place):
    return pltpu.make_async_remote_copy(
        landing, landing, send.at[0], recv.at[0], device_id=place(1), device_id_type=MESH
    )


def owner_of(at_row, at_col, rows, cols, slabs, walks):
    slab_of = jnp.floor(at_row / rows) - lax.axis_index("slab").astype(F32)
    walk_of = jnp.floor(at_col / cols) - lax.axis_index("walk").astype(F32)
    slab_of = jnp.where(slab_of < -2, slab_of + slabs, slab_of)
    slab_of = jnp.where(slab_of > 2, slab_of - slabs, slab_of)
    walk_of = jnp.where(walk_of < -1, walk_of + walks, walk_of)
    walk_of = jnp.where(walk_of > 1, walk_of - walks, walk_of)
    inside = (jnp.abs(slab_of) <= 2) & (jnp.abs(walk_of) <= 1)
    return jnp.where(inside, (slab_of + 2) * 3 + walk_of + 1, -1.0)


def lane_tops(value):
    most = jnp.max(value, axis=0, keepdims=True)
    top = most[:, 0:LANES]
    for i in range(1, value.shape[1] // LANES):
        top = jnp.maximum(top, most[:, i * LANES : (i + 1) * LANES])
    return top


def as_column(row):
    return jnp.broadcast_to(row, (LANES, LANES)).T


def squeeze(mask, rank):
    lane = whole_iota(mask.shape, 1)
    code = (lane - rank.astype(jnp.int32)) * LANES + lane + LANES * LANES
    code = jnp.where(mask, code, 0)
    step = 1
    while step < LANES:
        came = pltpu.roll(code, LANES - step, axis=1)
        bit = step * LANES
        stays = jnp.where((code & bit) != 0, 0, code)
        code = jnp.where((came & bit) != 0, came, stays)
        step *= 2
    return code & (LANES - 1)


def window_kernel(
    slabs, walks, rows, cols, own_blocks, close_blocks,
    bias_in, slab_in, row_in, col_in, depth_in, level_in, count_in, table_in,
    new_ref, top_ref, bias_ref, hills_ref, flag_ref,
    slab_ref, row_ref, col_ref, depth_ref, level_ref, count_ref, table_ref, in_sems,
    mine, hills, bias_parts, picked, tables, chosen, left, right, near, peak, peaks,
    a_send, a_recv, b_send, b_recv, c_send, c_recv,
):
    devices = slabs * walks
    cells, depth = bias_ref.shape
    radius = 2 * rows
    grid_rows, grid_cols = slabs * rows, walks * cols
    slab = lax.axis_index("slab")
    walk = lax.axis_index("walk")
    me = slab * walks + walk
    first_row = (slab * rows).astype(F32)
    first_col = (walk * cols).astype(F32)
    place, steps = mesh_steps(slabs, walks)
    barrier = greet(place, steps)

    inputs = (
        (slab_in, slab_ref), (row_in, row_ref), (col_in, col_ref), (depth_in, depth_ref),
        (level_in, level_ref), (count_in, count_ref), (table_in, table_ref), (bias_in, bias_ref),
    )
    fetches = [
        pltpu.make_async_copy(there, here, in_sems.at[i])
        for i, (there, here) in enumerate(inputs)
    ]
    for fetch in fetches:
        fetch.start()
    for fetch in fetches[:-1]:
        fetch.wait()

    def in_row(ref):
        value = ref[...].astype(F32)
        return jnp.concatenate([value[i : i + 1] for i in range(value.shape[0])], axis=1)

    slots = row_ref.shape[1]
    lane = iota((1, LANES), 1)
    live = jnp.zeros((1, LANES), F32)
    for i in range(row_ref.shape[0]):
        inside = (lane >= i * slots) & (lane < i * slots + count_ref[i].astype(F32))
        live = jnp.where(inside, 1.0, live)
    target, centre_col, centre_depth = in_row(slab_ref), in_row(col_ref), in_row(depth_ref)
    key = target * walks + jnp.floor(centre_col / cols)
    key = jnp.where(live > 0, key, float(devices)) * LANES + lane
    keys = as_column(key)
    ahead = jnp.sum(jnp.where(keys < key, 1.0, 0.0), axis=0, keepdims=True)
    starts = jnp.sum(jnp.where(keys < lane * LANES, 1.0, 0.0), axis=0, keepdims=True)
    col_high = jnp.floor(centre_col / 16.0)
    depth_high = jnp.floor(centre_depth / 16.0)
    unsorted = jnp.concatenate(
        [
            jnp.where(live > 0, in_row(level_ref) + 1.0, 0.0),
            target * rows + in_row(row_ref),
            col_high,
            centre_col - 16.0 * col_high,
            depth_high,
            centre_depth - 16.0 * depth_high,
            live,
            live,
        ],
        axis=0,
    ).astype(BF16)
    order = jnp.where(iota((LANES, LANES), 0) == ahead, 1.0, 0.0).astype(BF16)
    ordered = lax.dot_general(unsorted, order, NT, preferred_element_type=F32)
    level = ordered[0:1]
    base = jnp.zeros((1, LANES), F32)
    for i in range(table_ref.shape[0]):
        base = jnp.where(level == i + 1, BASE_HEIGHT * table_ref[i], base)
    fields = (
        base,
        ordered[1:2],
        ordered[2:3] * 16.0 + ordered[3:4],
        ordered[4:5] * 16.0 + ordered[5:6],
        starts,
    )
    for i, field in enumerate(fields):
        mine[i : i + 1, :] = field
        hills[me, i : i + 1, :] = field

    pl.semaphore_wait(barrier, devices - 1)
    sent = pl.ds(0, len(fields))
    a_copies = to_all(mine.at[sent], hills.at[me, sent], a_send, a_recv, place, steps)
    for copy in a_copies:
        copy.start()
    others = pl.ds(0, devices - 1)
    a_all = arrival(hills.at[others, sent], a_send, a_recv, place)

    fetches[-1].wait()
    high, low = halves(bias_ref[...])
    bias_parts[:, :depth] = high
    bias_parts[:, depth:] = low
    counting = jnp.concatenate(
        [
            jnp.where(iota((LANES, LANES), 0) < iota((LANES, LANES), 1), 1.0, 0.0),
            jnp.ones((LANES, LANES), F32),
        ],
        axis=1,
    ).astype(BF16)
    before = jnp.where(
        iota((devices, devices), 1) < iota((devices, devices), 0), 1.0, 0.0
    ).astype(BF16)
    lanes = whole_iota((devices, LANES), 1)

    a_all.wait_recv()

    all_base, all_row, all_col, all_depth, starts = [hills[:, i, :] for i in range(5)]
    there = all_base > 0
    owner = jnp.where(there, owner_of(all_row, all_col, rows, cols, slabs, walks), -1.0)

    counts = pltpu.roll(starts, LANES - 1, axis=1) - starts
    reached = jnp.dot(before, counts.astype(BF16), preferred_element_type=F32)

    def listed(values, index, moved, count, blocks):
        taken = [jnp.take_along_axis(value, index, axis=1) for value in values]
        result = []
        for block in range(blocks):
            spot = moved + block * LANES
            valid = (spot >= 0) & (spot < count)
            result.append([jnp.sum(jnp.where(valid, t, 0.0), axis=0, keepdims=True) for t in taken])
        return result

    here = jnp.full((devices, LANES), me, jnp.int32)
    own_start = jnp.take_along_axis(starts, here, axis=1).astype(jnp.int32)
    own_count = jnp.take_along_axis(counts, here, axis=1).astype(jnp.int32)
    own_reached = jnp.take_along_axis(reached, here, axis=1).astype(jnp.int32)
    own_cell = (all_row - first_row) * cols + all_col - first_col
    moved = lanes - own_reached
    own_lists = listed(
        [own_cell * depth + all_depth], (own_start + moved) & (LANES - 1), moved, own_count,
        own_blocks,
    )
    own_code = jnp.concatenate([block[0] for block in own_lists], axis=1).astype(jnp.int32)
    own_width = own_blocks * LANES
    select = jnp.where(
        whole_iota((depth, own_width), 0) == (own_code & (depth - 1)), 1.0, 0.0
    ).astype(BF16)
    lines = jnp.dot(
        bias_parts[...], jnp.concatenate([select, select], axis=0), preferred_element_type=F32
    )
    wanted = own_code >> (depth.bit_length() - 1)
    hit = whole_iota((cells, own_width), 0) == wanted
    value = jnp.sum(jnp.where(hit, lines, 0.0), axis=0, keepdims=True)
    value = jnp.exp(-value / TEMPER)
    for block in range(own_blocks):
        picked[block : block + 1, :] = value[:, block * LANES : (block + 1) * LANES]

    for copy in to_near(picked, tables, b_send, b_recv, slabs, walks):
        copy.start()
    b_all = arrival(tables.at[pl.ds(0, len(OFFSETS) - 1)], b_send, b_recv, place)
    a_all.wait_send()

    def past(away, extent, limit):
        away = away + (radius - 1)
        away = jnp.where(away < 0, away + extent, away)
        away = jnp.where(away >= extent, away - extent, away)
        return away < limit

    close = (
        there
        & past(all_row - first_row, grid_rows, rows + 2 * radius - 1)
        & past(all_col - first_col, grid_cols, cols + 2 * radius - 1)
    )
    close_one = jnp.where(close, 1.0, 0.0).astype(BF16)
    both = jnp.dot(close_one, counting, preferred_element_type=F32)
    rank, close_count = both[:, :LANES], both[:, LANES:]
    close_reached = jnp.dot(before, close_count.astype(BF16), preferred_element_type=F32)
    owner_index = jnp.floor(all_row / rows) * walks + jnp.floor(all_col / cols)
    shift = jnp.take_along_axis(reached - starts, owner_index.astype(jnp.int32), axis=1)
    spot = lanes.astype(F32) + shift + owner * own_width
    over = jnp.maximum(
        own_reached + own_count - own_width,
        (close_reached + close_count).astype(jnp.int32) - close_blocks * LANES,
    ).astype(F32)
    over = jnp.max(over, axis=(0, 1), keepdims=True)
    moved = lanes - close_reached.astype(jnp.int32)
    index = jnp.take_along_axis(squeeze(close, rank), moved & (LANES - 1), axis=1)
    close_lists = listed(
        [all_base, all_row, all_col, all_depth, spot], index, moved,
        close_count.astype(jnp.int32), close_blocks,
    )
    total = close_blocks * LANES
    depth_lane = iota((LANES, LANES), 1)
    col_id = iota((cols, LANES), 0)
    for block, parts in enumerate(close_lists):
        span = slice(block * LANES, (block + 1) * LANES)
        for i in (0, 1, 4):
            chosen[i, block : block + 1, :] = parts[i]
        at = as_column(parts[3])
        for i in range(depth // LANES):
            part = profile(wrapped(depth_lane + i * LANES - at, depth), radius)
            high, low = halves(part)
            for j, half in enumerate((high, high, low)):
                rows_at = slice(j * total + block * LANES, j * total + (block + 1) * LANES)
                right[rows_at, i * LANES : (i + 1) * LANES] = half
        near[:, span] = profile(wrapped(col_id + first_col - parts[2], grid_cols), radius)
    hills_ref[...] = hills[:, 0:4, :]

    at_base, at_row = chosen[0], chosen[1]
    at_spot = chosen[4].astype(jnp.int32)
    at_lane = at_spot & (LANES - 1)
    at_table = at_spot >> (LANES.bit_length() - 1)
    row_parts = [
        at_base * profile(wrapped(first_row + r - at_row, grid_rows), radius) for r in range(rows)
    ]

    b_all.wait_recv()
    factor = jnp.zeros((close_blocks, LANES), F32)
    for n in range(len(OFFSETS)):
        for block in range(own_blocks):
            table = picked if n == HERE else tables.at[n]
            line = jnp.broadcast_to(table[block : block + 1, :], factor.shape)
            value = jnp.take_along_axis(line, at_lane, axis=1)
            factor = jnp.where(at_table == n * own_blocks + block, value, factor)
    row_parts = [factor * part for part in row_parts]
    for r in range(rows):
        for block in range(close_blocks):
            span = slice(block * LANES, (block + 1) * LANES)
            high, low = halves(near[:, span] * row_parts[r][block : block + 1])
            for j, half in enumerate((high, low, high)):
                lanes_at = slice(j * total + block * LANES, j * total + (block + 1) * LANES)
                left[r * cols : (r + 1) * cols, lanes_at] = half

    added = jnp.dot(left[...], right[...], preferred_element_type=F32)
    value = bias_ref[...] + added
    new_ref[...] = value
    top = jnp.where(over > 0, jnp.inf, lane_tops(value))
    peak[...] = top
    peaks[me] = top
    for copy in to_all(peak, peaks.at[me], c_send, c_recv, place, steps):
        copy.start()
    c_all = arrival(peaks.at[others], c_send, c_recv, place)
    b_all.wait_send()
    c_all.wait_send()
    c_all.wait_recv()
    highest = jnp.max(peaks[...])
    top_ref[...] = jnp.broadcast_to(highest, top_ref.shape)
    flag_ref[0] = jnp.where(highest == jnp.inf, 1, 0)


def by_kernel(own_blocks, close_blocks, slabs, walks, arrays):
    bias_grid, hill_slab, hill_row, hill_col, hill_depth, hill_level, hill_count, table = arrays
    rows, cols, depth = bias_grid.shape
    devices = slabs * walks
    total = close_blocks * LANES
    cells = rows * cols
    walkers = hill_row.shape
    vmem = pl.BlockSpec(memory_space=pltpu.VMEM)
    smem = pl.BlockSpec(memory_space=pltpu.SMEM)
    hbm = pl.BlockSpec(memory_space=pltpu.HBM)
    return pl.pallas_call(
        functools.partial(window_kernel, slabs, walks, rows, cols, own_blocks, close_blocks),
        out_shape=(
            jax.ShapeDtypeStruct((cells, depth), F32),
            jax.ShapeDtypeStruct((8, LANES), F32),
            jax.ShapeDtypeStruct((cells, depth), F32),
            jax.ShapeDtypeStruct((devices, 4, LANES), F32),
            jax.ShapeDtypeStruct((1,), jnp.int32),
        ),
        in_specs=[hbm] * 8,
        out_specs=(vmem, vmem, vmem, vmem, smem),
        scratch_shapes=[
            pltpu.VMEM(walkers, jnp.int32),
            pltpu.VMEM(walkers, jnp.int32),
            pltpu.VMEM(walkers, jnp.int32),
            pltpu.VMEM(walkers, jnp.int32),
            pltpu.VMEM(walkers, jnp.int32),
            pltpu.SMEM(hill_count.shape, jnp.int32),
            pltpu.SMEM(table.shape, F32),
            pltpu.SemaphoreType.DMA((8,)),
            pltpu.VMEM((8, LANES), F32),
            pltpu.VMEM((devices, 8, LANES), F32),
            pltpu.VMEM((cells, 2 * depth), BF16),
            pltpu.VMEM((own_blocks, LANES), F32),
            pltpu.VMEM((len(OFFSETS), own_blocks, LANES), F32),
            pltpu.VMEM((5, close_blocks, LANES), F32),
            pltpu.VMEM((cells, 3 * total), BF16),
            pltpu.VMEM((3 * total, depth), BF16),
            pltpu.VMEM((cols, total), F32),
            pltpu.VMEM((1, LANES), F32),
            pltpu.VMEM((devices, 1, LANES), F32),
            pltpu.SemaphoreType.DMA((1,)),
            pltpu.SemaphoreType.DMA((1,)),
            pltpu.SemaphoreType.DMA((1,)),
            pltpu.SemaphoreType.DMA((1,)),
            pltpu.SemaphoreType.DMA((1,)),
            pltpu.SemaphoreType.DMA((1,)),
        ],
        compiler_params=pltpu.CompilerParams(
            collective_id=0, has_side_effects=True, vmem_limit_bytes=58 * 2**20
        ),
    )(
        bias_grid.reshape(cells, depth),
        hill_slab.reshape(hill_row.shape),
        hill_row,
        hill_col,
        hill_depth,
        hill_level,
        hill_count,
        table,
    )


def full_kernel(
    slabs, walks, rows, cols,
    bias_ref, hills_ref, new_ref, top_ref,
    bias_high, bias_low, picked, tables, peak, peaks,
    b_send, b_recv, c_send, c_recv,
):
    devices = slabs * walks
    cells, depth = bias_ref.shape
    radius = 2 * rows
    grid_rows, grid_cols = slabs * rows, walks * cols
    slab = lax.axis_index("slab")
    walk = lax.axis_index("walk")
    me = slab * walks + walk
    first_row = (slab * rows).astype(F32)
    first_col = (walk * cols).astype(F32)
    place, steps = mesh_steps(slabs, walks)
    barrier = greet(place, steps)
    high, low = halves(bias_ref[...])
    bias_high[...] = high
    bias_low[...] = low

    def pick(sender, carry):
        part = hills_ref[sender]
        cell = (part[1:2] - first_row) * cols + part[2:3] - first_col
        owner = owner_of(part[1:2], part[2:3], rows, cols, slabs, walks)
        cell = jnp.where(owner == HERE, cell, -1.0)
        select = jnp.where(iota((depth, LANES), 0) == part[3:4], 1.0, 0.0).astype(BF16)
        lines = jnp.dot(bias_high[...], select, preferred_element_type=F32)
        lines = lines + jnp.dot(bias_low[...], select, preferred_element_type=F32)
        hit = iota((cells, LANES), 0) == cell
        value = jnp.sum(jnp.where(hit, lines, 0.0), axis=0, keepdims=True)
        picked[pl.ds(sender, 1), :] = jnp.exp(-value / TEMPER)
        return carry

    lax.fori_loop(0, devices, pick, 0)
    pl.semaphore_wait(barrier, devices - 1)
    for copy in to_near(picked, tables, b_send, b_recv, slabs, walks):
        copy.start()
    b_all = arrival(tables.at[pl.ds(0, len(OFFSETS) - 1)], b_send, b_recv, place)
    tables[HERE] = picked[...]
    b_all.wait_recv()
    new_ref[...] = bias_ref[...]

    def add(sender, carry):
        part = hills_ref[sender]
        owner = owner_of(part[1:2], part[2:3], rows, cols, slabs, walks)
        height = jnp.zeros((1, LANES), F32)
        for n in range(len(OFFSETS)):
            height = jnp.where(owner == n, part[0:1] * tables[n, pl.ds(sender, 1), :], height)
        at = as_column(part[3:4])[:, 0:1]
        right = profile(wrapped(iota((LANES, depth), 1) - at, depth), radius)
        right_high, right_low = halves(right)
        col_offset = iota((cols, LANES), 0) + first_col - part[2:3]
        near = profile(wrapped(col_offset, grid_cols), radius)
        for r in range(rows):
            along = profile(wrapped(first_row + r - part[1:2], grid_rows), radius)
            left_high, left_low = halves(near * (height * along))
            added = jnp.dot(left_high, right_high, preferred_element_type=F32)
            added += jnp.dot(left_low, right_high, preferred_element_type=F32)
            added += jnp.dot(left_high, right_low, preferred_element_type=F32)
            new_ref[r * cols : (r + 1) * cols, :] += added
        return carry

    lax.fori_loop(0, devices, add, 0)
    top = lane_tops(new_ref[...])
    peak[...] = top
    peaks[me] = top
    for copy in to_all(peak, peaks.at[me], c_send, c_recv, place, steps):
        copy.start()
    c_all = arrival(peaks.at[pl.ds(0, devices - 1)], c_send, c_recv, place)
    b_all.wait_send()
    c_all.wait_send()
    c_all.wait_recv()
    top_ref[...] = jnp.broadcast_to(jnp.max(peaks[...]), top_ref.shape)


def by_full_kernel(rows, slabs, walks, bias, hills):
    cells, depth = bias.shape
    devices = slabs * walks
    vmem = pl.BlockSpec(memory_space=pltpu.VMEM)
    return pl.pallas_call(
        functools.partial(full_kernel, slabs, walks, rows, cells // rows),
        out_shape=(
            jax.ShapeDtypeStruct((cells, depth), F32),
            jax.ShapeDtypeStruct((8, LANES), F32),
        ),
        in_specs=[vmem] * 2,
        out_specs=(vmem, vmem),
        scratch_shapes=[
            pltpu.VMEM((cells, depth), BF16),
            pltpu.VMEM((cells, depth), BF16),
            pltpu.VMEM((devices, LANES), F32),
            pltpu.VMEM((len(OFFSETS), devices, LANES), F32),
            pltpu.VMEM((1, LANES), F32),
            pltpu.VMEM((devices, 1, LANES), F32),
            pltpu.SemaphoreType.DMA((1,)),
            pltpu.SemaphoreType.DMA((1,)),
            pltpu.SemaphoreType.DMA((1,)),
            pltpu.SemaphoreType.DMA((1,)),
        ],
        compiler_params=pltpu.CompilerParams(
            collective_id=1, has_side_effects=True, vmem_limit_bytes=20 * 2**20
        ),
    )(bias, hills)


def output_kernel(new_ref, top_ref, new_out, free_out, free_ref, sems):
    parts = 4
    span = new_ref.shape[0] // parts
    first = pltpu.make_async_copy(new_ref, new_out, sems.at[0])
    first.start()
    copies = [first]
    for i in range(parts):
        rows = pl.ds(i * span, span)
        free_ref[rows, :] = FREE_SCALE * (top_ref[0:1, 0:1] - new_ref[rows, :])
        copy = pltpu.make_async_copy(free_ref.at[rows], free_out.at[rows], sems.at[1 + i])
        copy.start()
        copies.append(copy)
    for copy in copies:
        copy.wait()


def outputs(new_bias, top):
    hbm = pl.BlockSpec(memory_space=pltpu.HBM)
    return pl.pallas_call(
        output_kernel,
        out_shape=(jax.ShapeDtypeStruct(new_bias.shape, F32),) * 2,
        in_specs=[pl.BlockSpec(memory_space=pltpu.VMEM)] * 2,
        out_specs=(hbm, hbm),
        scratch_shapes=[pltpu.VMEM(new_bias.shape, F32), pltpu.SemaphoreType.DMA((5,))],
        compiler_params=pltpu.CompilerParams(vmem_limit_bytes=4 * 2**20),
    )(new_bias, top)


def per_device(*arrays):
    bias_grid = arrays[0]
    shape = bias_grid.shape
    slabs, walks = lax.axis_size("slab"), lax.axis_size("walk")
    devices = slabs * walks
    fits = (
        arrays[2].size == LANES
        and slabs >= 5
        and walks >= 3
        and devices <= 64
        and devices % 8 == 0
        and shape[1] % LANES == 0
        and shape[1] >= 2 * shape[0]
        and shape[2] % LANES == 0
        and max(walks * shape[1], shape[2]) <= 4096
        and max(slabs * shape[0], arrays[7].size) <= 255
        and all(size & (size - 1) == 0 for size in (slabs, walks, shape[2]))
        and shape[0] * shape[1] * shape[2] <= 2**24
    )
    if not fits:
        return by_collectives(*arrays)

    def finish(new_bias, top):
        new_out, free_out = outputs(new_bias, top)
        return new_out.reshape(shape), free_out.reshape(shape)

    new_bias, top, bias, hills, flag = by_kernel(3, 5, slabs, walks, arrays)
    return lax.cond(
        flag.reshape(()),
        lambda: finish(*by_full_kernel(shape[0], slabs, walks, bias, hills)),
        lambda: finish(new_bias, top),
    )


def solution(mesh):
    in_specs = (
        P("slab", "walk", None),
        P(("slab", "walk"), None, None),
        P(("slab", "walk"), None),
        P(("slab", "walk"), None),
        P(("slab", "walk"), None),
        P(("slab", "walk"), None),
        P(("slab", "walk")),
        P(),
    )
    out_specs = (P("slab", "walk", None), P("slab", "walk", None))
    return jax.shard_map(
        per_device, mesh=mesh, in_specs=in_specs, out_specs=out_specs, check_vma=False
    )
```

```python
import functools
import math

import jax
import jax.numpy as jnp
from jax import lax
from jax.experimental import pallas as pl
from jax.experimental.pallas import tpu as pltpu
from jax.sharding import PartitionSpec as P

BASE_HEIGHT = 1.2
TEMPER = 4.0
SIGMA_SHARE = 0.3125
FREE_SCALE = 10.0 / 9.0


def from_behind(block, axis, distance):
    devices = range(lax.axis_size(axis))
    route = [((i - distance) % len(devices), i) for i in devices]
    return lax.ppermute(block, axis, route)


def gaussian(position, centre, extent, radius):
    offset = jnp.mod(position - centre + extent // 2, extent) - extent // 2
    inside = (offset >= -radius) & (offset < radius)
    spread = SIGMA_SHARE * radius
    distance = offset.astype(jnp.float32)
    return jnp.where(inside, jnp.exp(-(distance * distance) / (2.0 * spread * spread)), 0.0)


def deposit(row_ids, col_ids, depth_ids, hill_lists, grid_rows, grid_cols, grid_depth, radius):
    slot_total = hill_lists.shape[1]
    block_size = math.gcd(slot_total, 256)
    row_count = row_ids.shape[0]
    col_count = col_ids.shape[0]
    depth_count = depth_ids.shape[0]

    def one_block(carry_sum, index):
        portion = lax.dynamic_slice_in_dim(hill_lists, index * block_size, block_size, 1)
        row_gauss = (
            gaussian(row_ids[:, None], portion[1].astype(jnp.int32)[None, :], grid_rows, radius)
            * portion[0][None, :]
        )
        col_gauss = gaussian(
            col_ids[:, None], portion[2].astype(jnp.int32)[None, :], grid_cols, radius
        )
        depth_gauss = gaussian(
            depth_ids[None, :], portion[3].astype(jnp.int32)[:, None], grid_depth, radius
        )
        plane_gauss = (row_gauss[:, None, :] * col_gauss[None, :, :]).reshape(
            row_count * col_count, block_size
        )
        added = jnp.dot(
            plane_gauss,
            depth_gauss,
            precision=lax.Precision.HIGHEST,
            preferred_element_type=jnp.float32,
        )
        return (carry_sum + added, None)

    start = jnp.zeros((row_count * col_count, depth_count), jnp.float32)
    result, unused = lax.scan(one_block, start, jnp.arange(slot_total // block_size))
    return result.reshape(row_count, col_count, depth_count)


def by_collectives(
    bias_grid, hill_slab, hill_row, hill_col, hill_depth, hill_level, hill_count, height_levels
):
    rows_dev, cols_dev, depth_bins = bias_grid.shape
    slab_count = lax.axis_size("slab")
    walk_count = lax.axis_size("walk")
    radius = 2 * rows_dev
    grid_rows = rows_dev * slab_count
    grid_cols = cols_dev * walk_count
    walkers_dev, hill_slots = hill_row.shape
    sent_rows = walkers_dev * hill_slots
    capacity = max(2, 4 * sent_rows // slab_count)
    target = hill_slab[:, :, 0].reshape(-1)
    centre_row = target * rows_dev + hill_row.reshape(-1)
    is_live = (
        lax.broadcasted_iota(jnp.int32, (walkers_dev, hill_slots), 1) < hill_count[:, None]
    ).reshape(-1)
    level_match = hill_level.reshape(-1)[:, None] == lax.broadcasted_iota(
        jnp.int32, (1, height_levels.shape[0]), 1
    )
    base_height = jnp.sum(jnp.where(level_match, height_levels[None, :], 0.0), axis=1)
    base_height = jnp.where(is_live, BASE_HEIGHT * base_height, 0.0)
    same_slab = target[:, None] == target[None, :]
    earlier = lax.broadcasted_iota(jnp.int32, (sent_rows, sent_rows), 1) < lax.broadcasted_iota(
        jnp.int32, (sent_rows, sent_rows), 0
    )
    slot_rank = jnp.sum((same_slab & earlier).astype(jnp.int32), axis=1)
    slot_place = target * capacity + slot_rank
    placing = (
        slot_place[:, None] == lax.broadcasted_iota(jnp.int32, (1, slab_count * capacity), 1)
    ).astype(jnp.float32)
    fields = jnp.stack(
        [
            base_height,
            centre_row.astype(jnp.float32),
            hill_col.reshape(-1).astype(jnp.float32),
            hill_depth.reshape(-1).astype(jnp.float32),
        ]
    )
    outgoing = jnp.dot(
        fields, placing, precision=lax.Precision.HIGHEST, preferred_element_type=jnp.float32
    )
    outgoing = outgoing.reshape(4, slab_count, capacity)
    arrived = lax.all_to_all(outgoing, "slab", split_axis=1, concat_axis=1, tiled=True).reshape(
        4, slab_count * capacity
    )
    shared = lax.all_gather(arrived, "walk", axis=1, tiled=True)
    slab_index = lax.axis_index("slab")
    walk_index = lax.axis_index("walk")
    local_row = jnp.clip(shared[1].astype(jnp.int32) - slab_index * rows_dev, 0, rows_dev - 1)
    local_col = shared[2].astype(jnp.int32) - walk_index * cols_dev
    local_depth = jnp.clip(shared[3].astype(jnp.int32), 0, depth_bins - 1)
    owned = (local_col >= 0) & (local_col < cols_dev)
    flat_place = (
        local_row * cols_dev + jnp.clip(local_col, 0, cols_dev - 1)
    ) * depth_bins + local_depth
    picked = bias_grid.reshape(-1)[flat_place]
    centre_value = lax.psum(jnp.where(owned, picked, 0.0), "walk")
    height = shared[0] * jnp.exp(-centre_value / TEMPER)
    hill_lists = jnp.stack([height, shared[1], shared[2], shared[3]])
    col_ids = walk_index * cols_dev + lax.broadcasted_iota(jnp.int32, (cols_dev,), 0)
    depth_ids = lax.broadcasted_iota(jnp.int32, (depth_bins,), 0)
    collected = [hill_lists]
    for offset in (-2, -1, 1, 2):
        collected.append(from_behind(hill_lists, "slab", offset))
    row_ids = slab_index * rows_dev + lax.broadcasted_iota(jnp.int32, (rows_dev,), 0)
    added = deposit(
        row_ids,
        col_ids,
        depth_ids,
        jnp.concatenate(collected, axis=1),
        grid_rows,
        grid_cols,
        depth_bins,
        radius,
    )
    new_bias = bias_grid + added
    highest = lax.pmax(jnp.max(new_bias), ("slab", "walk"))
    free_energy = FREE_SCALE * (highest - new_bias)
    return (new_bias, free_energy)


LANES = 128
F32 = jnp.float32
BF16 = jnp.bfloat16
MESH = pl.DeviceIdType.MESH
NT = (((1,), (1,)), ((), ()))


def wrapped(offset, extent):
    offset = jnp.where(offset >= extent // 2, offset - extent, offset)
    return jnp.where(offset < -(extent // 2), offset + extent, offset)


def profile(offset, radius):
    spread = SIGMA_SHARE * radius
    value = jnp.exp(-(offset * offset) / (2.0 * spread * spread))
    return jnp.where((offset >= -radius) & (offset < radius), value, 0.0)


def halves(value):
    high = value.astype(BF16)
    return high, (value - high.astype(F32)).astype(BF16)


def iota(shape, dim):
    return lax.broadcasted_iota(jnp.int32, shape, dim).astype(F32)


def whole_iota(shape, dim):
    return lax.broadcasted_iota(jnp.int32, shape, dim)


OFFSETS = [(i, j) for i in (-2, -1, 0, 1, 2) for j in (-1, 0, 1)]
HERE = OFFSETS.index((0, 0))


def flipped(index, extent):
    values = [index]
    bit = 1
    while bit < extent:
        turn = bit * (1 - 2 * lax.rem(index // bit, 2))
        values += [value + turn for value in values]
        bit *= 2
    return values


def mesh_steps(slabs, walks):
    slab_at = flipped(lax.axis_index("slab"), slabs)
    walk_at = flipped(lax.axis_index("walk"), walks)

    def place(step):
        return (slab_at[step // walks], walk_at[step % walks])

    return place, range(slabs * walks - 1, 0, -1)


def greet(place, steps):
    barrier = pltpu.get_barrier_semaphore()
    for step in steps:
        pl.semaphore_signal(barrier, inc=1, device_id=place(step), device_id_type=MESH)
    return barrier


def to_all(source, target, send, recv, place, steps):
    return [
        pltpu.make_async_remote_copy(
            source, target, send.at[0], recv.at[0],
            device_id=place(step), device_id_type=MESH,
        )
        for step in steps
    ]


def to_near(source, tables, send, recv, slabs, walks):
    slab, walk = lax.axis_index("slab"), lax.axis_index("walk")
    copies = []
    for n, (i, j) in sorted(enumerate(OFFSETS), key=lambda item: -abs(item[1][0])):
        if n == HERE:
            continue
        device = (lax.rem(slab - i + slabs, slabs), lax.rem(walk - j + walks, walks))
        copies.append(
            pltpu.make_async_remote_copy(
                source, tables.at[n], send.at[0], recv.at[0],
                device_id=device, device_id_type=MESH,
            )
        )
    return copies


def arrival(landing, send, recv, place):
    return pltpu.make_async_remote_copy(
        landing, landing, send.at[0], recv.at[0], device_id=place(1), device_id_type=MESH
    )


def owner_of(at_row, at_col, rows, cols, slabs, walks):
    slab_of = jnp.floor(at_row / rows) - lax.axis_index("slab").astype(F32)
    walk_of = jnp.floor(at_col / cols) - lax.axis_index("walk").astype(F32)
    slab_of = jnp.where(slab_of < -2, slab_of + slabs, slab_of)
    slab_of = jnp.where(slab_of > 2, slab_of - slabs, slab_of)
    walk_of = jnp.where(walk_of < -1, walk_of + walks, walk_of)
    walk_of = jnp.where(walk_of > 1, walk_of - walks, walk_of)
    inside = (jnp.abs(slab_of) <= 2) & (jnp.abs(walk_of) <= 1)
    return jnp.where(inside, (slab_of + 2) * 3 + walk_of + 1, -1.0)


def lane_tops(value):
    most = jnp.max(value, axis=0, keepdims=True)
    top = most[:, 0:LANES]
    for i in range(1, value.shape[1] // LANES):
        top = jnp.maximum(top, most[:, i * LANES : (i + 1) * LANES])
    return top


def as_column(row):
    return jnp.broadcast_to(row, (LANES, LANES)).T


def squeeze(mask, rank):
    lane = whole_iota(mask.shape, 1)
    code = (lane - rank.astype(jnp.int32)) * LANES + lane + LANES * LANES
    code = jnp.where(mask, code, 0)
    step = 1
    while step < LANES:
        came = pltpu.roll(code, LANES - step, axis=1)
        bit = step * LANES
        stays = jnp.where((code & bit) != 0, 0, code)
        code = jnp.where((came & bit) != 0, came, stays)
        step *= 2
    return code & (LANES - 1)


def window_kernel(
    slabs, walks, rows, cols, own_parts, close_blocks,
    bias_in, slab_in, row_in, col_in, depth_in, level_in, count_in, table_in,
    new_ref, top_ref, bias_ref, hills_ref, flag_ref,
    slab_ref, row_ref, col_ref, depth_ref, level_ref, count_ref, table_ref, in_sems,
    mine, hills, bias_parts, picked, tables, chosen, left, right, near, peak, peaks,
    a_send, a_recv, b_send, b_recv, c_send, c_recv,
):
    devices = slabs * walks
    cells, depth = bias_ref.shape
    radius = 2 * rows
    grid_rows, grid_cols = slabs * rows, walks * cols
    slab = lax.axis_index("slab")
    walk = lax.axis_index("walk")
    me = slab * walks + walk
    first_row = (slab * rows).astype(F32)
    first_col = (walk * cols).astype(F32)
    part_depth = depth // own_parts
    place, steps = mesh_steps(slabs, walks)
    barrier = greet(place, steps)

    def bucket_of(at_slab, at_col, at_depth):
        owner = at_slab * walks + jnp.floor(at_col / cols)
        return owner * own_parts + jnp.floor(at_depth / part_depth)

    inputs = (
        (slab_in, slab_ref), (row_in, row_ref), (col_in, col_ref), (depth_in, depth_ref),
        (level_in, level_ref), (count_in, count_ref), (table_in, table_ref), (bias_in, bias_ref),
    )
    fetches = [
        pltpu.make_async_copy(there, here, in_sems.at[i])
        for i, (there, here) in enumerate(inputs)
    ]
    for fetch in fetches:
        fetch.start()
    for fetch in fetches[:-1]:
        fetch.wait()

    def in_row(ref):
        value = ref[...].astype(F32)
        return jnp.concatenate([value[i : i + 1] for i in range(value.shape[0])], axis=1)

    slots = row_ref.shape[1]
    lane = iota((1, LANES), 1)
    live = jnp.zeros((1, LANES), F32)
    for i in range(row_ref.shape[0]):
        inside = (lane >= i * slots) & (lane < i * slots + count_ref[i].astype(F32))
        live = jnp.where(inside, 1.0, live)
    target, centre_col, centre_depth = in_row(slab_ref), in_row(col_ref), in_row(depth_ref)
    bucket = bucket_of(target, centre_col, centre_depth)
    key = jnp.where(live > 0, bucket, float(devices * own_parts)) * LANES + lane
    keys = as_column(key)
    ahead = jnp.sum(jnp.where(keys < key, 1.0, 0.0), axis=0, keepdims=True)
    first = lane * LANES
    inside = (keys >= first) & (keys < first + LANES)
    counts = jnp.sum(jnp.where(inside & (lane < devices * own_parts), 1.0, 0.0), axis=0, keepdims=True)
    col_high = jnp.floor(centre_col / 16.0)
    depth_high = jnp.floor(centre_depth / 16.0)
    unsorted = jnp.concatenate(
        [
            jnp.where(live > 0, in_row(level_ref) + 1.0, 0.0),
            target * rows + in_row(row_ref),
            col_high,
            centre_col - 16.0 * col_high,
            depth_high,
            centre_depth - 16.0 * depth_high,
            live,
            live,
        ],
        axis=0,
    ).astype(BF16)
    order = jnp.where(iota((LANES, LANES), 0) == ahead, 1.0, 0.0).astype(BF16)
    ordered = lax.dot_general(unsorted, order, NT, preferred_element_type=F32)
    level = ordered[0:1]
    base = jnp.zeros((1, LANES), F32)
    for i in range(table_ref.shape[0]):
        base = jnp.where(level == i + 1, BASE_HEIGHT * table_ref[i], base)
    fields = (
        base,
        ordered[1:2],
        ordered[2:3] * 16.0 + ordered[3:4],
        ordered[4:5] * 16.0 + ordered[5:6],
        counts,
    )
    for i, field in enumerate(fields):
        mine[i : i + 1, :] = field
        hills[me, i : i + 1, :] = field

    pl.semaphore_wait(barrier, devices - 1)
    sent = pl.ds(0, len(fields))
    a_copies = to_all(mine.at[sent], hills.at[me, sent], a_send, a_recv, place, steps)
    for copy in a_copies:
        copy.start()
    others = pl.ds(0, devices - 1)
    a_all = arrival(hills.at[others, sent], a_send, a_recv, place)

    fetches[-1].wait()
    high, low = halves(bias_ref[...])
    for part in range(own_parts):
        span = slice(part * part_depth, (part + 1) * part_depth)
        bias_parts[part, :, :part_depth] = high[:, span]
        bias_parts[part, :, part_depth:] = low[:, span]
    counting = jnp.concatenate(
        [
            jnp.where(iota((LANES, LANES), 0) < iota((LANES, LANES), 1), 1.0, 0.0),
            jnp.ones((LANES, LANES), F32),
        ],
        axis=1,
    ).astype(BF16)
    before = jnp.where(
        iota((devices, devices), 1) < iota((devices, devices), 0), 1.0, 0.0
    ).astype(BF16)
    lanes = whole_iota((devices, LANES), 1)

    a_all.wait_recv()

    all_base, all_row, all_col, all_depth, counts = [hills[:, i, :] for i in range(5)]
    there = all_base > 0
    owner = jnp.where(there, owner_of(all_row, all_col, rows, cols, slabs, walks), -1.0)

    exact = counts.astype(BF16)
    starts = jnp.dot(exact, counting[:, :LANES], preferred_element_type=F32)
    reached = jnp.dot(before, exact, preferred_element_type=F32)

    def listed(values, index, moved, count, blocks):
        taken = [jnp.take_along_axis(value, index, axis=1) for value in values]
        result = []
        for block in range(blocks):
            spot = moved + block * LANES
            valid = (spot >= 0) & (spot < count)
            result.append([jnp.sum(jnp.where(valid, t, 0.0), axis=0, keepdims=True) for t in taken])
        return result

    own_cell = (all_row - first_row) * cols + all_col - first_col
    own_code = own_cell * depth + all_depth
    own_over = jnp.zeros((devices, LANES), jnp.int32)
    for part in range(own_parts):
        here = jnp.full((devices, LANES), me * own_parts + part, jnp.int32)
        own_start, own_count, own_reached = [
            jnp.take_along_axis(value, here, axis=1).astype(jnp.int32)
            for value in (starts, counts, reached)
        ]
        own_over = jnp.maximum(own_over, own_reached + own_count - LANES)
        moved = lanes - own_reached
        (own_list,) = listed(
            [own_code], (own_start + moved) & (LANES - 1), moved, own_count, 1
        )
        code = own_list[0].astype(jnp.int32)
        at = (code & (depth - 1)) - part * part_depth
        select = jnp.where(whole_iota((part_depth, LANES), 0) == at, 1.0, 0.0).astype(BF16)
        lines = jnp.dot(
            bias_parts[part], jnp.concatenate([select, select], axis=0),
            preferred_element_type=F32,
        )
        hit = whole_iota((cells, LANES), 0) == (code >> (depth.bit_length() - 1))
        value = jnp.sum(jnp.where(hit, lines, 0.0), axis=0, keepdims=True)
        picked[part : part + 1, :] = jnp.exp(-value / TEMPER)

    for copy in to_near(picked, tables, b_send, b_recv, slabs, walks):
        copy.start()
    b_all = arrival(tables.at[pl.ds(0, len(OFFSETS) - 1)], b_send, b_recv, place)
    a_all.wait_send()

    def past(away, extent, limit):
        away = away + (radius - 1)
        away = jnp.where(away < 0, away + extent, away)
        away = jnp.where(away >= extent, away - extent, away)
        return away < limit

    half_cols, half_depth, total = cols // 2, depth // 2, close_blocks * LANES
    close_row = there & past(all_row - first_row, grid_rows, rows + 2 * radius - 1)
    quarters = [(a, b) for a in (0, 1) for b in (0, 1)]
    close = [
        close_row
        & past(all_col - first_col - a * half_cols, grid_cols, half_cols + 2 * radius - 1)
        & past(all_depth - b * half_depth, depth, half_depth + 2 * radius - 1)
        for a, b in quarters
    ]
    ones = jnp.concatenate([jnp.where(mask, 1.0, 0.0) for mask in close], axis=0)
    both = jnp.dot(ones.astype(BF16), counting, preferred_element_type=F32)
    close_count = jnp.concatenate(
        [both[q * devices : (q + 1) * devices, LANES:] for q in range(4)], axis=1
    )
    close_reached = jnp.dot(before, close_count.astype(BF16), preferred_element_type=F32)
    close_over = jnp.max(close_reached + close_count - total)
    over = jnp.maximum(jnp.max(own_over.astype(F32)), close_over)
    close_lane = squeeze(ones > 0, both[:, :LANES])
    all_bucket = bucket_of(jnp.floor(all_row / rows), all_col, all_depth).astype(jnp.int32)
    shift = jnp.take_along_axis(reached - starts, all_bucket, axis=1)
    spot_part = owner * own_parts + jnp.floor(all_depth / part_depth)
    spot = lanes.astype(F32) + shift + spot_part * LANES
    position = (all_row * grid_cols + all_col) * depth + all_depth
    depth_lane = iota((LANES, LANES), 1)
    col_id = iota((half_cols, LANES), 0)
    depth_bits, col_bits = depth.bit_length() - 1, grid_cols.bit_length() - 1
    for q, (a, b) in enumerate(quarters):
        span = slice(q * LANES, (q + 1) * LANES)
        moved = lanes - close_reached[:, span].astype(jnp.int32)
        index = jnp.take_along_axis(
            close_lane[q * devices : (q + 1) * devices], moved & (LANES - 1), axis=1
        )
        lists = listed(
            [all_base, position, spot], index, moved, close_count[:, span].astype(jnp.int32),
            close_blocks,
        )
        for block, parts in enumerate(lists):
            code = parts[1].astype(jnp.int32)
            at_depth = (code & (depth - 1)).astype(F32)
            at_col = ((code >> depth_bits) & (grid_cols - 1)).astype(F32)
            at_row = (code >> (depth_bits + col_bits)).astype(F32)
            line = q * close_blocks + block
            for i, part in enumerate((parts[0], at_row, parts[2])):
                chosen[i, line : line + 1, :] = part
            at = as_column(at_depth)
            for i in range(half_depth // LANES):
                offset = depth_lane + (b * half_depth + i * LANES) - at
                high, low = halves(profile(wrapped(offset, depth), radius))
                for j, half in enumerate((high, high, low)):
                    rows_at = slice(j * total + block * LANES, j * total + (block + 1) * LANES)
                    right[q, rows_at, i * LANES : (i + 1) * LANES] = half
            offset = col_id + (first_col + a * half_cols) - at_col
            near[q, :, block * LANES : (block + 1) * LANES] = profile(
                wrapped(offset, grid_cols), radius
            )
    hills_ref[...] = hills[:, 0:4, :]

    at_base, at_row = chosen[0], chosen[1]
    at_spot = chosen[2].astype(jnp.int32)
    at_lane = at_spot & (LANES - 1)
    at_table = at_spot >> (LANES.bit_length() - 1)
    row_parts = [
        at_base * profile(wrapped(first_row + r - at_row, grid_rows), radius) for r in range(rows)
    ]

    b_all.wait_recv()
    factor = jnp.zeros(at_base.shape, F32)
    for n in range(len(OFFSETS)):
        for part in range(own_parts):
            table = picked if n == HERE else tables.at[n]
            line = jnp.broadcast_to(table[part : part + 1, :], factor.shape)
            value = jnp.take_along_axis(line, at_lane, axis=1)
            factor = jnp.where(at_table == n * own_parts + part, value, factor)
    row_parts = [factor * part for part in row_parts]
    tops = []
    for q, (a, b) in enumerate(quarters):
        for r in range(rows):
            for block in range(close_blocks):
                line = q * close_blocks + block
                span = slice(block * LANES, (block + 1) * LANES)
                high, low = halves(near[q, :, span] * row_parts[r][line : line + 1])
                for j, half in enumerate((high, low, high)):
                    lanes_at = slice(j * total + block * LANES, j * total + (block + 1) * LANES)
                    left[q, r * half_cols : (r + 1) * half_cols, lanes_at] = half
        added = jnp.dot(left[q], right[q], preferred_element_type=F32)
        depths = slice(b * half_depth, (b + 1) * half_depth)
        for r in range(rows):
            first = r * cols + a * half_cols
            value = added[r * half_cols : (r + 1) * half_cols]
            value = bias_ref[first : first + half_cols, depths] + value
            new_ref[first : first + half_cols, depths] = value
            tops.append(lane_tops(value))
    top = jnp.where(over > 0, jnp.inf, functools.reduce(jnp.maximum, tops))
    peak[...] = top
    peaks[me] = top
    for copy in to_all(peak, peaks.at[me], c_send, c_recv, place, steps):
        copy.start()
    c_all = arrival(peaks.at[others], c_send, c_recv, place)
    b_all.wait_send()
    c_all.wait_send()
    c_all.wait_recv()
    highest = jnp.max(peaks[...])
    top_ref[...] = jnp.broadcast_to(highest, top_ref.shape)
    flag_ref[0] = jnp.where(highest == jnp.inf, 1, 0)


def by_kernel(own_parts, close_blocks, slabs, walks, arrays):
    bias_grid, hill_slab, hill_row, hill_col, hill_depth, hill_level, hill_count, table = arrays
    rows, cols, depth = bias_grid.shape
    devices = slabs * walks
    total = close_blocks * LANES
    cells = rows * cols
    walkers = hill_row.shape
    vmem = pl.BlockSpec(memory_space=pltpu.VMEM)
    smem = pl.BlockSpec(memory_space=pltpu.SMEM)
    hbm = pl.BlockSpec(memory_space=pltpu.HBM)
    return pl.pallas_call(
        functools.partial(window_kernel, slabs, walks, rows, cols, own_parts, close_blocks),
        out_shape=(
            jax.ShapeDtypeStruct((cells, depth), F32),
            jax.ShapeDtypeStruct((8, LANES), F32),
            jax.ShapeDtypeStruct((cells, depth), F32),
            jax.ShapeDtypeStruct((devices, 4, LANES), F32),
            jax.ShapeDtypeStruct((1,), jnp.int32),
        ),
        in_specs=[hbm] * 8,
        out_specs=(vmem, vmem, vmem, vmem, smem),
        scratch_shapes=[
            pltpu.VMEM(walkers, jnp.int32),
            pltpu.VMEM(walkers, jnp.int32),
            pltpu.VMEM(walkers, jnp.int32),
            pltpu.VMEM(walkers, jnp.int32),
            pltpu.VMEM(walkers, jnp.int32),
            pltpu.SMEM(hill_count.shape, jnp.int32),
            pltpu.SMEM(table.shape, F32),
            pltpu.SemaphoreType.DMA((8,)),
            pltpu.VMEM((8, LANES), F32),
            pltpu.VMEM((devices, 8, LANES), F32),
            pltpu.VMEM((own_parts, cells, 2 * depth // own_parts), BF16),
            pltpu.VMEM((own_parts, LANES), F32),
            pltpu.VMEM((len(OFFSETS), own_parts, LANES), F32),
            pltpu.VMEM((3, 4 * close_blocks, LANES), F32),
            pltpu.VMEM((4, cells // 2, 3 * total), BF16),
            pltpu.VMEM((4, 3 * total, depth // 2), BF16),
            pltpu.VMEM((4, cols // 2, total), F32),
            pltpu.VMEM((1, LANES), F32),
            pltpu.VMEM((devices, 1, LANES), F32),
            pltpu.SemaphoreType.DMA((1,)),
            pltpu.SemaphoreType.DMA((1,)),
            pltpu.SemaphoreType.DMA((1,)),
            pltpu.SemaphoreType.DMA((1,)),
            pltpu.SemaphoreType.DMA((1,)),
            pltpu.SemaphoreType.DMA((1,)),
        ],
        compiler_params=pltpu.CompilerParams(
            collective_id=0, has_side_effects=True, vmem_limit_bytes=58 * 2**20
        ),
    )(
        bias_grid.reshape(cells, depth),
        hill_slab.reshape(hill_row.shape),
        hill_row,
        hill_col,
        hill_depth,
        hill_level,
        hill_count,
        table,
    )


def full_kernel(
    slabs, walks, rows, cols,
    bias_ref, hills_ref, new_ref, top_ref,
    bias_high, bias_low, picked, tables, peak, peaks,
    b_send, b_recv, c_send, c_recv,
):
    devices = slabs * walks
    cells, depth = bias_ref.shape
    radius = 2 * rows
    grid_rows, grid_cols = slabs * rows, walks * cols
    slab = lax.axis_index("slab")
    walk = lax.axis_index("walk")
    me = slab * walks + walk
    first_row = (slab * rows).astype(F32)
    first_col = (walk * cols).astype(F32)
    place, steps = mesh_steps(slabs, walks)
    barrier = greet(place, steps)
    high, low = halves(bias_ref[...])
    bias_high[...] = high
    bias_low[...] = low

    def pick(sender, carry):
        part = hills_ref[sender]
        cell = (part[1:2] - first_row) * cols + part[2:3] - first_col
        owner = owner_of(part[1:2], part[2:3], rows, cols, slabs, walks)
        cell = jnp.where(owner == HERE, cell, -1.0)
        select = jnp.where(iota((depth, LANES), 0) == part[3:4], 1.0, 0.0).astype(BF16)
        lines = jnp.dot(bias_high[...], select, preferred_element_type=F32)
        lines = lines + jnp.dot(bias_low[...], select, preferred_element_type=F32)
        hit = iota((cells, LANES), 0) == cell
        value = jnp.sum(jnp.where(hit, lines, 0.0), axis=0, keepdims=True)
        picked[pl.ds(sender, 1), :] = jnp.exp(-value / TEMPER)
        return carry

    lax.fori_loop(0, devices, pick, 0)
    pl.semaphore_wait(barrier, devices - 1)
    for copy in to_near(picked, tables, b_send, b_recv, slabs, walks):
        copy.start()
    b_all = arrival(tables.at[pl.ds(0, len(OFFSETS) - 1)], b_send, b_recv, place)
    tables[HERE] = picked[...]
    b_all.wait_recv()
    new_ref[...] = bias_ref[...]

    def add(sender, carry):
        part = hills_ref[sender]
        owner = owner_of(part[1:2], part[2:3], rows, cols, slabs, walks)
        height = jnp.zeros((1, LANES), F32)
        for n in range(len(OFFSETS)):
            height = jnp.where(owner == n, part[0:1] * tables[n, pl.ds(sender, 1), :], height)
        at = as_column(part[3:4])[:, 0:1]
        right = profile(wrapped(iota((LANES, depth), 1) - at, depth), radius)
        right_high, right_low = halves(right)
        col_offset = iota((cols, LANES), 0) + first_col - part[2:3]
        near = profile(wrapped(col_offset, grid_cols), radius)
        for r in range(rows):
            along = profile(wrapped(first_row + r - part[1:2], grid_rows), radius)
            left_high, left_low = halves(near * (height * along))
            added = jnp.dot(left_high, right_high, preferred_element_type=F32)
            added += jnp.dot(left_low, right_high, preferred_element_type=F32)
            added += jnp.dot(left_high, right_low, preferred_element_type=F32)
            new_ref[r * cols : (r + 1) * cols, :] += added
        return carry

    lax.fori_loop(0, devices, add, 0)
    top = lane_tops(new_ref[...])
    peak[...] = top
    peaks[me] = top
    for copy in to_all(peak, peaks.at[me], c_send, c_recv, place, steps):
        copy.start()
    c_all = arrival(peaks.at[pl.ds(0, devices - 1)], c_send, c_recv, place)
    b_all.wait_send()
    c_all.wait_send()
    c_all.wait_recv()
    top_ref[...] = jnp.broadcast_to(jnp.max(peaks[...]), top_ref.shape)


def by_full_kernel(rows, slabs, walks, bias, hills):
    cells, depth = bias.shape
    devices = slabs * walks
    vmem = pl.BlockSpec(memory_space=pltpu.VMEM)
    return pl.pallas_call(
        functools.partial(full_kernel, slabs, walks, rows, cells // rows),
        out_shape=(
            jax.ShapeDtypeStruct((cells, depth), F32),
            jax.ShapeDtypeStruct((8, LANES), F32),
        ),
        in_specs=[vmem] * 2,
        out_specs=(vmem, vmem),
        scratch_shapes=[
            pltpu.VMEM((cells, depth), BF16),
            pltpu.VMEM((cells, depth), BF16),
            pltpu.VMEM((devices, LANES), F32),
            pltpu.VMEM((len(OFFSETS), devices, LANES), F32),
            pltpu.VMEM((1, LANES), F32),
            pltpu.VMEM((devices, 1, LANES), F32),
            pltpu.SemaphoreType.DMA((1,)),
            pltpu.SemaphoreType.DMA((1,)),
            pltpu.SemaphoreType.DMA((1,)),
            pltpu.SemaphoreType.DMA((1,)),
        ],
        compiler_params=pltpu.CompilerParams(
            collective_id=1, has_side_effects=True, vmem_limit_bytes=20 * 2**20
        ),
    )(bias, hills)


def output_kernel(new_ref, top_ref, new_out, free_out, free_ref, sems):
    parts = 4
    span = new_ref.shape[0] // parts
    first = pltpu.make_async_copy(new_ref, new_out, sems.at[0])
    first.start()
    copies = [first]
    for i in range(parts):
        rows = pl.ds(i * span, span)
        free_ref[rows, :] = FREE_SCALE * (top_ref[0:1, 0:1] - new_ref[rows, :])
        copy = pltpu.make_async_copy(free_ref.at[rows], free_out.at[rows], sems.at[1 + i])
        copy.start()
        copies.append(copy)
    for copy in copies:
        copy.wait()


def outputs(new_bias, top):
    hbm = pl.BlockSpec(memory_space=pltpu.HBM)
    return pl.pallas_call(
        output_kernel,
        out_shape=(jax.ShapeDtypeStruct(new_bias.shape, F32),) * 2,
        in_specs=[pl.BlockSpec(memory_space=pltpu.VMEM)] * 2,
        out_specs=(hbm, hbm),
        scratch_shapes=[pltpu.VMEM(new_bias.shape, F32), pltpu.SemaphoreType.DMA((5,))],
        compiler_params=pltpu.CompilerParams(vmem_limit_bytes=4 * 2**20),
    )(new_bias, top)


def per_device(*arrays):
    bias_grid = arrays[0]
    shape = bias_grid.shape
    slabs, walks = lax.axis_size("slab"), lax.axis_size("walk")
    devices = slabs * walks
    fits = (
        arrays[2].size == LANES
        and slabs >= 5
        and walks >= 3
        and devices <= 64
        and devices % 8 == 0
        and shape[1] % LANES == 0
        and shape[1] >= 2 * shape[0]
        and shape[2] % (4 * LANES) == 0
        and max(walks * shape[1], shape[2]) <= 4096
        and max(slabs * shape[0], arrays[7].size) <= 255
        and all(size & (size - 1) == 0 for size in (slabs, walks, shape[1], shape[2]))
        and devices * shape[0] * shape[1] * shape[2] <= 2**24
    )
    if not fits:
        return by_collectives(*arrays)

    def finish(new_bias, top):
        new_out, free_out = outputs(new_bias, top)
        return new_out.reshape(shape), free_out.reshape(shape)

    new_bias, top, bias, hills, flag = by_kernel(min(4, LANES // devices), 2, slabs, walks, arrays)
    return lax.cond(
        flag.reshape(()),
        lambda: finish(*by_full_kernel(shape[0], slabs, walks, bias, hills)),
        lambda: finish(new_bias, top),
    )


def solution(mesh):
    in_specs = (
        P("slab", "walk", None),
        P(("slab", "walk"), None, None),
        P(("slab", "walk"), None),
        P(("slab", "walk"), None),
        P(("slab", "walk"), None),
        P(("slab", "walk"), None),
        P(("slab", "walk")),
        P(),
    )
    out_specs = (P("slab", "walk", None), P("slab", "walk", None))
    return jax.shard_map(
        per_device, mesh=mesh, in_specs=in_specs, out_specs=out_specs, check_vma=False
    )
```

```python
import functools
import math

import jax
import jax.numpy as jnp
from jax import lax
from jax.experimental import pallas as pl
from jax.experimental.pallas import tpu as pltpu
from jax.sharding import PartitionSpec as P

BASE_HEIGHT = 1.2
TEMPER = 4.0
SIGMA_SHARE = 0.3125
FREE_SCALE = 10.0 / 9.0


def from_behind(block, axis, distance):
    devices = range(lax.axis_size(axis))
    route = [((i - distance) % len(devices), i) for i in devices]
    return lax.ppermute(block, axis, route)


def gaussian(position, centre, extent, radius):
    offset = jnp.mod(position - centre + extent // 2, extent) - extent // 2
    inside = (offset >= -radius) & (offset < radius)
    spread = SIGMA_SHARE * radius
    distance = offset.astype(jnp.float32)
    return jnp.where(inside, jnp.exp(-(distance * distance) / (2.0 * spread * spread)), 0.0)


def deposit(row_ids, col_ids, depth_ids, hill_lists, grid_rows, grid_cols, grid_depth, radius):
    slot_total = hill_lists.shape[1]
    block_size = math.gcd(slot_total, 256)
    row_count = row_ids.shape[0]
    col_count = col_ids.shape[0]
    depth_count = depth_ids.shape[0]

    def one_block(carry_sum, index):
        portion = lax.dynamic_slice_in_dim(hill_lists, index * block_size, block_size, 1)
        row_gauss = (
            gaussian(row_ids[:, None], portion[1].astype(jnp.int32)[None, :], grid_rows, radius)
            * portion[0][None, :]
        )
        col_gauss = gaussian(
            col_ids[:, None], portion[2].astype(jnp.int32)[None, :], grid_cols, radius
        )
        depth_gauss = gaussian(
            depth_ids[None, :], portion[3].astype(jnp.int32)[:, None], grid_depth, radius
        )
        plane_gauss = (row_gauss[:, None, :] * col_gauss[None, :, :]).reshape(
            row_count * col_count, block_size
        )
        added = jnp.dot(
            plane_gauss,
            depth_gauss,
            precision=lax.Precision.HIGHEST,
            preferred_element_type=jnp.float32,
        )
        return (carry_sum + added, None)

    start = jnp.zeros((row_count * col_count, depth_count), jnp.float32)
    result, unused = lax.scan(one_block, start, jnp.arange(slot_total // block_size))
    return result.reshape(row_count, col_count, depth_count)


def by_collectives(
    bias_grid, hill_slab, hill_row, hill_col, hill_depth, hill_level, hill_count, height_levels
):
    rows_dev, cols_dev, depth_bins = bias_grid.shape
    slab_count = lax.axis_size("slab")
    walk_count = lax.axis_size("walk")
    radius = 2 * rows_dev
    grid_rows = rows_dev * slab_count
    grid_cols = cols_dev * walk_count
    walkers_dev, hill_slots = hill_row.shape
    sent_rows = walkers_dev * hill_slots
    capacity = max(2, 4 * sent_rows // slab_count)
    target = hill_slab[:, :, 0].reshape(-1)
    centre_row = target * rows_dev + hill_row.reshape(-1)
    is_live = (
        lax.broadcasted_iota(jnp.int32, (walkers_dev, hill_slots), 1) < hill_count[:, None]
    ).reshape(-1)
    level_match = hill_level.reshape(-1)[:, None] == lax.broadcasted_iota(
        jnp.int32, (1, height_levels.shape[0]), 1
    )
    base_height = jnp.sum(jnp.where(level_match, height_levels[None, :], 0.0), axis=1)
    base_height = jnp.where(is_live, BASE_HEIGHT * base_height, 0.0)
    same_slab = target[:, None] == target[None, :]
    earlier = lax.broadcasted_iota(jnp.int32, (sent_rows, sent_rows), 1) < lax.broadcasted_iota(
        jnp.int32, (sent_rows, sent_rows), 0
    )
    slot_rank = jnp.sum((same_slab & earlier).astype(jnp.int32), axis=1)
    slot_place = target * capacity + slot_rank
    placing = (
        slot_place[:, None] == lax.broadcasted_iota(jnp.int32, (1, slab_count * capacity), 1)
    ).astype(jnp.float32)
    fields = jnp.stack(
        [
            base_height,
            centre_row.astype(jnp.float32),
            hill_col.reshape(-1).astype(jnp.float32),
            hill_depth.reshape(-1).astype(jnp.float32),
        ]
    )
    outgoing = jnp.dot(
        fields, placing, precision=lax.Precision.HIGHEST, preferred_element_type=jnp.float32
    )
    outgoing = outgoing.reshape(4, slab_count, capacity)
    arrived = lax.all_to_all(outgoing, "slab", split_axis=1, concat_axis=1, tiled=True).reshape(
        4, slab_count * capacity
    )
    shared = lax.all_gather(arrived, "walk", axis=1, tiled=True)
    slab_index = lax.axis_index("slab")
    walk_index = lax.axis_index("walk")
    local_row = jnp.clip(shared[1].astype(jnp.int32) - slab_index * rows_dev, 0, rows_dev - 1)
    local_col = shared[2].astype(jnp.int32) - walk_index * cols_dev
    local_depth = jnp.clip(shared[3].astype(jnp.int32), 0, depth_bins - 1)
    owned = (local_col >= 0) & (local_col < cols_dev)
    flat_place = (
        local_row * cols_dev + jnp.clip(local_col, 0, cols_dev - 1)
    ) * depth_bins + local_depth
    picked = bias_grid.reshape(-1)[flat_place]
    centre_value = lax.psum(jnp.where(owned, picked, 0.0), "walk")
    height = shared[0] * jnp.exp(-centre_value / TEMPER)
    hill_lists = jnp.stack([height, shared[1], shared[2], shared[3]])
    col_ids = walk_index * cols_dev + lax.broadcasted_iota(jnp.int32, (cols_dev,), 0)
    depth_ids = lax.broadcasted_iota(jnp.int32, (depth_bins,), 0)
    collected = [hill_lists]
    for offset in (-2, -1, 1, 2):
        collected.append(from_behind(hill_lists, "slab", offset))
    row_ids = slab_index * rows_dev + lax.broadcasted_iota(jnp.int32, (rows_dev,), 0)
    added = deposit(
        row_ids,
        col_ids,
        depth_ids,
        jnp.concatenate(collected, axis=1),
        grid_rows,
        grid_cols,
        depth_bins,
        radius,
    )
    new_bias = bias_grid + added
    highest = lax.pmax(jnp.max(new_bias), ("slab", "walk"))
    free_energy = FREE_SCALE * (highest - new_bias)
    return (new_bias, free_energy)


LANES = 128
F32 = jnp.float32
BF16 = jnp.bfloat16
MESH = pl.DeviceIdType.MESH
NT = (((1,), (1,)), ((), ()))


def wrapped(offset, extent):
    offset = jnp.where(offset >= extent // 2, offset - extent, offset)
    return jnp.where(offset < -(extent // 2), offset + extent, offset)


def profile(offset, radius):
    spread = SIGMA_SHARE * radius
    value = jnp.exp(-(offset * offset) / (2.0 * spread * spread))
    return jnp.where((offset >= -radius) & (offset < radius), value, 0.0)


def halves(value):
    high = value.astype(BF16)
    return high, (value - high.astype(F32)).astype(BF16)


def iota(shape, dim):
    return lax.broadcasted_iota(jnp.int32, shape, dim).astype(F32)


def whole_iota(shape, dim):
    return lax.broadcasted_iota(jnp.int32, shape, dim)


OFFSETS = [(i, j) for i in (-2, -1, 0, 1, 2) for j in (-1, 0, 1)]
HERE = OFFSETS.index((0, 0))


def flipped(index, extent):
    values = [index]
    bit = 1
    while bit < extent:
        turn = bit * (1 - 2 * lax.rem(index // bit, 2))
        values += [value + turn for value in values]
        bit *= 2
    return values


def mesh_steps(slabs, walks):
    slab_at = flipped(lax.axis_index("slab"), slabs)
    walk_at = flipped(lax.axis_index("walk"), walks)

    def place(step):
        return (slab_at[step // walks], walk_at[step % walks])

    return place, range(slabs * walks - 1, 0, -1)


def greet(place, steps):
    barrier = pltpu.get_barrier_semaphore()
    for step in steps:
        pl.semaphore_signal(barrier, inc=1, device_id=place(step), device_id_type=MESH)
    return barrier


def to_all(source, target, send, recv, place, steps):
    return [
        pltpu.make_async_remote_copy(
            source, target, send.at[0], recv.at[0],
            device_id=place(step), device_id_type=MESH,
        )
        for step in steps
    ]


def to_near(source, tables, send, recv, slabs, walks):
    slab, walk = lax.axis_index("slab"), lax.axis_index("walk")
    copies = []
    for n, (i, j) in sorted(enumerate(OFFSETS), key=lambda item: -abs(item[1][0])):
        if n == HERE:
            continue
        device = (lax.rem(slab - i + slabs, slabs), lax.rem(walk - j + walks, walks))
        copies.append(
            pltpu.make_async_remote_copy(
                source, tables.at[n], send.at[0], recv.at[0],
                device_id=device, device_id_type=MESH,
            )
        )
    return copies


def arrival(landing, send, recv, place):
    return pltpu.make_async_remote_copy(
        landing, landing, send.at[0], recv.at[0], device_id=place(1), device_id_type=MESH
    )


def owner_of(at_row, at_col, rows, cols, slabs, walks):
    slab_of = jnp.floor(at_row / rows) - lax.axis_index("slab").astype(F32)
    walk_of = jnp.floor(at_col / cols) - lax.axis_index("walk").astype(F32)
    slab_of = jnp.where(slab_of < -2, slab_of + slabs, slab_of)
    slab_of = jnp.where(slab_of > 2, slab_of - slabs, slab_of)
    walk_of = jnp.where(walk_of < -1, walk_of + walks, walk_of)
    walk_of = jnp.where(walk_of > 1, walk_of - walks, walk_of)
    inside = (jnp.abs(slab_of) <= 2) & (jnp.abs(walk_of) <= 1)
    return jnp.where(inside, (slab_of + 2) * 3 + walk_of + 1, -1.0)


def lane_tops(value):
    most = jnp.max(value, axis=0, keepdims=True)
    top = most[:, 0:LANES]
    for i in range(1, value.shape[1] // LANES):
        top = jnp.maximum(top, most[:, i * LANES : (i + 1) * LANES])
    return top


def as_column(row):
    return jnp.broadcast_to(row, (LANES, LANES)).T


def squeeze(mask, rank):
    lane = whole_iota(mask.shape, 1)
    code = (lane - rank.astype(jnp.int32)) * LANES + lane + LANES * LANES
    code = jnp.where(mask, code, 0)
    step = 1
    while step < LANES:
        came = pltpu.roll(code, LANES - step, axis=1)
        bit = step * LANES
        stays = jnp.where((code & bit) != 0, 0, code)
        code = jnp.where((came & bit) != 0, came, stays)
        step *= 2
    return code & (LANES - 1)


def window_kernel(
    slabs, walks, rows, cols, own_parts, close_blocks,
    bias_in, slab_in, row_in, col_in, depth_in, level_in, count_in, table_in,
    new_ref, top_ref, bias_ref, hills_ref, flag_ref,
    slab_ref, row_ref, col_ref, depth_ref, level_ref, count_ref, table_ref, in_sems,
    mine, hills, bias_parts, picked, tables, chosen, left, right, near, peak, peaks,
    a_send, a_recv, h_send, h_recv, b_send, b_recv, c_send, c_recv,
):
    devices = slabs * walks
    cells, depth = bias_ref.shape
    radius = 2 * rows
    grid_rows, grid_cols = slabs * rows, walks * cols
    slab = lax.axis_index("slab")
    walk = lax.axis_index("walk")
    me = slab * walks + walk
    first_row = (slab * rows).astype(F32)
    first_col = (walk * cols).astype(F32)
    part_depth = depth // own_parts
    place, steps = mesh_steps(slabs, walks)
    barrier = greet(place, steps)

    def bucket_of(at_slab, at_col, at_depth):
        owner = at_slab * walks + jnp.floor(at_col / cols)
        return owner * own_parts + jnp.floor(at_depth / part_depth)

    inputs = (
        (slab_in, slab_ref), (row_in, row_ref), (col_in, col_ref), (depth_in, depth_ref),
        (level_in, level_ref), (count_in, count_ref), (table_in, table_ref), (bias_in, bias_ref),
    )
    fetches = [
        pltpu.make_async_copy(there, here, in_sems.at[i])
        for i, (there, here) in enumerate(inputs)
    ]
    for fetch in fetches:
        fetch.start()
    for fetch in fetches[:-1]:
        fetch.wait()

    def in_row(ref):
        value = ref[...].astype(F32)
        return jnp.concatenate([value[i : i + 1] for i in range(value.shape[0])], axis=1)

    slots = row_ref.shape[1]
    lane = iota((1, LANES), 1)
    live = jnp.zeros((1, LANES), F32)
    for i in range(row_ref.shape[0]):
        inside = (lane >= i * slots) & (lane < i * slots + count_ref[i].astype(F32))
        live = jnp.where(inside, 1.0, live)
    target, centre_col, centre_depth = in_row(slab_ref), in_row(col_ref), in_row(depth_ref)
    bucket = bucket_of(target, centre_col, centre_depth)
    key = jnp.where(live > 0, bucket, float(devices * own_parts)) * LANES + lane
    keys = as_column(key)
    ahead = jnp.sum(jnp.where(keys < key, 1.0, 0.0), axis=0, keepdims=True)
    first = lane * LANES
    inside = (keys >= first) & (keys < first + LANES)
    counts = jnp.sum(jnp.where(inside & (lane < devices * own_parts), 1.0, 0.0), axis=0, keepdims=True)
    col_high = jnp.floor(centre_col / 16.0)
    depth_high = jnp.floor(centre_depth / 16.0)
    unsorted = jnp.concatenate(
        [
            jnp.where(live > 0, in_row(level_ref) + 1.0, 0.0),
            target * rows + in_row(row_ref),
            col_high,
            centre_col - 16.0 * col_high,
            depth_high,
            centre_depth - 16.0 * depth_high,
            live,
            live,
        ],
        axis=0,
    ).astype(BF16)
    order = jnp.where(iota((LANES, LANES), 0) == ahead, 1.0, 0.0).astype(BF16)
    ordered = lax.dot_general(unsorted, order, NT, preferred_element_type=F32)
    level = ordered[0:1]
    base = jnp.zeros((1, LANES), F32)
    for i in range(table_ref.shape[0]):
        base = jnp.where(level == i + 1, BASE_HEIGHT * table_ref[i], base)
    fields = (
        counts,
        ordered[1:2],
        ordered[2:3] * 16.0 + ordered[3:4],
        ordered[4:5] * 16.0 + ordered[5:6],
        base,
    )
    for i, field in enumerate(fields):
        mine[i : i + 1, :] = field
        hills[me, i : i + 1, :] = field

    pl.semaphore_wait(barrier, devices - 1)
    others = pl.ds(0, devices - 1)
    places, heights = pl.ds(0, 4), pl.ds(4, 1)
    for copy in to_all(mine.at[places], hills.at[me, places], a_send, a_recv, place, steps):
        copy.start()
    a_all = arrival(hills.at[others, places], a_send, a_recv, place)
    for copy in to_all(mine.at[heights], hills.at[me, heights], h_send, h_recv, place, steps):
        copy.start()
    h_all = arrival(hills.at[others, heights], h_send, h_recv, place)

    fetches[-1].wait()
    high, low = halves(bias_ref[...])
    for part in range(own_parts):
        span = slice(part * part_depth, (part + 1) * part_depth)
        bias_parts[part, :, :part_depth] = high[:, span]
        bias_parts[part, :, part_depth:] = low[:, span]
    counting = jnp.concatenate(
        [
            jnp.where(iota((LANES, LANES), 0) < iota((LANES, LANES), 1), 1.0, 0.0),
            jnp.ones((LANES, LANES), F32),
        ],
        axis=1,
    ).astype(BF16)
    before = jnp.where(
        iota((devices, devices), 1) < iota((devices, devices), 0), 1.0, 0.0
    ).astype(BF16)
    lanes = whole_iota((devices, LANES), 1)

    a_all.wait_recv()

    counts, all_row, all_col, all_depth = [hills[:, i, :] for i in range(4)]

    exact = counts.astype(BF16)
    starts = jnp.dot(exact, counting[:, :LANES], preferred_element_type=F32)
    reached = jnp.dot(before, exact, preferred_element_type=F32)

    def listed(values, index, moved, count, blocks):
        taken = [jnp.take_along_axis(value, index, axis=1) for value in values]
        result = []
        for block in range(blocks):
            spot = moved + block * LANES
            valid = (spot >= 0) & (spot < count)
            result.append([jnp.sum(jnp.where(valid, t, 0.0), axis=0, keepdims=True) for t in taken])
        return result

    own_cell = (all_row - first_row) * cols + all_col - first_col
    own_code = own_cell * depth + all_depth
    own_over = jnp.zeros((devices, LANES), jnp.int32)
    for part in range(own_parts):
        here = jnp.full((devices, LANES), me * own_parts + part, jnp.int32)
        own_start, own_count, own_reached = [
            jnp.take_along_axis(value, here, axis=1).astype(jnp.int32)
            for value in (starts, counts, reached)
        ]
        own_over = jnp.maximum(own_over, own_reached + own_count - LANES)
        moved = lanes - own_reached
        (own_list,) = listed(
            [own_code], (own_start + moved) & (LANES - 1), moved, own_count, 1
        )
        code = own_list[0].astype(jnp.int32)
        at = (code & (depth - 1)) - part * part_depth
        select = jnp.where(whole_iota((part_depth, LANES), 0) == at, 1.0, 0.0).astype(BF16)
        lines = jnp.dot(
            bias_parts[part], jnp.concatenate([select, select], axis=0),
            preferred_element_type=F32,
        )
        cell = code >> (depth.bit_length() - 1)
        at_row = cell >> (cols.bit_length() - 1)
        line = lines[:cols]
        for r in range(1, rows):
            line = jnp.where(at_row == r, lines[r * cols : (r + 1) * cols], line)
        hit = whole_iota((cols, LANES), 0) == (cell & (cols - 1))
        value = jnp.sum(jnp.where(hit, line, 0.0), axis=0, keepdims=True)
        picked[part : part + 1, :] = jnp.exp(-value / TEMPER)

    for copy in to_near(picked, tables, b_send, b_recv, slabs, walks):
        copy.start()
    b_all = arrival(tables.at[pl.ds(0, len(OFFSETS) - 1)], b_send, b_recv, place)
    h_all.wait_recv()
    all_base = hills[:, 4, :]
    there = all_base > 0
    owner = jnp.where(there, owner_of(all_row, all_col, rows, cols, slabs, walks), -1.0)
    a_all.wait_send()
    h_all.wait_send()

    def past(away, extent, limit):
        away = away + (radius - 1)
        away = jnp.where(away < 0, away + extent, away)
        away = jnp.where(away >= extent, away - extent, away)
        return away < limit

    half_cols, half_depth, total = cols // 2, depth // 2, close_blocks * LANES
    close_row = there & past(all_row - first_row, grid_rows, rows + 2 * radius - 1)
    quarters = [(a, b) for a in (0, 1) for b in (0, 1)]
    close = [
        close_row
        & past(all_col - first_col - a * half_cols, grid_cols, half_cols + 2 * radius - 1)
        & past(all_depth - b * half_depth, depth, half_depth + 2 * radius - 1)
        for a, b in quarters
    ]
    ones = jnp.concatenate([jnp.where(mask, 1.0, 0.0) for mask in close], axis=0)
    both = jnp.dot(ones.astype(BF16), counting, preferred_element_type=F32)
    close_count = jnp.concatenate(
        [both[q * devices : (q + 1) * devices, LANES:] for q in range(4)], axis=1
    )
    close_reached = jnp.dot(before, close_count.astype(BF16), preferred_element_type=F32)
    close_over = jnp.max(close_reached + close_count - total)
    over = jnp.maximum(jnp.max(own_over.astype(F32)), close_over)
    close_lane = squeeze(ones > 0, both[:, :LANES])
    all_bucket = bucket_of(jnp.floor(all_row / rows), all_col, all_depth).astype(jnp.int32)
    shift = jnp.take_along_axis(reached - starts, all_bucket, axis=1)
    spot_part = owner * own_parts + jnp.floor(all_depth / part_depth)
    spot = lanes.astype(F32) + shift + spot_part * LANES
    position = (all_row * grid_cols + all_col) * depth + all_depth
    depth_lane = iota((LANES, LANES), 1)
    col_id = iota((half_cols, LANES), 0)
    depth_bits, col_bits = depth.bit_length() - 1, grid_cols.bit_length() - 1
    for q, (a, b) in enumerate(quarters):
        span = slice(q * LANES, (q + 1) * LANES)
        moved = lanes - close_reached[:, span].astype(jnp.int32)
        index = jnp.take_along_axis(
            close_lane[q * devices : (q + 1) * devices], moved & (LANES - 1), axis=1
        )
        lists = listed(
            [all_base, position, spot], index, moved, close_count[:, span].astype(jnp.int32),
            close_blocks,
        )
        for block, parts in enumerate(lists):
            code = parts[1].astype(jnp.int32)
            at_depth = (code & (depth - 1)).astype(F32)
            at_col = ((code >> depth_bits) & (grid_cols - 1)).astype(F32)
            at_row = (code >> (depth_bits + col_bits)).astype(F32)
            line = q * close_blocks + block
            for i, part in enumerate((parts[0], at_row, parts[2])):
                chosen[i, line : line + 1, :] = part
            at = as_column(at_depth)
            for i in range(half_depth // LANES):
                offset = depth_lane + (b * half_depth + i * LANES) - at
                high, low = halves(profile(wrapped(offset, depth), radius))
                for j, half in enumerate((high, high, low)):
                    rows_at = slice(j * total + block * LANES, j * total + (block + 1) * LANES)
                    right[q, rows_at, i * LANES : (i + 1) * LANES] = half
            offset = col_id + (first_col + a * half_cols) - at_col
            near[q, :, block * LANES : (block + 1) * LANES] = profile(
                wrapped(offset, grid_cols), radius
            )
    hills_ref[:, 0:1, :] = hills[:, 4:5, :]
    hills_ref[:, 1:4, :] = hills[:, 1:4, :]

    at_base, at_row = chosen[0], chosen[1]
    at_spot = chosen[2].astype(jnp.int32)
    at_lane = at_spot & (LANES - 1)
    at_table = at_spot >> (LANES.bit_length() - 1)
    row_parts = [
        at_base * profile(wrapped(first_row + r - at_row, grid_rows), radius) for r in range(rows)
    ]

    b_all.wait_recv()
    factor = jnp.zeros(at_base.shape, F32)
    for n in range(len(OFFSETS)):
        for part in range(own_parts):
            table = picked if n == HERE else tables.at[n]
            line = jnp.broadcast_to(table[part : part + 1, :], factor.shape)
            value = jnp.take_along_axis(line, at_lane, axis=1)
            factor = jnp.where(at_table == n * own_parts + part, value, factor)
    row_parts = [factor * part for part in row_parts]
    tops = []
    for q, (a, b) in enumerate(quarters):
        for r in range(rows):
            for block in range(close_blocks):
                line = q * close_blocks + block
                span = slice(block * LANES, (block + 1) * LANES)
                high, low = halves(near[q, :, span] * row_parts[r][line : line + 1])
                for j, half in enumerate((high, low)):
                    lanes_at = slice(j * total + block * LANES, j * total + (block + 1) * LANES)
                    left[q, r * half_cols : (r + 1) * half_cols, lanes_at] = half
        added = jnp.dot(left[q], right[q, : 2 * total], preferred_element_type=F32)
        added += jnp.dot(left[q, :, :total], right[q, 2 * total :], preferred_element_type=F32)
        depths = slice(b * half_depth, (b + 1) * half_depth)
        for r in range(rows):
            first = r * cols + a * half_cols
            value = added[r * half_cols : (r + 1) * half_cols]
            value = bias_ref[first : first + half_cols, depths] + value
            new_ref[first : first + half_cols, depths] = value
            tops.append(lane_tops(value))
    top = jnp.where(over > 0, jnp.inf, functools.reduce(jnp.maximum, tops))
    peak[...] = top
    peaks[me] = top
    for copy in to_all(peak, peaks.at[me], c_send, c_recv, place, steps):
        copy.start()
    c_all = arrival(peaks.at[others], c_send, c_recv, place)
    b_all.wait_send()
    c_all.wait_send()
    c_all.wait_recv()
    highest = jnp.max(peaks[...])
    top_ref[...] = jnp.broadcast_to(highest, top_ref.shape)
    flag_ref[0] = jnp.where(highest == jnp.inf, 1, 0)


def by_kernel(own_parts, close_blocks, slabs, walks, arrays):
    bias_grid, hill_slab, hill_row, hill_col, hill_depth, hill_level, hill_count, table = arrays
    rows, cols, depth = bias_grid.shape
    devices = slabs * walks
    total = close_blocks * LANES
    cells = rows * cols
    walkers = hill_row.shape
    vmem = pl.BlockSpec(memory_space=pltpu.VMEM)
    smem = pl.BlockSpec(memory_space=pltpu.SMEM)
    hbm = pl.BlockSpec(memory_space=pltpu.HBM)
    return pl.pallas_call(
        functools.partial(window_kernel, slabs, walks, rows, cols, own_parts, close_blocks),
        out_shape=(
            jax.ShapeDtypeStruct((cells, depth), F32),
            jax.ShapeDtypeStruct((8, LANES), F32),
            jax.ShapeDtypeStruct((cells, depth), F32),
            jax.ShapeDtypeStruct((devices, 4, LANES), F32),
            jax.ShapeDtypeStruct((1,), jnp.int32),
        ),
        in_specs=[hbm] * 8,
        out_specs=(vmem, vmem, vmem, vmem, smem),
        scratch_shapes=[
            pltpu.VMEM(walkers, jnp.int32),
            pltpu.VMEM(walkers, jnp.int32),
            pltpu.VMEM(walkers, jnp.int32),
            pltpu.VMEM(walkers, jnp.int32),
            pltpu.VMEM(walkers, jnp.int32),
            pltpu.SMEM(hill_count.shape, jnp.int32),
            pltpu.SMEM(table.shape, F32),
            pltpu.SemaphoreType.DMA((8,)),
            pltpu.VMEM((8, LANES), F32),
            pltpu.VMEM((devices, 8, LANES), F32),
            pltpu.VMEM((own_parts, cells, 2 * depth // own_parts), BF16),
            pltpu.VMEM((own_parts, LANES), F32),
            pltpu.VMEM((len(OFFSETS), own_parts, LANES), F32),
            pltpu.VMEM((3, 4 * close_blocks, LANES), F32),
            pltpu.VMEM((4, cells // 2, 2 * total), BF16),
            pltpu.VMEM((4, 3 * total, depth // 2), BF16),
            pltpu.VMEM((4, cols // 2, total), F32),
            pltpu.VMEM((1, LANES), F32),
            pltpu.VMEM((devices, 1, LANES), F32),
            pltpu.SemaphoreType.DMA((1,)),
            pltpu.SemaphoreType.DMA((1,)),
            pltpu.SemaphoreType.DMA((1,)),
            pltpu.SemaphoreType.DMA((1,)),
            pltpu.SemaphoreType.DMA((1,)),
            pltpu.SemaphoreType.DMA((1,)),
            pltpu.SemaphoreType.DMA((1,)),
            pltpu.SemaphoreType.DMA((1,)),
        ],
        compiler_params=pltpu.CompilerParams(
            collective_id=0, has_side_effects=True, vmem_limit_bytes=58 * 2**20
        ),
    )(
        bias_grid.reshape(cells, depth),
        hill_slab.reshape(hill_row.shape),
        hill_row,
        hill_col,
        hill_depth,
        hill_level,
        hill_count,
        table,
    )


def full_kernel(
    slabs, walks, rows, cols,
    bias_ref, hills_ref, new_ref, top_ref,
    bias_high, bias_low, picked, tables, peak, peaks,
    b_send, b_recv, c_send, c_recv,
):
    devices = slabs * walks
    cells, depth = bias_ref.shape
    radius = 2 * rows
    grid_rows, grid_cols = slabs * rows, walks * cols
    slab = lax.axis_index("slab")
    walk = lax.axis_index("walk")
    me = slab * walks + walk
    first_row = (slab * rows).astype(F32)
    first_col = (walk * cols).astype(F32)
    place, steps = mesh_steps(slabs, walks)
    barrier = greet(place, steps)
    high, low = halves(bias_ref[...])
    bias_high[...] = high
    bias_low[...] = low

    def pick(sender, carry):
        part = hills_ref[sender]
        cell = (part[1:2] - first_row) * cols + part[2:3] - first_col
        owner = owner_of(part[1:2], part[2:3], rows, cols, slabs, walks)
        cell = jnp.where(owner == HERE, cell, -1.0)
        select = jnp.where(iota((depth, LANES), 0) == part[3:4], 1.0, 0.0).astype(BF16)
        lines = jnp.dot(bias_high[...], select, preferred_element_type=F32)
        lines = lines + jnp.dot(bias_low[...], select, preferred_element_type=F32)
        hit = iota((cells, LANES), 0) == cell
        value = jnp.sum(jnp.where(hit, lines, 0.0), axis=0, keepdims=True)
        picked[pl.ds(sender, 1), :] = jnp.exp(-value / TEMPER)
        return carry

    lax.fori_loop(0, devices, pick, 0)
    pl.semaphore_wait(barrier, devices - 1)
    for copy in to_near(picked, tables, b_send, b_recv, slabs, walks):
        copy.start()
    b_all = arrival(tables.at[pl.ds(0, len(OFFSETS) - 1)], b_send, b_recv, place)
    tables[HERE] = picked[...]
    b_all.wait_recv()
    new_ref[...] = bias_ref[...]

    def add(sender, carry):
        part = hills_ref[sender]
        owner = owner_of(part[1:2], part[2:3], rows, cols, slabs, walks)
        height = jnp.zeros((1, LANES), F32)
        for n in range(len(OFFSETS)):
            height = jnp.where(owner == n, part[0:1] * tables[n, pl.ds(sender, 1), :], height)
        at = as_column(part[3:4])[:, 0:1]
        right = profile(wrapped(iota((LANES, depth), 1) - at, depth), radius)
        right_high, right_low = halves(right)
        col_offset = iota((cols, LANES), 0) + first_col - part[2:3]
        near = profile(wrapped(col_offset, grid_cols), radius)
        for r in range(rows):
            along = profile(wrapped(first_row + r - part[1:2], grid_rows), radius)
            left_high, left_low = halves(near * (height * along))
            added = jnp.dot(left_high, right_high, preferred_element_type=F32)
            added += jnp.dot(left_low, right_high, preferred_element_type=F32)
            added += jnp.dot(left_high, right_low, preferred_element_type=F32)
            new_ref[r * cols : (r + 1) * cols, :] += added
        return carry

    lax.fori_loop(0, devices, add, 0)
    top = lane_tops(new_ref[...])
    peak[...] = top
    peaks[me] = top
    for copy in to_all(peak, peaks.at[me], c_send, c_recv, place, steps):
        copy.start()
    c_all = arrival(peaks.at[pl.ds(0, devices - 1)], c_send, c_recv, place)
    b_all.wait_send()
    c_all.wait_send()
    c_all.wait_recv()
    top_ref[...] = jnp.broadcast_to(jnp.max(peaks[...]), top_ref.shape)


def by_full_kernel(rows, slabs, walks, bias, hills):
    cells, depth = bias.shape
    devices = slabs * walks
    vmem = pl.BlockSpec(memory_space=pltpu.VMEM)
    return pl.pallas_call(
        functools.partial(full_kernel, slabs, walks, rows, cells // rows),
        out_shape=(
            jax.ShapeDtypeStruct((cells, depth), F32),
            jax.ShapeDtypeStruct((8, LANES), F32),
        ),
        in_specs=[vmem] * 2,
        out_specs=(vmem, vmem),
        scratch_shapes=[
            pltpu.VMEM((cells, depth), BF16),
            pltpu.VMEM((cells, depth), BF16),
            pltpu.VMEM((devices, LANES), F32),
            pltpu.VMEM((len(OFFSETS), devices, LANES), F32),
            pltpu.VMEM((1, LANES), F32),
            pltpu.VMEM((devices, 1, LANES), F32),
            pltpu.SemaphoreType.DMA((1,)),
            pltpu.SemaphoreType.DMA((1,)),
            pltpu.SemaphoreType.DMA((1,)),
            pltpu.SemaphoreType.DMA((1,)),
        ],
        compiler_params=pltpu.CompilerParams(
            collective_id=1, has_side_effects=True, vmem_limit_bytes=20 * 2**20
        ),
    )(bias, hills)


def output_kernel(new_ref, top_ref, new_out, free_out, free_ref, sems):
    parts = 2
    span = new_ref.shape[0] // parts
    first = pltpu.make_async_copy(new_ref, new_out, sems.at[0])
    first.start()
    for i in range(parts):
        rows = pl.ds(i * span, span)
        free_ref[rows, :] = FREE_SCALE * (top_ref[0:1, 0:1] - new_ref[rows, :])
        pltpu.make_async_copy(free_ref.at[rows], free_out.at[rows], sems.at[1]).start()
    first.wait()
    pltpu.make_async_copy(free_ref, free_out, sems.at[1]).wait()


def outputs(new_bias, top):
    hbm = pl.BlockSpec(memory_space=pltpu.HBM)
    return pl.pallas_call(
        output_kernel,
        out_shape=(jax.ShapeDtypeStruct(new_bias.shape, F32),) * 2,
        in_specs=[pl.BlockSpec(memory_space=pltpu.VMEM)] * 2,
        out_specs=(hbm, hbm),
        scratch_shapes=[pltpu.VMEM(new_bias.shape, F32), pltpu.SemaphoreType.DMA((2,))],
        compiler_params=pltpu.CompilerParams(vmem_limit_bytes=4 * 2**20),
    )(new_bias, top)


def per_device(*arrays):
    bias_grid = arrays[0]
    shape = bias_grid.shape
    slabs, walks = lax.axis_size("slab"), lax.axis_size("walk")
    devices = slabs * walks
    fits = (
        arrays[2].size == LANES
        and slabs >= 5
        and walks >= 3
        and devices <= 64
        and devices % 8 == 0
        and shape[1] % LANES == 0
        and shape[1] >= 2 * shape[0]
        and shape[2] % (4 * LANES) == 0
        and max(walks * shape[1], shape[2]) <= 4096
        and max(slabs * shape[0], arrays[7].size) <= 255
        and all(size & (size - 1) == 0 for size in (slabs, walks, shape[1], shape[2]))
        and devices * shape[0] * shape[1] * shape[2] <= 2**24
    )
    if not fits:
        return by_collectives(*arrays)

    def finish(new_bias, top):
        new_out, free_out = outputs(new_bias, top)
        return new_out.reshape(shape), free_out.reshape(shape)

    new_bias, top, bias, hills, flag = by_kernel(min(4, LANES // devices), 2, slabs, walks, arrays)
    return lax.cond(
        flag.reshape(()),
        lambda: finish(*by_full_kernel(shape[0], slabs, walks, bias, hills)),
        lambda: finish(new_bias, top),
    )


def solution(mesh):
    in_specs = (
        P("slab", "walk", None),
        P(("slab", "walk"), None, None),
        P(("slab", "walk"), None),
        P(("slab", "walk"), None),
        P(("slab", "walk"), None),
        P(("slab", "walk"), None),
        P(("slab", "walk")),
        P(),
    )
    out_specs = (P("slab", "walk", None), P("slab", "walk", None))
    return jax.shard_map(
        per_device, mesh=mesh, in_specs=in_specs, out_specs=out_specs, check_vma=False
    )
```

```python
import functools
import math

import jax
import jax.numpy as jnp
from jax import lax
from jax.experimental import pallas as pl
from jax.experimental.pallas import tpu as pltpu
from jax.sharding import PartitionSpec as P

BASE_HEIGHT = 1.2
TEMPER = 4.0
SIGMA_SHARE = 0.3125
FREE_SCALE = 10.0 / 9.0


def from_behind(block, axis, distance):
    devices = range(lax.axis_size(axis))
    route = [((i - distance) % len(devices), i) for i in devices]
    return lax.ppermute(block, axis, route)


def gaussian(position, centre, extent, radius):
    offset = jnp.mod(position - centre + extent // 2, extent) - extent // 2
    inside = (offset >= -radius) & (offset < radius)
    spread = SIGMA_SHARE * radius
    distance = offset.astype(jnp.float32)
    return jnp.where(inside, jnp.exp(-(distance * distance) / (2.0 * spread * spread)), 0.0)


def deposit(row_ids, col_ids, depth_ids, hill_lists, grid_rows, grid_cols, grid_depth, radius):
    slot_total = hill_lists.shape[1]
    block_size = math.gcd(slot_total, 256)
    row_count = row_ids.shape[0]
    col_count = col_ids.shape[0]
    depth_count = depth_ids.shape[0]

    def one_block(carry_sum, index):
        portion = lax.dynamic_slice_in_dim(hill_lists, index * block_size, block_size, 1)
        row_gauss = (
            gaussian(row_ids[:, None], portion[1].astype(jnp.int32)[None, :], grid_rows, radius)
            * portion[0][None, :]
        )
        col_gauss = gaussian(
            col_ids[:, None], portion[2].astype(jnp.int32)[None, :], grid_cols, radius
        )
        depth_gauss = gaussian(
            depth_ids[None, :], portion[3].astype(jnp.int32)[:, None], grid_depth, radius
        )
        plane_gauss = (row_gauss[:, None, :] * col_gauss[None, :, :]).reshape(
            row_count * col_count, block_size
        )
        added = jnp.dot(
            plane_gauss,
            depth_gauss,
            precision=lax.Precision.HIGHEST,
            preferred_element_type=jnp.float32,
        )
        return (carry_sum + added, None)

    start = jnp.zeros((row_count * col_count, depth_count), jnp.float32)
    result, unused = lax.scan(one_block, start, jnp.arange(slot_total // block_size))
    return result.reshape(row_count, col_count, depth_count)


def by_collectives(
    bias_grid, hill_slab, hill_row, hill_col, hill_depth, hill_level, hill_count, height_levels
):
    rows_dev, cols_dev, depth_bins = bias_grid.shape
    slab_count = lax.axis_size("slab")
    walk_count = lax.axis_size("walk")
    radius = 2 * rows_dev
    grid_rows = rows_dev * slab_count
    grid_cols = cols_dev * walk_count
    walkers_dev, hill_slots = hill_row.shape
    sent_rows = walkers_dev * hill_slots
    capacity = max(2, 4 * sent_rows // slab_count)
    target = hill_slab[:, :, 0].reshape(-1)
    centre_row = target * rows_dev + hill_row.reshape(-1)
    is_live = (
        lax.broadcasted_iota(jnp.int32, (walkers_dev, hill_slots), 1) < hill_count[:, None]
    ).reshape(-1)
    level_match = hill_level.reshape(-1)[:, None] == lax.broadcasted_iota(
        jnp.int32, (1, height_levels.shape[0]), 1
    )
    base_height = jnp.sum(jnp.where(level_match, height_levels[None, :], 0.0), axis=1)
    base_height = jnp.where(is_live, BASE_HEIGHT * base_height, 0.0)
    same_slab = target[:, None] == target[None, :]
    earlier = lax.broadcasted_iota(jnp.int32, (sent_rows, sent_rows), 1) < lax.broadcasted_iota(
        jnp.int32, (sent_rows, sent_rows), 0
    )
    slot_rank = jnp.sum((same_slab & earlier).astype(jnp.int32), axis=1)
    slot_place = target * capacity + slot_rank
    placing = (
        slot_place[:, None] == lax.broadcasted_iota(jnp.int32, (1, slab_count * capacity), 1)
    ).astype(jnp.float32)
    fields = jnp.stack(
        [
            base_height,
            centre_row.astype(jnp.float32),
            hill_col.reshape(-1).astype(jnp.float32),
            hill_depth.reshape(-1).astype(jnp.float32),
        ]
    )
    outgoing = jnp.dot(
        fields, placing, precision=lax.Precision.HIGHEST, preferred_element_type=jnp.float32
    )
    outgoing = outgoing.reshape(4, slab_count, capacity)
    arrived = lax.all_to_all(outgoing, "slab", split_axis=1, concat_axis=1, tiled=True).reshape(
        4, slab_count * capacity
    )
    shared = lax.all_gather(arrived, "walk", axis=1, tiled=True)
    slab_index = lax.axis_index("slab")
    walk_index = lax.axis_index("walk")
    local_row = jnp.clip(shared[1].astype(jnp.int32) - slab_index * rows_dev, 0, rows_dev - 1)
    local_col = shared[2].astype(jnp.int32) - walk_index * cols_dev
    local_depth = jnp.clip(shared[3].astype(jnp.int32), 0, depth_bins - 1)
    owned = (local_col >= 0) & (local_col < cols_dev)
    flat_place = (
        local_row * cols_dev + jnp.clip(local_col, 0, cols_dev - 1)
    ) * depth_bins + local_depth
    picked = bias_grid.reshape(-1)[flat_place]
    centre_value = lax.psum(jnp.where(owned, picked, 0.0), "walk")
    height = shared[0] * jnp.exp(-centre_value / TEMPER)
    hill_lists = jnp.stack([height, shared[1], shared[2], shared[3]])
    col_ids = walk_index * cols_dev + lax.broadcasted_iota(jnp.int32, (cols_dev,), 0)
    depth_ids = lax.broadcasted_iota(jnp.int32, (depth_bins,), 0)
    collected = [hill_lists]
    for offset in (-2, -1, 1, 2):
        collected.append(from_behind(hill_lists, "slab", offset))
    row_ids = slab_index * rows_dev + lax.broadcasted_iota(jnp.int32, (rows_dev,), 0)
    added = deposit(
        row_ids,
        col_ids,
        depth_ids,
        jnp.concatenate(collected, axis=1),
        grid_rows,
        grid_cols,
        depth_bins,
        radius,
    )
    new_bias = bias_grid + added
    highest = lax.pmax(jnp.max(new_bias), ("slab", "walk"))
    free_energy = FREE_SCALE * (highest - new_bias)
    return (new_bias, free_energy)


LANES = 128
F32 = jnp.float32
BF16 = jnp.bfloat16
MESH = pl.DeviceIdType.MESH
NT = (((1,), (1,)), ((), ()))


def wrapped(offset, extent):
    offset = jnp.where(offset >= extent // 2, offset - extent, offset)
    return jnp.where(offset < -(extent // 2), offset + extent, offset)


def profile(offset, radius):
    spread = SIGMA_SHARE * radius
    value = jnp.exp(-(offset * offset) / (2.0 * spread * spread))
    return jnp.where((offset >= -radius) & (offset < radius), value, 0.0)


def halves(value):
    high = value.astype(BF16)
    return high, (value - high.astype(F32)).astype(BF16)


def iota(shape, dim):
    return lax.broadcasted_iota(jnp.int32, shape, dim).astype(F32)


def whole_iota(shape, dim):
    return lax.broadcasted_iota(jnp.int32, shape, dim)


OFFSETS = [(i, j) for i in (-2, -1, 0, 1, 2) for j in (-1, 0, 1)]
HERE = OFFSETS.index((0, 0))


def flipped(index, extent):
    values = [index]
    bit = 1
    while bit < extent:
        turn = bit * (1 - 2 * lax.rem(index // bit, 2))
        values += [value + turn for value in values]
        bit *= 2
    return values


def mesh_steps(slabs, walks):
    slab_at = flipped(lax.axis_index("slab"), slabs)
    walk_at = flipped(lax.axis_index("walk"), walks)

    def place(step):
        return (slab_at[step // walks], walk_at[step % walks])

    return place, range(slabs * walks - 1, 0, -1)


def greet(place, steps):
    barrier = pltpu.get_barrier_semaphore()
    for step in steps:
        pl.semaphore_signal(barrier, inc=1, device_id=place(step), device_id_type=MESH)
    return barrier


def to_all(source, target, send, recv, place, steps):
    return [
        pltpu.make_async_remote_copy(
            source, target, send.at[0], recv.at[0],
            device_id=place(step), device_id_type=MESH,
        )
        for step in steps
    ]


def to_near(source, tables, send, recv, slabs, walks):
    slab, walk = lax.axis_index("slab"), lax.axis_index("walk")
    copies = []
    for n, (i, j) in sorted(enumerate(OFFSETS), key=lambda item: -abs(item[1][0])):
        if n == HERE:
            continue
        device = (lax.rem(slab - i + slabs, slabs), lax.rem(walk - j + walks, walks))
        copies.append(
            pltpu.make_async_remote_copy(
                source, tables.at[n], send.at[0], recv.at[0],
                device_id=device, device_id_type=MESH,
            )
        )
    return copies


def arrival(landing, send, recv, place):
    return pltpu.make_async_remote_copy(
        landing, landing, send.at[0], recv.at[0], device_id=place(1), device_id_type=MESH
    )


def owner_of(at_row, at_col, rows, cols, slabs, walks):
    slab_of = jnp.floor(at_row / rows) - lax.axis_index("slab").astype(F32)
    walk_of = jnp.floor(at_col / cols) - lax.axis_index("walk").astype(F32)
    slab_of = jnp.where(slab_of < -2, slab_of + slabs, slab_of)
    slab_of = jnp.where(slab_of > 2, slab_of - slabs, slab_of)
    walk_of = jnp.where(walk_of < -1, walk_of + walks, walk_of)
    walk_of = jnp.where(walk_of > 1, walk_of - walks, walk_of)
    inside = (jnp.abs(slab_of) <= 2) & (jnp.abs(walk_of) <= 1)
    return jnp.where(inside, (slab_of + 2) * 3 + walk_of + 1, -1.0)


def lane_tops(value):
    most = jnp.max(value, axis=0, keepdims=True)
    top = most[:, 0:LANES]
    for i in range(1, value.shape[1] // LANES):
        top = jnp.maximum(top, most[:, i * LANES : (i + 1) * LANES])
    return top


def as_column(row):
    return jnp.broadcast_to(row, (LANES, LANES)).T


def squeeze(mask, rank):
    lane = whole_iota(mask.shape, 1)
    code = (lane - rank.astype(jnp.int32)) * LANES + lane + LANES * LANES
    code = jnp.where(mask, code, 0)
    step = 1
    while step < LANES:
        came = pltpu.roll(code, LANES - step, axis=1)
        bit = step * LANES
        stays = jnp.where((code & bit) != 0, 0, code)
        code = jnp.where((came & bit) != 0, came, stays)
        step *= 2
    return code & (LANES - 1)


def window_kernel(
    slabs, walks, rows, cols, close_blocks,
    bias_in, slab_in, row_in, col_in, depth_in, level_in, count_in, table_in,
    new_ref, top_ref, bias_ref, hills_ref, flag_ref,
    slab_ref, row_ref, col_ref, depth_ref, level_ref, count_ref, table_ref, in_sems,
    mine, hills, bias_parts, picked, tables, chosen, left, right, near, peak, peaks,
    a_send, a_recv, h_send, h_recv, b_send, b_recv, c_send, c_recv,
):
    devices = slabs * walks
    cells, depth = bias_ref.shape
    radius = 2 * rows
    grid_rows, grid_cols = slabs * rows, walks * cols
    slab = lax.axis_index("slab")
    walk = lax.axis_index("walk")
    me = slab * walks + walk
    first_row = (slab * rows).astype(F32)
    first_col = (walk * cols).astype(F32)
    place, steps = mesh_steps(slabs, walks)
    barrier = greet(place, steps)

    def bucket_of(at_slab, at_row, at_col):
        owner = at_slab * walks + jnp.floor(at_col / cols)
        return owner * rows + at_row

    inputs = (
        (slab_in, slab_ref), (row_in, row_ref), (col_in, col_ref), (depth_in, depth_ref),
        (level_in, level_ref), (count_in, count_ref), (table_in, table_ref), (bias_in, bias_ref),
    )
    fetches = [
        pltpu.make_async_copy(there, here, in_sems.at[i])
        for i, (there, here) in enumerate(inputs)
    ]
    for fetch in fetches:
        fetch.start()
    for fetch in fetches[:-1]:
        fetch.wait()

    def in_row(ref):
        value = ref[...].astype(F32)
        return jnp.concatenate([value[i : i + 1] for i in range(value.shape[0])], axis=1)

    slots = row_ref.shape[1]
    lane = iota((1, LANES), 1)
    live = jnp.zeros((1, LANES), F32)
    for i in range(row_ref.shape[0]):
        inside = (lane >= i * slots) & (lane < i * slots + count_ref[i].astype(F32))
        live = jnp.where(inside, 1.0, live)
    target, centre_col, centre_depth = in_row(slab_ref), in_row(col_ref), in_row(depth_ref)
    bucket = bucket_of(target, in_row(row_ref), centre_col)
    key = jnp.where(live > 0, bucket, float(devices * rows)) * LANES + lane
    keys = as_column(key)
    ahead = jnp.sum(jnp.where(keys < key, 1.0, 0.0), axis=0, keepdims=True)
    first = lane * LANES
    inside = (keys >= first) & (keys < first + LANES)
    counts = jnp.sum(jnp.where(inside & (lane < devices * rows), 1.0, 0.0), axis=0, keepdims=True)
    col_high = jnp.floor(centre_col / 16.0)
    depth_high = jnp.floor(centre_depth / 16.0)
    unsorted = jnp.concatenate(
        [
            jnp.where(live > 0, in_row(level_ref) + 1.0, 0.0),
            target * rows + in_row(row_ref),
            col_high,
            centre_col - 16.0 * col_high,
            depth_high,
            centre_depth - 16.0 * depth_high,
            live,
            live,
        ],
        axis=0,
    ).astype(BF16)
    order = jnp.where(iota((LANES, LANES), 0) == ahead, 1.0, 0.0).astype(BF16)
    ordered = lax.dot_general(unsorted, order, NT, preferred_element_type=F32)
    level = ordered[0:1]
    base = jnp.zeros((1, LANES), F32)
    for i in range(table_ref.shape[0]):
        base = jnp.where(level == i + 1, BASE_HEIGHT * table_ref[i], base)
    fields = (
        counts,
        ordered[2:3] * 16.0 + ordered[3:4],
        ordered[4:5] * 16.0 + ordered[5:6],
        ordered[1:2],
        base,
    )
    for i, field in enumerate(fields):
        mine[i : i + 1, :] = field
        hills[me, i : i + 1, :] = field

    pl.semaphore_wait(barrier, devices - 1)
    others = pl.ds(0, devices - 1)
    places, heights = pl.ds(0, 3), pl.ds(3, 2)
    for copy in to_all(mine.at[places], hills.at[me, places], a_send, a_recv, place, steps):
        copy.start()
    a_all = arrival(hills.at[others, places], a_send, a_recv, place)
    for copy in to_all(mine.at[heights], hills.at[me, heights], h_send, h_recv, place, steps):
        copy.start()
    h_all = arrival(hills.at[others, heights], h_send, h_recv, place)

    fetches[-1].wait()
    high, low = halves(bias_ref[...])
    for part in range(rows):
        span = slice(part * cols, (part + 1) * cols)
        bias_parts[part, :, :depth] = high[span]
        bias_parts[part, :, depth:] = low[span]
    counting = jnp.concatenate(
        [
            jnp.where(iota((LANES, LANES), 0) < iota((LANES, LANES), 1), 1.0, 0.0),
            jnp.ones((LANES, LANES), F32),
        ],
        axis=1,
    ).astype(BF16)
    before = jnp.where(
        iota((devices, devices), 1) < iota((devices, devices), 0), 1.0, 0.0
    ).astype(BF16)
    lanes = whole_iota((devices, LANES), 1)

    a_all.wait_recv()

    counts, all_col, all_depth = [hills[:, i, :] for i in range(3)]

    exact = counts.astype(BF16)
    starts = jnp.dot(exact, counting[:, :LANES], preferred_element_type=F32)
    reached = jnp.dot(before, exact, preferred_element_type=F32)

    def listed(values, index, moved, count, blocks):
        taken = [jnp.take_along_axis(value, index, axis=1) for value in values]
        result = []
        for block in range(blocks):
            spot = moved + block * LANES
            valid = (spot >= 0) & (spot < count)
            result.append([jnp.sum(jnp.where(valid, t, 0.0), axis=0, keepdims=True) for t in taken])
        return result

    own_code = (all_col - first_col) * depth + all_depth
    own_over = jnp.zeros((devices, LANES), jnp.int32)
    for part in range(rows):
        here = jnp.full((devices, LANES), me * rows + part, jnp.int32)
        own_start, own_count, own_reached = [
            jnp.take_along_axis(value, here, axis=1).astype(jnp.int32)
            for value in (starts, counts, reached)
        ]
        own_over = jnp.maximum(own_over, own_reached + own_count - LANES)
        moved = lanes - own_reached
        (own_list,) = listed(
            [own_code], (own_start + moved) & (LANES - 1), moved, own_count, 1
        )
        code = own_list[0].astype(jnp.int32)
        at = code & (depth - 1)
        select = jnp.where(whole_iota((depth, LANES), 0) == at, 1.0, 0.0).astype(BF16)
        lines = jnp.dot(
            bias_parts[part], jnp.concatenate([select, select], axis=0),
            preferred_element_type=F32,
        )
        hit = whole_iota((cols, LANES), 0) == (code >> (depth.bit_length() - 1))
        value = jnp.sum(jnp.where(hit, lines, 0.0), axis=0, keepdims=True)
        picked[part : part + 1, :] = jnp.exp(-value / TEMPER)

    for copy in to_near(picked, tables, b_send, b_recv, slabs, walks):
        copy.start()
    b_all = arrival(tables.at[pl.ds(0, len(OFFSETS) - 1)], b_send, b_recv, place)
    h_all.wait_recv()
    all_row, all_base = hills[:, 3, :], hills[:, 4, :]
    there = all_base > 0
    owner = jnp.where(there, owner_of(all_row, all_col, rows, cols, slabs, walks), -1.0)
    a_all.wait_send()
    h_all.wait_send()

    def past(away, extent, limit):
        away = away + (radius - 1)
        away = jnp.where(away < 0, away + extent, away)
        away = jnp.where(away >= extent, away - extent, away)
        return away < limit

    half_cols, half_depth, total = cols // 2, depth // 2, close_blocks * LANES
    close_row = there & past(all_row - first_row, grid_rows, rows + 2 * radius - 1)
    quarters = [(a, b) for a in (0, 1) for b in (0, 1)]
    close = [
        close_row
        & past(all_col - first_col - a * half_cols, grid_cols, half_cols + 2 * radius - 1)
        & past(all_depth - b * half_depth, depth, half_depth + 2 * radius - 1)
        for a, b in quarters
    ]
    ones = jnp.concatenate([jnp.where(mask, 1.0, 0.0) for mask in close], axis=0)
    both = jnp.dot(ones.astype(BF16), counting, preferred_element_type=F32)
    close_count = jnp.concatenate(
        [both[q * devices : (q + 1) * devices, LANES:] for q in range(4)], axis=1
    )
    close_reached = jnp.dot(before, close_count.astype(BF16), preferred_element_type=F32)
    close_over = jnp.max(close_reached + close_count - total)
    over = jnp.maximum(jnp.max(own_over.astype(F32)), close_over)
    close_lane = squeeze(ones > 0, both[:, :LANES])
    all_slab = jnp.floor(all_row / rows)
    slab_row = all_row - all_slab * rows
    all_bucket = bucket_of(all_slab, slab_row, all_col).astype(jnp.int32)
    shift = jnp.take_along_axis(reached - starts, all_bucket, axis=1)
    spot_part = owner * rows + slab_row
    spot = lanes.astype(F32) + shift + spot_part * LANES
    position = (all_row * grid_cols + all_col) * depth + all_depth
    depth_lane = iota((LANES, LANES), 1)
    col_id = iota((half_cols, LANES), 0)
    depth_bits, col_bits = depth.bit_length() - 1, grid_cols.bit_length() - 1
    for q, (a, b) in enumerate(quarters):
        span = slice(q * LANES, (q + 1) * LANES)
        moved = lanes - close_reached[:, span].astype(jnp.int32)
        index = jnp.take_along_axis(
            close_lane[q * devices : (q + 1) * devices], moved & (LANES - 1), axis=1
        )
        lists = listed(
            [all_base, position, spot], index, moved, close_count[:, span].astype(jnp.int32),
            close_blocks,
        )
        for block, parts in enumerate(lists):
            code = parts[1].astype(jnp.int32)
            at_depth = (code & (depth - 1)).astype(F32)
            at_col = ((code >> depth_bits) & (grid_cols - 1)).astype(F32)
            at_row = (code >> (depth_bits + col_bits)).astype(F32)
            line = q * close_blocks + block
            for i, part in enumerate((parts[0], at_row, parts[2])):
                chosen[i, line : line + 1, :] = part
            at = as_column(at_depth)
            for i in range(half_depth // LANES):
                offset = depth_lane + (b * half_depth + i * LANES) - at
                high, low = halves(profile(wrapped(offset, depth), radius))
                for j, half in enumerate((high, high, low)):
                    rows_at = slice(j * total + block * LANES, j * total + (block + 1) * LANES)
                    right[q, rows_at, i * LANES : (i + 1) * LANES] = half
            offset = col_id + (first_col + a * half_cols) - at_col
            near[q, :, block * LANES : (block + 1) * LANES] = profile(
                wrapped(offset, grid_cols), radius
            )
    hills_ref[:, 0:1, :] = hills[:, 4:5, :]
    hills_ref[:, 1:2, :] = hills[:, 3:4, :]
    hills_ref[:, 2:4, :] = hills[:, 1:3, :]

    at_base, at_row = chosen[0], chosen[1]
    at_spot = chosen[2].astype(jnp.int32)
    at_lane = at_spot & (LANES - 1)
    at_table = at_spot >> (LANES.bit_length() - 1)
    row_parts = [
        at_base * profile(wrapped(first_row + r - at_row, grid_rows), radius) for r in range(rows)
    ]

    b_all.wait_recv()
    factor = jnp.zeros(at_base.shape, F32)
    for n in range(len(OFFSETS)):
        for part in range(rows):
            table = picked if n == HERE else tables.at[n]
            line = jnp.broadcast_to(table[part : part + 1, :], factor.shape)
            value = jnp.take_along_axis(line, at_lane, axis=1)
            factor = jnp.where(at_table == n * rows + part, value, factor)
    row_parts = [factor * part for part in row_parts]
    tops = []
    for q, (a, b) in enumerate(quarters):
        for r in range(rows):
            for block in range(close_blocks):
                line = q * close_blocks + block
                span = slice(block * LANES, (block + 1) * LANES)
                high, low = halves(near[q, :, span] * row_parts[r][line : line + 1])
                for j, half in enumerate((high, low)):
                    lanes_at = slice(j * total + block * LANES, j * total + (block + 1) * LANES)
                    left[q, r * half_cols : (r + 1) * half_cols, lanes_at] = half
        added = jnp.dot(left[q], right[q, : 2 * total], preferred_element_type=F32)
        added += jnp.dot(left[q, :, :total], right[q, 2 * total :], preferred_element_type=F32)
        depths = slice(b * half_depth, (b + 1) * half_depth)
        for r in range(rows):
            first = r * cols + a * half_cols
            value = added[r * half_cols : (r + 1) * half_cols]
            value = bias_ref[first : first + half_cols, depths] + value
            new_ref[first : first + half_cols, depths] = value
            tops.append(lane_tops(value))
    top = jnp.where(over > 0, jnp.inf, functools.reduce(jnp.maximum, tops))
    peak[...] = top
    peaks[me] = top
    for copy in to_all(peak, peaks.at[me], c_send, c_recv, place, steps):
        copy.start()
    c_all = arrival(peaks.at[others], c_send, c_recv, place)
    b_all.wait_send()
    c_all.wait_send()
    c_all.wait_recv()
    highest = jnp.max(peaks[...])
    top_ref[...] = jnp.broadcast_to(highest, top_ref.shape)
    flag_ref[0] = jnp.where(highest == jnp.inf, 1, 0)


def by_kernel(close_blocks, slabs, walks, arrays):
    bias_grid, hill_slab, hill_row, hill_col, hill_depth, hill_level, hill_count, table = arrays
    rows, cols, depth = bias_grid.shape
    devices = slabs * walks
    total = close_blocks * LANES
    cells = rows * cols
    walkers = hill_row.shape
    vmem = pl.BlockSpec(memory_space=pltpu.VMEM)
    smem = pl.BlockSpec(memory_space=pltpu.SMEM)
    hbm = pl.BlockSpec(memory_space=pltpu.HBM)
    return pl.pallas_call(
        functools.partial(window_kernel, slabs, walks, rows, cols, close_blocks),
        out_shape=(
            jax.ShapeDtypeStruct((cells, depth), F32),
            jax.ShapeDtypeStruct((8, LANES), F32),
            jax.ShapeDtypeStruct((cells, depth), F32),
            jax.ShapeDtypeStruct((devices, 4, LANES), F32),
            jax.ShapeDtypeStruct((1,), jnp.int32),
        ),
        in_specs=[hbm] * 8,
        out_specs=(vmem, vmem, vmem, vmem, smem),
        scratch_shapes=[
            pltpu.VMEM(walkers, jnp.int32),
            pltpu.VMEM(walkers, jnp.int32),
            pltpu.VMEM(walkers, jnp.int32),
            pltpu.VMEM(walkers, jnp.int32),
            pltpu.VMEM(walkers, jnp.int32),
            pltpu.SMEM(hill_count.shape, jnp.int32),
            pltpu.SMEM(table.shape, F32),
            pltpu.SemaphoreType.DMA((8,)),
            pltpu.VMEM((8, LANES), F32),
            pltpu.VMEM((devices, 8, LANES), F32),
            pltpu.VMEM((rows, cols, 2 * depth), BF16),
            pltpu.VMEM((rows, LANES), F32),
            pltpu.VMEM((len(OFFSETS), rows, LANES), F32),
            pltpu.VMEM((3, 4 * close_blocks, LANES), F32),
            pltpu.VMEM((4, cells // 2, 2 * total), BF16),
            pltpu.VMEM((4, 3 * total, depth // 2), BF16),
            pltpu.VMEM((4, cols // 2, total), F32),
            pltpu.VMEM((1, LANES), F32),
            pltpu.VMEM((devices, 1, LANES), F32),
            pltpu.SemaphoreType.DMA((1,)),
            pltpu.SemaphoreType.DMA((1,)),
            pltpu.SemaphoreType.DMA((1,)),
            pltpu.SemaphoreType.DMA((1,)),
            pltpu.SemaphoreType.DMA((1,)),
            pltpu.SemaphoreType.DMA((1,)),
            pltpu.SemaphoreType.DMA((1,)),
            pltpu.SemaphoreType.DMA((1,)),
        ],
        compiler_params=pltpu.CompilerParams(
            collective_id=0, has_side_effects=True, vmem_limit_bytes=58 * 2**20
        ),
    )(
        bias_grid.reshape(cells, depth),
        hill_slab.reshape(hill_row.shape),
        hill_row,
        hill_col,
        hill_depth,
        hill_level,
        hill_count,
        table,
    )


def full_kernel(
    slabs, walks, rows, cols,
    bias_ref, hills_ref, new_ref, top_ref,
    bias_high, bias_low, picked, tables, peak, peaks,
    b_send, b_recv, c_send, c_recv,
):
    devices = slabs * walks
    cells, depth = bias_ref.shape
    radius = 2 * rows
    grid_rows, grid_cols = slabs * rows, walks * cols
    slab = lax.axis_index("slab")
    walk = lax.axis_index("walk")
    me = slab * walks + walk
    first_row = (slab * rows).astype(F32)
    first_col = (walk * cols).astype(F32)
    place, steps = mesh_steps(slabs, walks)
    barrier = greet(place, steps)
    high, low = halves(bias_ref[...])
    bias_high[...] = high
    bias_low[...] = low

    def pick(sender, carry):
        part = hills_ref[sender]
        cell = (part[1:2] - first_row) * cols + part[2:3] - first_col
        owner = owner_of(part[1:2], part[2:3], rows, cols, slabs, walks)
        cell = jnp.where(owner == HERE, cell, -1.0)
        select = jnp.where(iota((depth, LANES), 0) == part[3:4], 1.0, 0.0).astype(BF16)
        lines = jnp.dot(bias_high[...], select, preferred_element_type=F32)
        lines = lines + jnp.dot(bias_low[...], select, preferred_element_type=F32)
        hit = iota((cells, LANES), 0) == cell
        value = jnp.sum(jnp.where(hit, lines, 0.0), axis=0, keepdims=True)
        picked[pl.ds(sender, 1), :] = jnp.exp(-value / TEMPER)
        return carry

    lax.fori_loop(0, devices, pick, 0)
    pl.semaphore_wait(barrier, devices - 1)
    for copy in to_near(picked, tables, b_send, b_recv, slabs, walks):
        copy.start()
    b_all = arrival(tables.at[pl.ds(0, len(OFFSETS) - 1)], b_send, b_recv, place)
    tables[HERE] = picked[...]
    b_all.wait_recv()
    new_ref[...] = bias_ref[...]

    def add(sender, carry):
        part = hills_ref[sender]
        owner = owner_of(part[1:2], part[2:3], rows, cols, slabs, walks)
        height = jnp.zeros((1, LANES), F32)
        for n in range(len(OFFSETS)):
            height = jnp.where(owner == n, part[0:1] * tables[n, pl.ds(sender, 1), :], height)
        at = as_column(part[3:4])[:, 0:1]
        right = profile(wrapped(iota((LANES, depth), 1) - at, depth), radius)
        right_high, right_low = halves(right)
        col_offset = iota((cols, LANES), 0) + first_col - part[2:3]
        near = profile(wrapped(col_offset, grid_cols), radius)
        for r in range(rows):
            along = profile(wrapped(first_row + r - part[1:2], grid_rows), radius)
            left_high, left_low = halves(near * (height * along))
            added = jnp.dot(left_high, right_high, preferred_element_type=F32)
            added += jnp.dot(left_low, right_high, preferred_element_type=F32)
            added += jnp.dot(left_high, right_low, preferred_element_type=F32)
            new_ref[r * cols : (r + 1) * cols, :] += added
        return carry

    lax.fori_loop(0, devices, add, 0)
    top = lane_tops(new_ref[...])
    peak[...] = top
    peaks[me] = top
    for copy in to_all(peak, peaks.at[me], c_send, c_recv, place, steps):
        copy.start()
    c_all = arrival(peaks.at[pl.ds(0, devices - 1)], c_send, c_recv, place)
    b_all.wait_send()
    c_all.wait_send()
    c_all.wait_recv()
    top_ref[...] = jnp.broadcast_to(jnp.max(peaks[...]), top_ref.shape)


def by_full_kernel(rows, slabs, walks, bias, hills):
    cells, depth = bias.shape
    devices = slabs * walks
    vmem = pl.BlockSpec(memory_space=pltpu.VMEM)
    return pl.pallas_call(
        functools.partial(full_kernel, slabs, walks, rows, cells // rows),
        out_shape=(
            jax.ShapeDtypeStruct((cells, depth), F32),
            jax.ShapeDtypeStruct((8, LANES), F32),
        ),
        in_specs=[vmem] * 2,
        out_specs=(vmem, vmem),
        scratch_shapes=[
            pltpu.VMEM((cells, depth), BF16),
            pltpu.VMEM((cells, depth), BF16),
            pltpu.VMEM((devices, LANES), F32),
            pltpu.VMEM((len(OFFSETS), devices, LANES), F32),
            pltpu.VMEM((1, LANES), F32),
            pltpu.VMEM((devices, 1, LANES), F32),
            pltpu.SemaphoreType.DMA((1,)),
            pltpu.SemaphoreType.DMA((1,)),
            pltpu.SemaphoreType.DMA((1,)),
            pltpu.SemaphoreType.DMA((1,)),
        ],
        compiler_params=pltpu.CompilerParams(
            collective_id=1, has_side_effects=True, vmem_limit_bytes=20 * 2**20
        ),
    )(bias, hills)


def output_kernel(new_ref, top_ref, new_out, free_out, free_ref, sems):
    parts = 2
    span = new_ref.shape[0] // parts
    first = pltpu.make_async_copy(new_ref, new_out, sems.at[0])
    first.start()
    for i in range(parts):
        rows = pl.ds(i * span, span)
        free_ref[rows, :] = FREE_SCALE * (top_ref[0:1, 0:1] - new_ref[rows, :])
        pltpu.make_async_copy(free_ref.at[rows], free_out.at[rows], sems.at[1]).start()
    first.wait()
    pltpu.make_async_copy(free_ref, free_out, sems.at[1]).wait()


def outputs(new_bias, top):
    hbm = pl.BlockSpec(memory_space=pltpu.HBM)
    return pl.pallas_call(
        output_kernel,
        out_shape=(jax.ShapeDtypeStruct(new_bias.shape, F32),) * 2,
        in_specs=[pl.BlockSpec(memory_space=pltpu.VMEM)] * 2,
        out_specs=(hbm, hbm),
        scratch_shapes=[pltpu.VMEM(new_bias.shape, F32), pltpu.SemaphoreType.DMA((2,))],
        compiler_params=pltpu.CompilerParams(vmem_limit_bytes=4 * 2**20),
    )(new_bias, top)


def per_device(*arrays):
    bias_grid = arrays[0]
    shape = bias_grid.shape
    slabs, walks = lax.axis_size("slab"), lax.axis_size("walk")
    devices = slabs * walks
    fits = (
        arrays[2].size == LANES
        and slabs >= 5
        and walks >= 3
        and devices <= 64
        and devices % 8 == 0
        and devices * shape[0] <= LANES
        and shape[1] % LANES == 0
        and shape[1] >= 2 * shape[0]
        and shape[2] % (4 * LANES) == 0
        and max(walks * shape[1], shape[2]) <= 4096
        and max(slabs * shape[0], arrays[7].size) <= 255
        and all(size & (size - 1) == 0 for size in (slabs, walks, shape[1], shape[2]))
        and devices * shape[0] * shape[1] * shape[2] <= 2**24
    )
    if not fits:
        return by_collectives(*arrays)

    def finish(new_bias, top):
        new_out, free_out = outputs(new_bias, top)
        return new_out.reshape(shape), free_out.reshape(shape)

    new_bias, top, bias, hills, flag = by_kernel(2, slabs, walks, arrays)
    return lax.cond(
        flag.reshape(()),
        lambda: finish(*by_full_kernel(shape[0], slabs, walks, bias, hills)),
        lambda: finish(new_bias, top),
    )


def solution(mesh):
    in_specs = (
        P("slab", "walk", None),
        P(("slab", "walk"), None, None),
        P(("slab", "walk"), None),
        P(("slab", "walk"), None),
        P(("slab", "walk"), None),
        P(("slab", "walk"), None),
        P(("slab", "walk")),
        P(),
    )
    out_specs = (P("slab", "walk", None), P("slab", "walk", None))
    return jax.shard_map(
        per_device, mesh=mesh, in_specs=in_specs, out_specs=out_specs, check_vma=False
    )
```

```python
import functools
import math

import jax
import jax.numpy as jnp
from jax import lax
from jax.experimental import pallas as pl
from jax.experimental.pallas import tpu as pltpu
from jax.sharding import PartitionSpec as P

BASE_HEIGHT = 1.2
TEMPER = 4.0
SIGMA_SHARE = 0.3125
FREE_SCALE = 10.0 / 9.0


def from_behind(block, axis, distance):
    devices = range(lax.axis_size(axis))
    route = [((i - distance) % len(devices), i) for i in devices]
    return lax.ppermute(block, axis, route)


def gaussian(position, centre, extent, radius):
    offset = jnp.mod(position - centre + extent // 2, extent) - extent // 2
    inside = (offset >= -radius) & (offset < radius)
    spread = SIGMA_SHARE * radius
    distance = offset.astype(jnp.float32)
    return jnp.where(inside, jnp.exp(-(distance * distance) / (2.0 * spread * spread)), 0.0)


def deposit(row_ids, col_ids, depth_ids, hill_lists, grid_rows, grid_cols, grid_depth, radius):
    slot_total = hill_lists.shape[1]
    block_size = math.gcd(slot_total, 256)
    row_count = row_ids.shape[0]
    col_count = col_ids.shape[0]
    depth_count = depth_ids.shape[0]

    def one_block(carry_sum, index):
        portion = lax.dynamic_slice_in_dim(hill_lists, index * block_size, block_size, 1)
        row_gauss = (
            gaussian(row_ids[:, None], portion[1].astype(jnp.int32)[None, :], grid_rows, radius)
            * portion[0][None, :]
        )
        col_gauss = gaussian(
            col_ids[:, None], portion[2].astype(jnp.int32)[None, :], grid_cols, radius
        )
        depth_gauss = gaussian(
            depth_ids[None, :], portion[3].astype(jnp.int32)[:, None], grid_depth, radius
        )
        plane_gauss = (row_gauss[:, None, :] * col_gauss[None, :, :]).reshape(
            row_count * col_count, block_size
        )
        added = jnp.dot(
            plane_gauss,
            depth_gauss,
            precision=lax.Precision.HIGHEST,
            preferred_element_type=jnp.float32,
        )
        return (carry_sum + added, None)

    start = jnp.zeros((row_count * col_count, depth_count), jnp.float32)
    result, unused = lax.scan(one_block, start, jnp.arange(slot_total // block_size))
    return result.reshape(row_count, col_count, depth_count)


def by_collectives(
    bias_grid, hill_slab, hill_row, hill_col, hill_depth, hill_level, hill_count, height_levels
):
    rows_dev, cols_dev, depth_bins = bias_grid.shape
    slab_count = lax.axis_size("slab")
    walk_count = lax.axis_size("walk")
    radius = 2 * rows_dev
    grid_rows = rows_dev * slab_count
    grid_cols = cols_dev * walk_count
    walkers_dev, hill_slots = hill_row.shape
    sent_rows = walkers_dev * hill_slots
    capacity = max(2, 4 * sent_rows // slab_count)
    target = hill_slab[:, :, 0].reshape(-1)
    centre_row = target * rows_dev + hill_row.reshape(-1)
    is_live = (
        lax.broadcasted_iota(jnp.int32, (walkers_dev, hill_slots), 1) < hill_count[:, None]
    ).reshape(-1)
    level_match = hill_level.reshape(-1)[:, None] == lax.broadcasted_iota(
        jnp.int32, (1, height_levels.shape[0]), 1
    )
    base_height = jnp.sum(jnp.where(level_match, height_levels[None, :], 0.0), axis=1)
    base_height = jnp.where(is_live, BASE_HEIGHT * base_height, 0.0)
    same_slab = target[:, None] == target[None, :]
    earlier = lax.broadcasted_iota(jnp.int32, (sent_rows, sent_rows), 1) < lax.broadcasted_iota(
        jnp.int32, (sent_rows, sent_rows), 0
    )
    slot_rank = jnp.sum((same_slab & earlier).astype(jnp.int32), axis=1)
    slot_place = target * capacity + slot_rank
    placing = (
        slot_place[:, None] == lax.broadcasted_iota(jnp.int32, (1, slab_count * capacity), 1)
    ).astype(jnp.float32)
    fields = jnp.stack(
        [
            base_height,
            centre_row.astype(jnp.float32),
            hill_col.reshape(-1).astype(jnp.float32),
            hill_depth.reshape(-1).astype(jnp.float32),
        ]
    )
    outgoing = jnp.dot(
        fields, placing, precision=lax.Precision.HIGHEST, preferred_element_type=jnp.float32
    )
    outgoing = outgoing.reshape(4, slab_count, capacity)
    arrived = lax.all_to_all(outgoing, "slab", split_axis=1, concat_axis=1, tiled=True).reshape(
        4, slab_count * capacity
    )
    shared = lax.all_gather(arrived, "walk", axis=1, tiled=True)
    slab_index = lax.axis_index("slab")
    walk_index = lax.axis_index("walk")
    local_row = jnp.clip(shared[1].astype(jnp.int32) - slab_index * rows_dev, 0, rows_dev - 1)
    local_col = shared[2].astype(jnp.int32) - walk_index * cols_dev
    local_depth = jnp.clip(shared[3].astype(jnp.int32), 0, depth_bins - 1)
    owned = (local_col >= 0) & (local_col < cols_dev)
    flat_place = (
        local_row * cols_dev + jnp.clip(local_col, 0, cols_dev - 1)
    ) * depth_bins + local_depth
    picked = bias_grid.reshape(-1)[flat_place]
    centre_value = lax.psum(jnp.where(owned, picked, 0.0), "walk")
    height = shared[0] * jnp.exp(-centre_value / TEMPER)
    hill_lists = jnp.stack([height, shared[1], shared[2], shared[3]])
    col_ids = walk_index * cols_dev + lax.broadcasted_iota(jnp.int32, (cols_dev,), 0)
    depth_ids = lax.broadcasted_iota(jnp.int32, (depth_bins,), 0)
    collected = [hill_lists]
    for offset in (-2, -1, 1, 2):
        collected.append(from_behind(hill_lists, "slab", offset))
    row_ids = slab_index * rows_dev + lax.broadcasted_iota(jnp.int32, (rows_dev,), 0)
    added = deposit(
        row_ids,
        col_ids,
        depth_ids,
        jnp.concatenate(collected, axis=1),
        grid_rows,
        grid_cols,
        depth_bins,
        radius,
    )
    new_bias = bias_grid + added
    highest = lax.pmax(jnp.max(new_bias), ("slab", "walk"))
    free_energy = FREE_SCALE * (highest - new_bias)
    return (new_bias, free_energy)


LANES = 128
F32 = jnp.float32
BF16 = jnp.bfloat16
MESH = pl.DeviceIdType.MESH
NT = (((1,), (1,)), ((), ()))


def wrapped(offset, extent):
    offset = jnp.where(offset >= extent // 2, offset - extent, offset)
    return jnp.where(offset < -(extent // 2), offset + extent, offset)


def profile(offset, radius):
    spread = SIGMA_SHARE * radius
    value = jnp.exp(-(offset * offset) / (2.0 * spread * spread))
    return jnp.where((offset >= -radius) & (offset < radius), value, 0.0)


def halves(value):
    high = value.astype(BF16)
    return high, (value - high.astype(F32)).astype(BF16)


def iota(shape, dim):
    return lax.broadcasted_iota(jnp.int32, shape, dim).astype(F32)


def whole_iota(shape, dim):
    return lax.broadcasted_iota(jnp.int32, shape, dim)


OFFSETS = [(i, j) for i in (-2, -1, 0, 1, 2) for j in (-1, 0, 1)]
HERE = OFFSETS.index((0, 0))


def flipped(index, extent):
    values = [index]
    bit = 1
    while bit < extent:
        turn = bit * (1 - 2 * lax.rem(index // bit, 2))
        values += [value + turn for value in values]
        bit *= 2
    return values


def mesh_steps(slabs, walks):
    slab_at = flipped(lax.axis_index("slab"), slabs)
    walk_at = flipped(lax.axis_index("walk"), walks)

    def place(step):
        return (slab_at[step // walks], walk_at[step % walks])

    return place, range(slabs * walks - 1, 0, -1)


def greet(place, steps):
    barrier = pltpu.get_barrier_semaphore()
    for step in steps:
        pl.semaphore_signal(barrier, inc=1, device_id=place(step), device_id_type=MESH)
    return barrier


def to_all(source, target, send, recv, place, steps):
    return [
        pltpu.make_async_remote_copy(
            source, target, send.at[0], recv.at[0],
            device_id=place(step), device_id_type=MESH,
        )
        for step in steps
    ]


def to_near(source, tables, send, recv, slabs, walks):
    slab, walk = lax.axis_index("slab"), lax.axis_index("walk")
    copies = []
    for n, (i, j) in sorted(enumerate(OFFSETS), key=lambda item: -abs(item[1][0])):
        if n == HERE:
            continue
        device = (lax.rem(slab - i + slabs, slabs), lax.rem(walk - j + walks, walks))
        copies.append(
            pltpu.make_async_remote_copy(
                source, tables.at[n], send.at[0], recv.at[0],
                device_id=device, device_id_type=MESH,
            )
        )
    return copies


def arrival(landing, send, recv, place):
    return pltpu.make_async_remote_copy(
        landing, landing, send.at[0], recv.at[0], device_id=place(1), device_id_type=MESH
    )


def owner_of(at_row, at_col, rows, cols, slabs, walks):
    slab_of = jnp.floor(at_row / rows) - lax.axis_index("slab").astype(F32)
    walk_of = jnp.floor(at_col / cols) - lax.axis_index("walk").astype(F32)
    slab_of = jnp.where(slab_of < -2, slab_of + slabs, slab_of)
    slab_of = jnp.where(slab_of > 2, slab_of - slabs, slab_of)
    walk_of = jnp.where(walk_of < -1, walk_of + walks, walk_of)
    walk_of = jnp.where(walk_of > 1, walk_of - walks, walk_of)
    inside = (jnp.abs(slab_of) <= 2) & (jnp.abs(walk_of) <= 1)
    return jnp.where(inside, (slab_of + 2) * 3 + walk_of + 1, -1.0)


def lane_tops(value):
    most = jnp.max(value, axis=0, keepdims=True)
    top = most[:, 0:LANES]
    for i in range(1, value.shape[1] // LANES):
        top = jnp.maximum(top, most[:, i * LANES : (i + 1) * LANES])
    return top


def as_column(row):
    return jnp.broadcast_to(row, (LANES, LANES)).T


def squeeze(mask, rank):
    lane = whole_iota(mask.shape, 1)
    code = (lane - rank.astype(jnp.int32)) * LANES + lane + LANES * LANES
    code = jnp.where(mask, code, 0)
    step = 1
    while step < LANES:
        came = pltpu.roll(code, LANES - step, axis=1)
        bit = step * LANES
        stays = jnp.where((code & bit) != 0, 0, code)
        code = jnp.where((came & bit) != 0, came, stays)
        step *= 2
    return code & (LANES - 1)


def window_kernel(
    slabs, walks, rows, cols, close_blocks,
    bias_in, slab_in, row_in, col_in, depth_in, level_in, count_in, table_in,
    new_ref, top_ref, bias_ref, hills_ref, flag_ref,
    slab_ref, row_ref, col_ref, depth_ref, level_ref, count_ref, table_ref, in_sems,
    mine, hills, bias_parts, picked, tables, chosen, left, right, near, peak, peaks,
    a_send, a_recv, h_send, h_recv, b_send, b_recv, c_send, c_recv,
):
    devices = slabs * walks
    cells, depth = bias_ref.shape
    radius = 2 * rows
    grid_rows, grid_cols = slabs * rows, walks * cols
    slab = lax.axis_index("slab")
    walk = lax.axis_index("walk")
    me = slab * walks + walk
    first_row = (slab * rows).astype(F32)
    first_col = (walk * cols).astype(F32)
    place, steps = mesh_steps(slabs, walks)
    barrier = greet(place, steps)

    def bucket_of(at_slab, at_row, at_col):
        owner = at_slab * walks + jnp.floor(at_col / cols)
        return owner * rows + at_row

    inputs = (
        (slab_in, slab_ref), (row_in, row_ref), (col_in, col_ref), (depth_in, depth_ref),
        (level_in, level_ref), (count_in, count_ref), (table_in, table_ref), (bias_in, bias_ref),
    )
    fetches = [
        pltpu.make_async_copy(there, here, in_sems.at[i])
        for i, (there, here) in enumerate(inputs)
    ]
    for fetch in fetches:
        fetch.start()
    for fetch in fetches[:-1]:
        fetch.wait()

    def in_row(ref):
        value = ref[...].astype(F32)
        return jnp.concatenate([value[i : i + 1] for i in range(value.shape[0])], axis=1)

    slots = row_ref.shape[1]
    lane = iota((1, LANES), 1)
    live = jnp.zeros((1, LANES), F32)
    for i in range(row_ref.shape[0]):
        inside = (lane >= i * slots) & (lane < i * slots + count_ref[i].astype(F32))
        live = jnp.where(inside, 1.0, live)
    target, centre_col, centre_depth = in_row(slab_ref), in_row(col_ref), in_row(depth_ref)
    bucket = bucket_of(target, in_row(row_ref), centre_col)
    key = jnp.where(live > 0, bucket, float(devices * rows)) * LANES + lane
    keys = as_column(key)
    ahead = jnp.sum(jnp.where(keys < key, 1.0, 0.0), axis=0, keepdims=True)
    first = lane * LANES
    inside = (keys >= first) & (keys < first + LANES)
    counts = jnp.sum(jnp.where(inside & (lane < devices * rows), 1.0, 0.0), axis=0, keepdims=True)
    col_high = jnp.floor(centre_col / 16.0)
    depth_high = jnp.floor(centre_depth / 16.0)
    unsorted = jnp.concatenate(
        [
            jnp.where(live > 0, in_row(level_ref) + 1.0, 0.0),
            target * rows + in_row(row_ref),
            col_high,
            centre_col - 16.0 * col_high,
            depth_high,
            centre_depth - 16.0 * depth_high,
            live,
            live,
        ],
        axis=0,
    ).astype(BF16)
    order = jnp.where(iota((LANES, LANES), 0) == ahead, 1.0, 0.0).astype(BF16)
    ordered = lax.dot_general(unsorted, order, NT, preferred_element_type=F32)
    level = ordered[0:1]
    base = jnp.zeros((1, LANES), F32)
    for i in range(table_ref.shape[0]):
        base = jnp.where(level == i + 1, BASE_HEIGHT * table_ref[i], base)
    fields = (
        counts,
        ordered[2:3] * 16.0 + ordered[3:4],
        ordered[4:5] * 16.0 + ordered[5:6],
        ordered[1:2],
        base,
    )
    for i, field in enumerate(fields):
        mine[i : i + 1, :] = field
        hills[me, i : i + 1, :] = field

    pl.semaphore_wait(barrier, devices - 1)
    others = pl.ds(0, devices - 1)
    places, heights = pl.ds(0, 3), pl.ds(3, 2)
    for copy in to_all(mine.at[places], hills.at[me, places], a_send, a_recv, place, steps):
        copy.start()
    a_all = arrival(hills.at[others, places], a_send, a_recv, place)
    for copy in to_all(mine.at[heights], hills.at[me, heights], h_send, h_recv, place, steps):
        copy.start()
    h_all = arrival(hills.at[others, heights], h_send, h_recv, place)

    fetches[-1].wait()
    high, low = halves(bias_ref[...])
    for part in range(rows):
        span = slice(part * cols, (part + 1) * cols)
        bias_parts[part, :, :depth] = high[span]
        bias_parts[part, :, depth:] = low[span]
    counting = jnp.concatenate(
        [
            jnp.where(iota((LANES, LANES), 0) < iota((LANES, LANES), 1), 1.0, 0.0),
            jnp.ones((LANES, LANES), F32),
        ],
        axis=1,
    ).astype(BF16)
    before = jnp.where(
        iota((devices, devices), 1) < iota((devices, devices), 0), 1.0, 0.0
    ).astype(BF16)
    lanes = whole_iota((devices, LANES), 1)

    a_all.wait_recv()

    counts, all_col, all_depth = [hills[:, i, :] for i in range(3)]

    exact = counts.astype(BF16)
    starts = jnp.dot(exact, counting[:, :LANES], preferred_element_type=F32)
    reached = jnp.dot(before, exact, preferred_element_type=F32)

    def listed(values, index, moved, count, blocks):
        taken = [jnp.take_along_axis(value, index, axis=1) for value in values]
        result = []
        for block in range(blocks):
            spot = moved + block * LANES
            valid = (spot >= 0) & (spot < count)
            result.append([jnp.sum(jnp.where(valid, t, 0.0), axis=0, keepdims=True) for t in taken])
        return result

    own_code = (all_col - first_col) * depth + all_depth
    own_over = jnp.zeros((devices, LANES), jnp.int32)
    for part in range(rows):
        here = jnp.full((devices, LANES), me * rows + part, jnp.int32)
        own_start, own_count, own_reached = [
            jnp.take_along_axis(value, here, axis=1).astype(jnp.int32)
            for value in (starts, counts, reached)
        ]
        own_over = jnp.maximum(own_over, own_reached + own_count - LANES)
        moved = lanes - own_reached
        (own_list,) = listed(
            [own_code], (own_start + moved) & (LANES - 1), moved, own_count, 1
        )
        code = own_list[0].astype(jnp.int32)
        at = code & (depth - 1)
        select = jnp.where(whole_iota((depth, LANES), 0) == at, 1.0, 0.0).astype(BF16)
        lines = jnp.dot(
            bias_parts[part], jnp.concatenate([select, select], axis=0),
            preferred_element_type=F32,
        )
        hit = whole_iota((cols, LANES), 0) == (code >> (depth.bit_length() - 1))
        value = jnp.sum(jnp.where(hit, lines, 0.0), axis=0, keepdims=True)
        picked[part : part + 1, :] = jnp.exp(-value / TEMPER)

    for copy in to_near(picked, tables, b_send, b_recv, slabs, walks):
        copy.start()
    b_all = arrival(tables.at[pl.ds(0, len(OFFSETS) - 1)], b_send, b_recv, place)
    h_all.wait_recv()
    all_row, all_base = hills[:, 3, :], hills[:, 4, :]
    there = all_base > 0
    owner = jnp.where(there, owner_of(all_row, all_col, rows, cols, slabs, walks), -1.0)
    a_all.wait_send()
    h_all.wait_send()

    def past(away, extent, limit):
        away = away + (radius - 1)
        away = jnp.where(away < 0, away + extent, away)
        away = jnp.where(away >= extent, away - extent, away)
        return away < limit

    half_cols, half_depth, total = cols // 2, depth // 2, close_blocks * LANES
    close_row = there & past(all_row - first_row, grid_rows, rows + 2 * radius - 1)
    quarters = [(a, b) for a in (0, 1) for b in (0, 1)]
    close = [
        close_row
        & past(all_col - first_col - a * half_cols, grid_cols, half_cols + 2 * radius - 1)
        & past(all_depth - b * half_depth, depth, half_depth + 2 * radius - 1)
        for a, b in quarters
    ]
    ones = jnp.concatenate([jnp.where(mask, 1.0, 0.0) for mask in close], axis=0)
    both = jnp.dot(ones.astype(BF16), counting, preferred_element_type=F32)
    close_count = jnp.concatenate(
        [both[q * devices : (q + 1) * devices, LANES:] for q in range(4)], axis=1
    )
    close_reached = jnp.dot(before, close_count.astype(BF16), preferred_element_type=F32)
    close_over = jnp.max(close_reached + close_count - total)
    over = jnp.maximum(jnp.max(own_over.astype(F32)), close_over)
    close_lane = squeeze(ones > 0, both[:, :LANES])
    all_slab = jnp.floor(all_row / rows)
    slab_row = all_row - all_slab * rows
    all_bucket = bucket_of(all_slab, slab_row, all_col).astype(jnp.int32)
    shift = jnp.take_along_axis(reached - starts, all_bucket, axis=1)
    spot_part = owner * rows + slab_row
    spot = lanes.astype(F32) + shift + spot_part * LANES
    position = (all_row * grid_cols + all_col) * depth + all_depth
    depth_lane = iota((LANES, LANES), 1)
    col_id = iota((half_cols, LANES), 0)
    depth_bits, col_bits = depth.bit_length() - 1, grid_cols.bit_length() - 1
    for q, (a, b) in enumerate(quarters):
        span = slice(q * LANES, (q + 1) * LANES)
        moved = lanes - close_reached[:, span].astype(jnp.int32)
        index = jnp.take_along_axis(
            close_lane[q * devices : (q + 1) * devices], moved & (LANES - 1), axis=1
        )
        lists = listed(
            [all_base, position, spot], index, moved, close_count[:, span].astype(jnp.int32),
            close_blocks,
        )
        for block, parts in enumerate(lists):
            code = parts[1].astype(jnp.int32)
            at_depth = (code & (depth - 1)).astype(F32)
            at_col = ((code >> depth_bits) & (grid_cols - 1)).astype(F32)
            at_row = (code >> (depth_bits + col_bits)).astype(F32)
            line = q * close_blocks + block
            for i, part in enumerate((parts[0], at_row, parts[2])):
                chosen[i, line : line + 1, :] = part
            at = as_column(at_depth)
            for i in range(half_depth // LANES):
                offset = depth_lane + (b * half_depth + i * LANES) - at
                high, low = halves(profile(wrapped(offset, depth), radius))
                for j, half in enumerate((high, high, low)):
                    rows_at = slice(j * total + block * LANES, j * total + (block + 1) * LANES)
                    right[q, rows_at, i * LANES : (i + 1) * LANES] = half
            offset = col_id + (first_col + a * half_cols) - at_col
            near[q, :, block * LANES : (block + 1) * LANES] = profile(
                wrapped(offset, grid_cols), radius
            )
    hills_ref[:, 0:1, :] = hills[:, 4:5, :]
    hills_ref[:, 1:2, :] = hills[:, 3:4, :]
    hills_ref[:, 2:4, :] = hills[:, 1:3, :]

    at_base, at_row = chosen[0], chosen[1]
    at_spot = chosen[2].astype(jnp.int32)
    at_lane = at_spot & (LANES - 1)
    at_table = at_spot >> (LANES.bit_length() - 1)
    row_parts = [
        at_base * profile(wrapped(first_row + r - at_row, grid_rows), radius) for r in range(rows)
    ]

    b_all.wait_recv()
    factor = jnp.zeros(at_base.shape, F32)
    left_half = whole_iota(at_base.shape, 0) < 2 * close_blocks
    for middle in range(1, len(OFFSETS), 3):
        for part in range(rows):
            lines = [
                jnp.broadcast_to(table[part : part + 1, :], factor.shape)
                for table in (
                    tables.at[middle - 1],
                    picked if middle == HERE else tables.at[middle],
                    tables.at[middle + 1],
                )
            ]
            code = middle * rows + part
            value = jnp.take_along_axis(lines[1], at_lane, axis=1)
            factor = jnp.where(at_table == code, value, factor)
            line = jnp.where(left_half, lines[0], lines[2])
            code = jnp.where(left_half, code - rows, code + rows)
            value = jnp.take_along_axis(line, at_lane, axis=1)
            factor = jnp.where(at_table == code, value, factor)
    row_parts = [factor * part for part in row_parts]
    tops = []
    for q, (a, b) in enumerate(quarters):
        for r in range(rows):
            for block in range(close_blocks):
                line = q * close_blocks + block
                span = slice(block * LANES, (block + 1) * LANES)
                high, low = halves(near[q, :, span] * row_parts[r][line : line + 1])
                for j, half in enumerate((high, low)):
                    lanes_at = slice(j * total + block * LANES, j * total + (block + 1) * LANES)
                    left[q, r * half_cols : (r + 1) * half_cols, lanes_at] = half
        added = jnp.dot(left[q], right[q, : 2 * total], preferred_element_type=F32)
        added += jnp.dot(left[q, :, :total], right[q, 2 * total :], preferred_element_type=F32)
        depths = slice(b * half_depth, (b + 1) * half_depth)
        for r in range(rows):
            first = r * cols + a * half_cols
            value = added[r * half_cols : (r + 1) * half_cols]
            value = bias_ref[first : first + half_cols, depths] + value
            new_ref[first : first + half_cols, depths] = value
            tops.append(lane_tops(value))
    top = jnp.where(over > 0, jnp.inf, functools.reduce(jnp.maximum, tops))
    peak[...] = top
    peaks[me] = top
    for copy in to_all(peak, peaks.at[me], c_send, c_recv, place, steps):
        copy.start()
    c_all = arrival(peaks.at[others], c_send, c_recv, place)
    b_all.wait_send()
    c_all.wait_send()
    c_all.wait_recv()
    highest = jnp.max(peaks[...])
    top_ref[...] = jnp.broadcast_to(highest, top_ref.shape)
    flag_ref[0] = jnp.where(highest == jnp.inf, 1, 0)


def by_kernel(close_blocks, slabs, walks, arrays):
    bias_grid, hill_slab, hill_row, hill_col, hill_depth, hill_level, hill_count, table = arrays
    rows, cols, depth = bias_grid.shape
    devices = slabs * walks
    total = close_blocks * LANES
    cells = rows * cols
    walkers = hill_row.shape
    vmem = pl.BlockSpec(memory_space=pltpu.VMEM)
    smem = pl.BlockSpec(memory_space=pltpu.SMEM)
    hbm = pl.BlockSpec(memory_space=pltpu.HBM)
    return pl.pallas_call(
        functools.partial(window_kernel, slabs, walks, rows, cols, close_blocks),
        out_shape=(
            jax.ShapeDtypeStruct((cells, depth), F32),
            jax.ShapeDtypeStruct((8, LANES), F32),
            jax.ShapeDtypeStruct((cells, depth), F32),
            jax.ShapeDtypeStruct((devices, 4, LANES), F32),
            jax.ShapeDtypeStruct((1,), jnp.int32),
        ),
        in_specs=[hbm] * 8,
        out_specs=(vmem, vmem, vmem, vmem, smem),
        scratch_shapes=[
            pltpu.VMEM(walkers, jnp.int32),
            pltpu.VMEM(walkers, jnp.int32),
            pltpu.VMEM(walkers, jnp.int32),
            pltpu.VMEM(walkers, jnp.int32),
            pltpu.VMEM(walkers, jnp.int32),
            pltpu.SMEM(hill_count.shape, jnp.int32),
            pltpu.SMEM(table.shape, F32),
            pltpu.SemaphoreType.DMA((8,)),
            pltpu.VMEM((8, LANES), F32),
            pltpu.VMEM((devices, 8, LANES), F32),
            pltpu.VMEM((rows, cols, 2 * depth), BF16),
            pltpu.VMEM((rows, LANES), F32),
            pltpu.VMEM((len(OFFSETS), rows, LANES), F32),
            pltpu.VMEM((3, 4 * close_blocks, LANES), F32),
            pltpu.VMEM((4, cells // 2, 2 * total), BF16),
            pltpu.VMEM((4, 3 * total, depth // 2), BF16),
            pltpu.VMEM((4, cols // 2, total), F32),
            pltpu.VMEM((1, LANES), F32),
            pltpu.VMEM((devices, 1, LANES), F32),
            pltpu.SemaphoreType.DMA((1,)),
            pltpu.SemaphoreType.DMA((1,)),
            pltpu.SemaphoreType.DMA((1,)),
            pltpu.SemaphoreType.DMA((1,)),
            pltpu.SemaphoreType.DMA((1,)),
            pltpu.SemaphoreType.DMA((1,)),
            pltpu.SemaphoreType.DMA((1,)),
            pltpu.SemaphoreType.DMA((1,)),
        ],
        compiler_params=pltpu.CompilerParams(
            collective_id=0, has_side_effects=True, vmem_limit_bytes=58 * 2**20
        ),
    )(
        bias_grid.reshape(cells, depth),
        hill_slab.reshape(hill_row.shape),
        hill_row,
        hill_col,
        hill_depth,
        hill_level,
        hill_count,
        table,
    )


def full_kernel(
    slabs, walks, rows, cols,
    bias_ref, hills_ref, new_ref, top_ref,
    bias_high, bias_low, picked, tables, peak, peaks,
    b_send, b_recv, c_send, c_recv,
):
    devices = slabs * walks
    cells, depth = bias_ref.shape
    radius = 2 * rows
    grid_rows, grid_cols = slabs * rows, walks * cols
    slab = lax.axis_index("slab")
    walk = lax.axis_index("walk")
    me = slab * walks + walk
    first_row = (slab * rows).astype(F32)
    first_col = (walk * cols).astype(F32)
    place, steps = mesh_steps(slabs, walks)
    barrier = greet(place, steps)
    high, low = halves(bias_ref[...])
    bias_high[...] = high
    bias_low[...] = low

    def pick(sender, carry):
        part = hills_ref[sender]
        cell = (part[1:2] - first_row) * cols + part[2:3] - first_col
        owner = owner_of(part[1:2], part[2:3], rows, cols, slabs, walks)
        cell = jnp.where(owner == HERE, cell, -1.0)
        select = jnp.where(iota((depth, LANES), 0) == part[3:4], 1.0, 0.0).astype(BF16)
        lines = jnp.dot(bias_high[...], select, preferred_element_type=F32)
        lines = lines + jnp.dot(bias_low[...], select, preferred_element_type=F32)
        hit = iota((cells, LANES), 0) == cell
        value = jnp.sum(jnp.where(hit, lines, 0.0), axis=0, keepdims=True)
        picked[pl.ds(sender, 1), :] = jnp.exp(-value / TEMPER)
        return carry

    lax.fori_loop(0, devices, pick, 0)
    pl.semaphore_wait(barrier, devices - 1)
    for copy in to_near(picked, tables, b_send, b_recv, slabs, walks):
        copy.start()
    b_all = arrival(tables.at[pl.ds(0, len(OFFSETS) - 1)], b_send, b_recv, place)
    tables[HERE] = picked[...]
    b_all.wait_recv()
    new_ref[...] = bias_ref[...]

    def add(sender, carry):
        part = hills_ref[sender]
        owner = owner_of(part[1:2], part[2:3], rows, cols, slabs, walks)
        height = jnp.zeros((1, LANES), F32)
        for n in range(len(OFFSETS)):
            height = jnp.where(owner == n, part[0:1] * tables[n, pl.ds(sender, 1), :], height)
        at = as_column(part[3:4])[:, 0:1]
        right = profile(wrapped(iota((LANES, depth), 1) - at, depth), radius)
        right_high, right_low = halves(right)
        col_offset = iota((cols, LANES), 0) + first_col - part[2:3]
        near = profile(wrapped(col_offset, grid_cols), radius)
        for r in range(rows):
            along = profile(wrapped(first_row + r - part[1:2], grid_rows), radius)
            left_high, left_low = halves(near * (height * along))
            added = jnp.dot(left_high, right_high, preferred_element_type=F32)
            added += jnp.dot(left_low, right_high, preferred_element_type=F32)
            added += jnp.dot(left_high, right_low, preferred_element_type=F32)
            new_ref[r * cols : (r + 1) * cols, :] += added
        return carry

    lax.fori_loop(0, devices, add, 0)
    top = lane_tops(new_ref[...])
    peak[...] = top
    peaks[me] = top
    for copy in to_all(peak, peaks.at[me], c_send, c_recv, place, steps):
        copy.start()
    c_all = arrival(peaks.at[pl.ds(0, devices - 1)], c_send, c_recv, place)
    b_all.wait_send()
    c_all.wait_send()
    c_all.wait_recv()
    top_ref[...] = jnp.broadcast_to(jnp.max(peaks[...]), top_ref.shape)


def by_full_kernel(rows, slabs, walks, bias, hills):
    cells, depth = bias.shape
    devices = slabs * walks
    vmem = pl.BlockSpec(memory_space=pltpu.VMEM)
    return pl.pallas_call(
        functools.partial(full_kernel, slabs, walks, rows, cells // rows),
        out_shape=(
            jax.ShapeDtypeStruct((cells, depth), F32),
            jax.ShapeDtypeStruct((8, LANES), F32),
        ),
        in_specs=[vmem] * 2,
        out_specs=(vmem, vmem),
        scratch_shapes=[
            pltpu.VMEM((cells, depth), BF16),
            pltpu.VMEM((cells, depth), BF16),
            pltpu.VMEM((devices, LANES), F32),
            pltpu.VMEM((len(OFFSETS), devices, LANES), F32),
            pltpu.VMEM((1, LANES), F32),
            pltpu.VMEM((devices, 1, LANES), F32),
            pltpu.SemaphoreType.DMA((1,)),
            pltpu.SemaphoreType.DMA((1,)),
            pltpu.SemaphoreType.DMA((1,)),
            pltpu.SemaphoreType.DMA((1,)),
        ],
        compiler_params=pltpu.CompilerParams(
            collective_id=1, has_side_effects=True, vmem_limit_bytes=20 * 2**20
        ),
    )(bias, hills)


def output_kernel(new_ref, top_ref, new_out, free_out, free_ref, sems):
    parts = 2
    span = new_ref.shape[0] // parts
    first = pltpu.make_async_copy(new_ref, new_out, sems.at[0])
    first.start()
    for i in range(parts):
        rows = pl.ds(i * span, span)
        free_ref[rows, :] = FREE_SCALE * (top_ref[0:1, 0:1] - new_ref[rows, :])
        pltpu.make_async_copy(free_ref.at[rows], free_out.at[rows], sems.at[1]).start()
    first.wait()
    pltpu.make_async_copy(free_ref, free_out, sems.at[1]).wait()


def outputs(new_bias, top):
    hbm = pl.BlockSpec(memory_space=pltpu.HBM)
    return pl.pallas_call(
        output_kernel,
        out_shape=(jax.ShapeDtypeStruct(new_bias.shape, F32),) * 2,
        in_specs=[pl.BlockSpec(memory_space=pltpu.VMEM)] * 2,
        out_specs=(hbm, hbm),
        scratch_shapes=[pltpu.VMEM(new_bias.shape, F32), pltpu.SemaphoreType.DMA((2,))],
        compiler_params=pltpu.CompilerParams(vmem_limit_bytes=4 * 2**20),
    )(new_bias, top)


def per_device(*arrays):
    bias_grid = arrays[0]
    shape = bias_grid.shape
    slabs, walks = lax.axis_size("slab"), lax.axis_size("walk")
    devices = slabs * walks
    fits = (
        arrays[2].size == LANES
        and slabs >= 5
        and walks >= 3
        and devices <= 64
        and devices % 8 == 0
        and devices * shape[0] <= LANES
        and shape[1] % LANES == 0
        and shape[1] >= 4 * shape[0]
        and shape[2] % (4 * LANES) == 0
        and max(walks * shape[1], shape[2]) <= 4096
        and max(slabs * shape[0], arrays[7].size) <= 255
        and all(size & (size - 1) == 0 for size in (slabs, walks, shape[1], shape[2]))
        and devices * shape[0] * shape[1] * shape[2] <= 2**24
    )
    if not fits:
        return by_collectives(*arrays)

    def finish(new_bias, top):
        new_out, free_out = outputs(new_bias, top)
        return new_out.reshape(shape), free_out.reshape(shape)

    new_bias, top, bias, hills, flag = by_kernel(2, slabs, walks, arrays)
    return lax.cond(
        flag.reshape(()),
        lambda: finish(*by_full_kernel(shape[0], slabs, walks, bias, hills)),
        lambda: finish(new_bias, top),
    )


def solution(mesh):
    in_specs = (
        P("slab", "walk", None),
        P(("slab", "walk"), None, None),
        P(("slab", "walk"), None),
        P(("slab", "walk"), None),
        P(("slab", "walk"), None),
        P(("slab", "walk"), None),
        P(("slab", "walk")),
        P(),
    )
    out_specs = (P("slab", "walk", None), P("slab", "walk", None))
    return jax.shard_map(
        per_device, mesh=mesh, in_specs=in_specs, out_specs=out_specs, check_vma=False
    )
```

```python
import functools
import math

import jax
import jax.numpy as jnp
from jax import lax
from jax.experimental import pallas as pl
from jax.experimental.pallas import tpu as pltpu
from jax.sharding import PartitionSpec as P

BASE_HEIGHT = 1.2
TEMPER = 4.0
SIGMA_SHARE = 0.3125
FREE_SCALE = 10.0 / 9.0


def from_behind(block, axis, distance):
    devices = range(lax.axis_size(axis))
    route = [((i - distance) % len(devices), i) for i in devices]
    return lax.ppermute(block, axis, route)


def gaussian(position, centre, extent, radius):
    offset = jnp.mod(position - centre + extent // 2, extent) - extent // 2
    inside = (offset >= -radius) & (offset < radius)
    spread = SIGMA_SHARE * radius
    distance = offset.astype(jnp.float32)
    return jnp.where(inside, jnp.exp(-(distance * distance) / (2.0 * spread * spread)), 0.0)


def deposit(row_ids, col_ids, depth_ids, hill_lists, grid_rows, grid_cols, grid_depth, radius):
    slot_total = hill_lists.shape[1]
    block_size = math.gcd(slot_total, 256)
    row_count = row_ids.shape[0]
    col_count = col_ids.shape[0]
    depth_count = depth_ids.shape[0]

    def one_block(carry_sum, index):
        portion = lax.dynamic_slice_in_dim(hill_lists, index * block_size, block_size, 1)
        row_gauss = (
            gaussian(row_ids[:, None], portion[1].astype(jnp.int32)[None, :], grid_rows, radius)
            * portion[0][None, :]
        )
        col_gauss = gaussian(
            col_ids[:, None], portion[2].astype(jnp.int32)[None, :], grid_cols, radius
        )
        depth_gauss = gaussian(
            depth_ids[None, :], portion[3].astype(jnp.int32)[:, None], grid_depth, radius
        )
        plane_gauss = (row_gauss[:, None, :] * col_gauss[None, :, :]).reshape(
            row_count * col_count, block_size
        )
        added = jnp.dot(
            plane_gauss,
            depth_gauss,
            precision=lax.Precision.HIGHEST,
            preferred_element_type=jnp.float32,
        )
        return (carry_sum + added, None)

    start = jnp.zeros((row_count * col_count, depth_count), jnp.float32)
    result, unused = lax.scan(one_block, start, jnp.arange(slot_total // block_size))
    return result.reshape(row_count, col_count, depth_count)


def by_collectives(
    bias_grid, hill_slab, hill_row, hill_col, hill_depth, hill_level, hill_count, height_levels
):
    rows_dev, cols_dev, depth_bins = bias_grid.shape
    slab_count = lax.axis_size("slab")
    walk_count = lax.axis_size("walk")
    radius = 2 * rows_dev
    grid_rows = rows_dev * slab_count
    grid_cols = cols_dev * walk_count
    walkers_dev, hill_slots = hill_row.shape
    sent_rows = walkers_dev * hill_slots
    capacity = max(2, 4 * sent_rows // slab_count)
    target = hill_slab[:, :, 0].reshape(-1)
    centre_row = target * rows_dev + hill_row.reshape(-1)
    is_live = (
        lax.broadcasted_iota(jnp.int32, (walkers_dev, hill_slots), 1) < hill_count[:, None]
    ).reshape(-1)
    level_match = hill_level.reshape(-1)[:, None] == lax.broadcasted_iota(
        jnp.int32, (1, height_levels.shape[0]), 1
    )
    base_height = jnp.sum(jnp.where(level_match, height_levels[None, :], 0.0), axis=1)
    base_height = jnp.where(is_live, BASE_HEIGHT * base_height, 0.0)
    same_slab = target[:, None] == target[None, :]
    earlier = lax.broadcasted_iota(jnp.int32, (sent_rows, sent_rows), 1) < lax.broadcasted_iota(
        jnp.int32, (sent_rows, sent_rows), 0
    )
    slot_rank = jnp.sum((same_slab & earlier).astype(jnp.int32), axis=1)
    slot_place = target * capacity + slot_rank
    placing = (
        slot_place[:, None] == lax.broadcasted_iota(jnp.int32, (1, slab_count * capacity), 1)
    ).astype(jnp.float32)
    fields = jnp.stack(
        [
            base_height,
            centre_row.astype(jnp.float32),
            hill_col.reshape(-1).astype(jnp.float32),
            hill_depth.reshape(-1).astype(jnp.float32),
        ]
    )
    outgoing = jnp.dot(
        fields, placing, precision=lax.Precision.HIGHEST, preferred_element_type=jnp.float32
    )
    outgoing = outgoing.reshape(4, slab_count, capacity)
    arrived = lax.all_to_all(outgoing, "slab", split_axis=1, concat_axis=1, tiled=True).reshape(
        4, slab_count * capacity
    )
    shared = lax.all_gather(arrived, "walk", axis=1, tiled=True)
    slab_index = lax.axis_index("slab")
    walk_index = lax.axis_index("walk")
    local_row = jnp.clip(shared[1].astype(jnp.int32) - slab_index * rows_dev, 0, rows_dev - 1)
    local_col = shared[2].astype(jnp.int32) - walk_index * cols_dev
    local_depth = jnp.clip(shared[3].astype(jnp.int32), 0, depth_bins - 1)
    owned = (local_col >= 0) & (local_col < cols_dev)
    flat_place = (
        local_row * cols_dev + jnp.clip(local_col, 0, cols_dev - 1)
    ) * depth_bins + local_depth
    picked = bias_grid.reshape(-1)[flat_place]
    centre_value = lax.psum(jnp.where(owned, picked, 0.0), "walk")
    height = shared[0] * jnp.exp(-centre_value / TEMPER)
    hill_lists = jnp.stack([height, shared[1], shared[2], shared[3]])
    col_ids = walk_index * cols_dev + lax.broadcasted_iota(jnp.int32, (cols_dev,), 0)
    depth_ids = lax.broadcasted_iota(jnp.int32, (depth_bins,), 0)
    collected = [hill_lists]
    for offset in (-2, -1, 1, 2):
        collected.append(from_behind(hill_lists, "slab", offset))
    row_ids = slab_index * rows_dev + lax.broadcasted_iota(jnp.int32, (rows_dev,), 0)
    added = deposit(
        row_ids,
        col_ids,
        depth_ids,
        jnp.concatenate(collected, axis=1),
        grid_rows,
        grid_cols,
        depth_bins,
        radius,
    )
    new_bias = bias_grid + added
    highest = lax.pmax(jnp.max(new_bias), ("slab", "walk"))
    free_energy = FREE_SCALE * (highest - new_bias)
    return (new_bias, free_energy)


LANES = 128
F32 = jnp.float32
BF16 = jnp.bfloat16
MESH = pl.DeviceIdType.MESH
NT = (((1,), (1,)), ((), ()))


def wrapped(offset, extent):
    offset = jnp.where(offset >= extent // 2, offset - extent, offset)
    return jnp.where(offset < -(extent // 2), offset + extent, offset)


def profile(offset, radius):
    spread = SIGMA_SHARE * radius
    value = jnp.exp(-(offset * offset) / (2.0 * spread * spread))
    return jnp.where((offset >= -radius) & (offset < radius), value, 0.0)


def halves(value):
    high = value.astype(BF16)
    return high, (value - high.astype(F32)).astype(BF16)


def iota(shape, dim):
    return lax.broadcasted_iota(jnp.int32, shape, dim).astype(F32)


def whole_iota(shape, dim):
    return lax.broadcasted_iota(jnp.int32, shape, dim)


OFFSETS = [(i, j) for i in (-2, -1, 0, 1, 2) for j in (-1, 0, 1)]
HERE = OFFSETS.index((0, 0))


def flipped(index, extent):
    values = [index]
    bit = 1
    while bit < extent:
        turn = bit * (1 - 2 * lax.rem(index // bit, 2))
        values += [value + turn for value in values]
        bit *= 2
    return values


def mesh_steps(slabs, walks):
    slab_at = flipped(lax.axis_index("slab"), slabs)
    walk_at = flipped(lax.axis_index("walk"), walks)

    def place(step):
        return (slab_at[step // walks], walk_at[step % walks])

    return place, range(slabs * walks - 1, 0, -1)


def greet(place, steps):
    barrier = pltpu.get_barrier_semaphore()
    for step in steps:
        pl.semaphore_signal(barrier, inc=1, device_id=place(step), device_id_type=MESH)
    return barrier


def to_all(source, target, send, recv, place, steps):
    return [
        pltpu.make_async_remote_copy(
            source, target, send.at[0], recv.at[0],
            device_id=place(step), device_id_type=MESH,
        )
        for step in steps
    ]


def to_near(source, tables, send, recv, slabs, walks):
    slab, walk = lax.axis_index("slab"), lax.axis_index("walk")
    copies = []
    for n, (i, j) in sorted(enumerate(OFFSETS), key=lambda item: -abs(item[1][0])):
        if n == HERE:
            continue
        device = (lax.rem(slab - i + slabs, slabs), lax.rem(walk - j + walks, walks))
        copies.append(
            pltpu.make_async_remote_copy(
                source, tables.at[n], send.at[0], recv.at[0],
                device_id=device, device_id_type=MESH,
            )
        )
    return copies


def arrival(landing, send, recv, place):
    return pltpu.make_async_remote_copy(
        landing, landing, send.at[0], recv.at[0], device_id=place(1), device_id_type=MESH
    )


def owner_of(at_row, at_col, rows, cols, slabs, walks):
    slab_of = jnp.floor(at_row / rows) - lax.axis_index("slab").astype(F32)
    walk_of = jnp.floor(at_col / cols) - lax.axis_index("walk").astype(F32)
    slab_of = jnp.where(slab_of < -2, slab_of + slabs, slab_of)
    slab_of = jnp.where(slab_of > 2, slab_of - slabs, slab_of)
    walk_of = jnp.where(walk_of < -1, walk_of + walks, walk_of)
    walk_of = jnp.where(walk_of > 1, walk_of - walks, walk_of)
    inside = (jnp.abs(slab_of) <= 2) & (jnp.abs(walk_of) <= 1)
    return jnp.where(inside, (slab_of + 2) * 3 + walk_of + 1, -1.0)


def lane_tops(value):
    most = jnp.max(value, axis=0, keepdims=True)
    top = most[:, 0:LANES]
    for i in range(1, value.shape[1] // LANES):
        top = jnp.maximum(top, most[:, i * LANES : (i + 1) * LANES])
    return top


def as_column(row):
    return jnp.broadcast_to(row, (LANES, LANES)).T


def squeeze(mask, rank):
    lane = whole_iota(mask.shape, 1)
    code = (lane - rank.astype(jnp.int32)) * LANES + lane + LANES * LANES
    code = jnp.where(mask, code, 0)
    step = 1
    while step < LANES:
        came = pltpu.roll(code, LANES - step, axis=1)
        bit = step * LANES
        stays = jnp.where((code & bit) != 0, 0, code)
        code = jnp.where((came & bit) != 0, came, stays)
        step *= 2
    return code & (LANES - 1)


def window_kernel(
    slabs, walks, rows, cols, close_blocks,
    bias_in, slab_in, row_in, col_in, depth_in, level_in, count_in, table_in,
    new_ref, top_ref, bias_ref, hills_ref, flag_ref,
    slab_ref, row_ref, col_ref, depth_ref, level_ref, count_ref, table_ref, in_sems,
    mine, hills, bias_parts, picked, tables, chosen, left, right, near, peak, peaks,
    a_send, a_recv, h_send, h_recv, b_send, b_recv, c_send, c_recv,
):
    devices = slabs * walks
    cells, depth = bias_ref.shape
    radius = 2 * rows
    grid_rows, grid_cols = slabs * rows, walks * cols
    slab = lax.axis_index("slab")
    walk = lax.axis_index("walk")
    me = slab * walks + walk
    first_row = (slab * rows).astype(F32)
    first_col = (walk * cols).astype(F32)
    place, steps = mesh_steps(slabs, walks)
    barrier = greet(place, steps)

    def bucket_of(at_slab, at_row, at_col):
        owner = at_slab * walks + jnp.floor(at_col / cols)
        return owner * rows + at_row

    inputs = (
        (slab_in, slab_ref), (row_in, row_ref), (col_in, col_ref), (depth_in, depth_ref),
        (level_in, level_ref), (count_in, count_ref), (table_in, table_ref), (bias_in, bias_ref),
    )
    fetches = [
        pltpu.make_async_copy(there, here, in_sems.at[i])
        for i, (there, here) in enumerate(inputs)
    ]
    for fetch in fetches:
        fetch.start()
    for fetch in fetches[:-1]:
        fetch.wait()

    def in_row(ref):
        value = ref[...].astype(F32)
        return jnp.concatenate([value[i : i + 1] for i in range(value.shape[0])], axis=1)

    slots = row_ref.shape[1]
    lane = iota((1, LANES), 1)
    live = jnp.zeros((1, LANES), F32)
    for i in range(row_ref.shape[0]):
        inside = (lane >= i * slots) & (lane < i * slots + count_ref[i].astype(F32))
        live = jnp.where(inside, 1.0, live)
    target, centre_col, centre_depth = in_row(slab_ref), in_row(col_ref), in_row(depth_ref)
    bucket = bucket_of(target, in_row(row_ref), centre_col)
    key = jnp.where(live > 0, bucket, float(devices * rows)) * LANES + lane
    keys = as_column(key)
    ahead = jnp.sum(jnp.where(keys < key, 1.0, 0.0), axis=0, keepdims=True)
    first = lane * LANES
    inside = (keys >= first) & (keys < first + LANES)
    counts = jnp.sum(jnp.where(inside & (lane < devices * rows), 1.0, 0.0), axis=0, keepdims=True)
    col_high = jnp.floor(centre_col / 16.0)
    depth_high = jnp.floor(centre_depth / 16.0)
    unsorted = jnp.concatenate(
        [
            jnp.where(live > 0, in_row(level_ref) + 1.0, 0.0),
            target * rows + in_row(row_ref),
            col_high,
            centre_col - 16.0 * col_high,
            depth_high,
            centre_depth - 16.0 * depth_high,
            live,
            live,
        ],
        axis=0,
    ).astype(BF16)
    order = jnp.where(iota((LANES, LANES), 0) == ahead, 1.0, 0.0).astype(BF16)
    ordered = lax.dot_general(unsorted, order, NT, preferred_element_type=F32)
    level = ordered[0:1]
    base = jnp.zeros((1, LANES), F32)
    for i in range(table_ref.shape[0]):
        base = jnp.where(level == i + 1, BASE_HEIGHT * table_ref[i], base)
    fields = (
        counts,
        ordered[2:3] * 16.0 + ordered[3:4],
        ordered[4:5] * 16.0 + ordered[5:6],
        ordered[1:2],
        base,
    )
    for i, field in enumerate(fields):
        mine[i : i + 1, :] = field
        hills[me, i : i + 1, :] = field

    pl.semaphore_wait(barrier, devices - 1)
    others = pl.ds(0, devices - 1)
    places, heights = pl.ds(0, 3), pl.ds(3, 2)
    for copy in to_all(mine.at[places], hills.at[me, places], a_send, a_recv, place, steps):
        copy.start()
    a_all = arrival(hills.at[others, places], a_send, a_recv, place)
    h_all = arrival(hills.at[others, heights], h_send, h_recv, place)

    fetches[-1].wait()
    high, low = halves(bias_ref[...])
    for part in range(rows):
        span = slice(part * cols, (part + 1) * cols)
        bias_parts[part, :, :depth] = high[span]
        bias_parts[part, :, depth:] = low[span]
    counting = jnp.concatenate(
        [
            jnp.where(iota((LANES, LANES), 0) < iota((LANES, LANES), 1), 1.0, 0.0),
            jnp.ones((LANES, LANES), F32),
        ],
        axis=1,
    ).astype(BF16)
    before = jnp.where(
        iota((devices, devices), 1) < iota((devices, devices), 0), 1.0, 0.0
    ).astype(BF16)
    lanes = whole_iota((devices, LANES), 1)

    for copy in to_all(mine.at[heights], hills.at[me, heights], h_send, h_recv, place, steps):
        copy.start()
    a_all.wait_recv()

    counts, all_col, all_depth = [hills[:, i, :] for i in range(3)]

    exact = counts.astype(BF16)
    starts = jnp.dot(exact, counting[:, :LANES], preferred_element_type=F32)
    reached = jnp.dot(before, exact, preferred_element_type=F32)

    def listed(values, index, moved, count, blocks):
        taken = [jnp.take_along_axis(value, index, axis=1) for value in values]
        result = []
        for block in range(blocks):
            spot = moved + block * LANES
            valid = (spot >= 0) & (spot < count)
            result.append([jnp.sum(jnp.where(valid, t, 0.0), axis=0, keepdims=True) for t in taken])
        return result

    own_code = (all_col - first_col) * depth + all_depth
    own_over = jnp.zeros((devices, LANES), jnp.int32)
    for part in range(rows):
        here = jnp.full((devices, LANES), me * rows + part, jnp.int32)
        own_start, own_count, own_reached = [
            jnp.take_along_axis(value, here, axis=1).astype(jnp.int32)
            for value in (starts, counts, reached)
        ]
        own_over = jnp.maximum(own_over, own_reached + own_count - LANES)
        moved = lanes - own_reached
        (own_list,) = listed(
            [own_code], (own_start + moved) & (LANES - 1), moved, own_count, 1
        )
        code = own_list[0].astype(jnp.int32)
        at = code & (depth - 1)
        select = jnp.where(whole_iota((depth, LANES), 0) == at, 1.0, 0.0).astype(BF16)
        lines = jnp.dot(
            bias_parts[part], jnp.concatenate([select, select], axis=0),
            preferred_element_type=F32,
        )
        hit = whole_iota((cols, LANES), 0) == (code >> (depth.bit_length() - 1))
        value = jnp.sum(jnp.where(hit, lines, 0.0), axis=0, keepdims=True)
        picked[part : part + 1, :] = jnp.exp(-value / TEMPER)

    for copy in to_near(picked, tables, b_send, b_recv, slabs, walks):
        copy.start()
    b_all = arrival(tables.at[pl.ds(0, len(OFFSETS) - 1)], b_send, b_recv, place)
    h_all.wait_recv()
    all_row, all_base = hills[:, 3, :], hills[:, 4, :]
    there = all_base > 0
    owner = jnp.where(there, owner_of(all_row, all_col, rows, cols, slabs, walks), -1.0)
    a_all.wait_send()
    h_all.wait_send()

    def past(away, extent, limit):
        away = away + (radius - 1)
        away = jnp.where(away < 0, away + extent, away)
        away = jnp.where(away >= extent, away - extent, away)
        return away < limit

    half_cols, half_depth, total = cols // 2, depth // 2, close_blocks * LANES
    close_row = there & past(all_row - first_row, grid_rows, rows + 2 * radius - 1)
    quarters = [(a, b) for a in (0, 1) for b in (0, 1)]
    close = [
        close_row
        & past(all_col - first_col - a * half_cols, grid_cols, half_cols + 2 * radius - 1)
        & past(all_depth - b * half_depth, depth, half_depth + 2 * radius - 1)
        for a, b in quarters
    ]
    ones = jnp.concatenate([jnp.where(mask, 1.0, 0.0) for mask in close], axis=0)
    both = jnp.dot(ones.astype(BF16), counting, preferred_element_type=F32)
    close_count = jnp.concatenate(
        [both[q * devices : (q + 1) * devices, LANES:] for q in range(4)], axis=1
    )
    close_reached = jnp.dot(before, close_count.astype(BF16), preferred_element_type=F32)
    close_over = jnp.max(close_reached + close_count - total)
    over = jnp.maximum(jnp.max(own_over.astype(F32)), close_over)
    close_lane = squeeze(ones > 0, both[:, :LANES])
    all_slab = jnp.floor(all_row / rows)
    slab_row = all_row - all_slab * rows
    all_bucket = bucket_of(all_slab, slab_row, all_col).astype(jnp.int32)
    shift = jnp.take_along_axis(reached - starts, all_bucket, axis=1)
    spot_part = owner * rows + slab_row
    spot = lanes.astype(F32) + shift + spot_part * LANES
    position = (all_row * grid_cols + all_col) * depth + all_depth
    depth_lane = iota((LANES, LANES), 1)
    col_id = iota((half_cols, LANES), 0)
    depth_bits, col_bits = depth.bit_length() - 1, grid_cols.bit_length() - 1
    for q, (a, b) in enumerate(quarters):
        span = slice(q * LANES, (q + 1) * LANES)
        moved = lanes - close_reached[:, span].astype(jnp.int32)
        index = jnp.take_along_axis(
            close_lane[q * devices : (q + 1) * devices], moved & (LANES - 1), axis=1
        )
        lists = listed(
            [all_base, position, spot], index, moved, close_count[:, span].astype(jnp.int32),
            close_blocks,
        )
        for block, parts in enumerate(lists):
            code = parts[1].astype(jnp.int32)
            at_depth = (code & (depth - 1)).astype(F32)
            at_col = ((code >> depth_bits) & (grid_cols - 1)).astype(F32)
            at_row = (code >> (depth_bits + col_bits)).astype(F32)
            line = q * close_blocks + block
            for i, part in enumerate((parts[0], at_row, parts[2])):
                chosen[i, line : line + 1, :] = part
            at = as_column(at_depth)
            for i in range(half_depth // LANES):
                offset = depth_lane + (b * half_depth + i * LANES) - at
                high, low = halves(profile(wrapped(offset, depth), radius))
                for j, half in enumerate((high, high, low)):
                    rows_at = slice(j * total + block * LANES, j * total + (block + 1) * LANES)
                    right[q, rows_at, i * LANES : (i + 1) * LANES] = half
            offset = col_id + (first_col + a * half_cols) - at_col
            near[q, :, block * LANES : (block + 1) * LANES] = profile(
                wrapped(offset, grid_cols), radius
            )
    hills_ref[:, 0:1, :] = hills[:, 4:5, :]
    hills_ref[:, 1:2, :] = hills[:, 3:4, :]
    hills_ref[:, 2:4, :] = hills[:, 1:3, :]

    at_base, at_row = chosen[0], chosen[1]
    at_spot = chosen[2].astype(jnp.int32)
    at_lane = at_spot & (LANES - 1)
    at_table = at_spot >> (LANES.bit_length() - 1)
    row_parts = [
        at_base * profile(wrapped(first_row + r - at_row, grid_rows), radius) for r in range(rows)
    ]

    b_all.wait_recv()
    factor = jnp.zeros(at_base.shape, F32)
    for n in range(len(OFFSETS)):
        for part in range(rows):
            table = picked if n == HERE else tables.at[n]
            line = jnp.broadcast_to(table[part : part + 1, :], factor.shape)
            value = jnp.take_along_axis(line, at_lane, axis=1)
            factor = jnp.where(at_table == n * rows + part, value, factor)
    row_parts = [factor * part for part in row_parts]
    tops = []
    for q, (a, b) in enumerate(quarters):
        for r in range(rows):
            for block in range(close_blocks):
                line = q * close_blocks + block
                span = slice(block * LANES, (block + 1) * LANES)
                high, low = halves(near[q, :, span] * row_parts[r][line : line + 1])
                for j, half in enumerate((high, low)):
                    lanes_at = slice(j * total + block * LANES, j * total + (block + 1) * LANES)
                    left[q, r * half_cols : (r + 1) * half_cols, lanes_at] = half
        added = jnp.dot(left[q], right[q, : 2 * total], preferred_element_type=F32)
        added += jnp.dot(left[q, :, :total], right[q, 2 * total :], preferred_element_type=F32)
        depths = slice(b * half_depth, (b + 1) * half_depth)
        for r in range(rows):
            first = r * cols + a * half_cols
            value = added[r * half_cols : (r + 1) * half_cols]
            value = bias_ref[first : first + half_cols, depths] + value
            new_ref[first : first + half_cols, depths] = value
            tops.append(lane_tops(value))
    top = jnp.where(over > 0, jnp.inf, functools.reduce(jnp.maximum, tops))
    peak[...] = top
    peaks[me] = top
    for copy in to_all(peak, peaks.at[me], c_send, c_recv, place, steps):
        copy.start()
    c_all = arrival(peaks.at[others], c_send, c_recv, place)
    b_all.wait_send()
    c_all.wait_send()
    c_all.wait_recv()
    highest = jnp.max(peaks[...])
    top_ref[...] = jnp.broadcast_to(highest, top_ref.shape)
    flag_ref[0] = jnp.where(highest == jnp.inf, 1, 0)


def by_kernel(close_blocks, slabs, walks, arrays):
    bias_grid, hill_slab, hill_row, hill_col, hill_depth, hill_level, hill_count, table = arrays
    rows, cols, depth = bias_grid.shape
    devices = slabs * walks
    total = close_blocks * LANES
    cells = rows * cols
    walkers = hill_row.shape
    vmem = pl.BlockSpec(memory_space=pltpu.VMEM)
    smem = pl.BlockSpec(memory_space=pltpu.SMEM)
    hbm = pl.BlockSpec(memory_space=pltpu.HBM)
    return pl.pallas_call(
        functools.partial(window_kernel, slabs, walks, rows, cols, close_blocks),
        out_shape=(
            jax.ShapeDtypeStruct((cells, depth), F32),
            jax.ShapeDtypeStruct((8, LANES), F32),
            jax.ShapeDtypeStruct((cells, depth), F32),
            jax.ShapeDtypeStruct((devices, 4, LANES), F32),
            jax.ShapeDtypeStruct((1,), jnp.int32),
        ),
        in_specs=[hbm] * 8,
        out_specs=(vmem, vmem, vmem, vmem, smem),
        scratch_shapes=[
            pltpu.VMEM(walkers, jnp.int32),
            pltpu.VMEM(walkers, jnp.int32),
            pltpu.VMEM(walkers, jnp.int32),
            pltpu.VMEM(walkers, jnp.int32),
            pltpu.VMEM(walkers, jnp.int32),
            pltpu.SMEM(hill_count.shape, jnp.int32),
            pltpu.SMEM(table.shape, F32),
            pltpu.SemaphoreType.DMA((8,)),
            pltpu.VMEM((8, LANES), F32),
            pltpu.VMEM((devices, 8, LANES), F32),
            pltpu.VMEM((rows, cols, 2 * depth), BF16),
            pltpu.VMEM((rows, LANES), F32),
            pltpu.VMEM((len(OFFSETS), rows, LANES), F32),
            pltpu.VMEM((3, 4 * close_blocks, LANES), F32),
            pltpu.VMEM((4, cells // 2, 2 * total), BF16),
            pltpu.VMEM((4, 3 * total, depth // 2), BF16),
            pltpu.VMEM((4, cols // 2, total), F32),
            pltpu.VMEM((1, LANES), F32),
            pltpu.VMEM((devices, 1, LANES), F32),
            pltpu.SemaphoreType.DMA((1,)),
            pltpu.SemaphoreType.DMA((1,)),
            pltpu.SemaphoreType.DMA((1,)),
            pltpu.SemaphoreType.DMA((1,)),
            pltpu.SemaphoreType.DMA((1,)),
            pltpu.SemaphoreType.DMA((1,)),
            pltpu.SemaphoreType.DMA((1,)),
            pltpu.SemaphoreType.DMA((1,)),
        ],
        compiler_params=pltpu.CompilerParams(
            collective_id=0, has_side_effects=True, vmem_limit_bytes=58 * 2**20
        ),
    )(
        bias_grid.reshape(cells, depth),
        hill_slab.reshape(hill_row.shape),
        hill_row,
        hill_col,
        hill_depth,
        hill_level,
        hill_count,
        table,
    )


def full_kernel(
    slabs, walks, rows, cols,
    bias_ref, hills_ref, new_ref, top_ref,
    bias_high, bias_low, picked, tables, peak, peaks,
    b_send, b_recv, c_send, c_recv,
):
    devices = slabs * walks
    cells, depth = bias_ref.shape
    radius = 2 * rows
    grid_rows, grid_cols = slabs * rows, walks * cols
    slab = lax.axis_index("slab")
    walk = lax.axis_index("walk")
    me = slab * walks + walk
    first_row = (slab * rows).astype(F32)
    first_col = (walk * cols).astype(F32)
    place, steps = mesh_steps(slabs, walks)
    barrier = greet(place, steps)
    high, low = halves(bias_ref[...])
    bias_high[...] = high
    bias_low[...] = low

    def pick(sender, carry):
        part = hills_ref[sender]
        cell = (part[1:2] - first_row) * cols + part[2:3] - first_col
        owner = owner_of(part[1:2], part[2:3], rows, cols, slabs, walks)
        cell = jnp.where(owner == HERE, cell, -1.0)
        select = jnp.where(iota((depth, LANES), 0) == part[3:4], 1.0, 0.0).astype(BF16)
        lines = jnp.dot(bias_high[...], select, preferred_element_type=F32)
        lines = lines + jnp.dot(bias_low[...], select, preferred_element_type=F32)
        hit = iota((cells, LANES), 0) == cell
        value = jnp.sum(jnp.where(hit, lines, 0.0), axis=0, keepdims=True)
        picked[pl.ds(sender, 1), :] = jnp.exp(-value / TEMPER)
        return carry

    lax.fori_loop(0, devices, pick, 0)
    pl.semaphore_wait(barrier, devices - 1)
    for copy in to_near(picked, tables, b_send, b_recv, slabs, walks):
        copy.start()
    b_all = arrival(tables.at[pl.ds(0, len(OFFSETS) - 1)], b_send, b_recv, place)
    tables[HERE] = picked[...]
    b_all.wait_recv()
    new_ref[...] = bias_ref[...]

    def add(sender, carry):
        part = hills_ref[sender]
        owner = owner_of(part[1:2], part[2:3], rows, cols, slabs, walks)
        height = jnp.zeros((1, LANES), F32)
        for n in range(len(OFFSETS)):
            height = jnp.where(owner == n, part[0:1] * tables[n, pl.ds(sender, 1), :], height)
        at = as_column(part[3:4])[:, 0:1]
        right = profile(wrapped(iota((LANES, depth), 1) - at, depth), radius)
        right_high, right_low = halves(right)
        col_offset = iota((cols, LANES), 0) + first_col - part[2:3]
        near = profile(wrapped(col_offset, grid_cols), radius)
        for r in range(rows):
            along = profile(wrapped(first_row + r - part[1:2], grid_rows), radius)
            left_high, left_low = halves(near * (height * along))
            added = jnp.dot(left_high, right_high, preferred_element_type=F32)
            added += jnp.dot(left_low, right_high, preferred_element_type=F32)
            added += jnp.dot(left_high, right_low, preferred_element_type=F32)
            new_ref[r * cols : (r + 1) * cols, :] += added
        return carry

    lax.fori_loop(0, devices, add, 0)
    top = lane_tops(new_ref[...])
    peak[...] = top
    peaks[me] = top
    for copy in to_all(peak, peaks.at[me], c_send, c_recv, place, steps):
        copy.start()
    c_all = arrival(peaks.at[pl.ds(0, devices - 1)], c_send, c_recv, place)
    b_all.wait_send()
    c_all.wait_send()
    c_all.wait_recv()
    top_ref[...] = jnp.broadcast_to(jnp.max(peaks[...]), top_ref.shape)


def by_full_kernel(rows, slabs, walks, bias, hills):
    cells, depth = bias.shape
    devices = slabs * walks
    vmem = pl.BlockSpec(memory_space=pltpu.VMEM)
    return pl.pallas_call(
        functools.partial(full_kernel, slabs, walks, rows, cells // rows),
        out_shape=(
            jax.ShapeDtypeStruct((cells, depth), F32),
            jax.ShapeDtypeStruct((8, LANES), F32),
        ),
        in_specs=[vmem] * 2,
        out_specs=(vmem, vmem),
        scratch_shapes=[
            pltpu.VMEM((cells, depth), BF16),
            pltpu.VMEM((cells, depth), BF16),
            pltpu.VMEM((devices, LANES), F32),
            pltpu.VMEM((len(OFFSETS), devices, LANES), F32),
            pltpu.VMEM((1, LANES), F32),
            pltpu.VMEM((devices, 1, LANES), F32),
            pltpu.SemaphoreType.DMA((1,)),
            pltpu.SemaphoreType.DMA((1,)),
            pltpu.SemaphoreType.DMA((1,)),
            pltpu.SemaphoreType.DMA((1,)),
        ],
        compiler_params=pltpu.CompilerParams(
            collective_id=1, has_side_effects=True, vmem_limit_bytes=20 * 2**20
        ),
    )(bias, hills)


def output_kernel(new_ref, top_ref, new_out, free_out, free_ref, sems):
    parts = 2
    span = new_ref.shape[0] // parts
    first = pltpu.make_async_copy(new_ref, new_out, sems.at[0])
    first.start()
    for i in range(parts):
        rows = pl.ds(i * span, span)
        free_ref[rows, :] = FREE_SCALE * (top_ref[0:1, 0:1] - new_ref[rows, :])
        pltpu.make_async_copy(free_ref.at[rows], free_out.at[rows], sems.at[1]).start()
    first.wait()
    pltpu.make_async_copy(free_ref, free_out, sems.at[1]).wait()


def outputs(new_bias, top):
    hbm = pl.BlockSpec(memory_space=pltpu.HBM)
    return pl.pallas_call(
        output_kernel,
        out_shape=(jax.ShapeDtypeStruct(new_bias.shape, F32),) * 2,
        in_specs=[pl.BlockSpec(memory_space=pltpu.VMEM)] * 2,
        out_specs=(hbm, hbm),
        scratch_shapes=[pltpu.VMEM(new_bias.shape, F32), pltpu.SemaphoreType.DMA((2,))],
        compiler_params=pltpu.CompilerParams(vmem_limit_bytes=4 * 2**20),
    )(new_bias, top)


def per_device(*arrays):
    bias_grid = arrays[0]
    shape = bias_grid.shape
    slabs, walks = lax.axis_size("slab"), lax.axis_size("walk")
    devices = slabs * walks
    fits = (
        arrays[2].size == LANES
        and slabs >= 5
        and walks >= 3
        and devices <= 64
        and devices % 8 == 0
        and devices * shape[0] <= LANES
        and shape[1] % LANES == 0
        and shape[1] >= 2 * shape[0]
        and shape[2] % (4 * LANES) == 0
        and max(walks * shape[1], shape[2]) <= 4096
        and max(slabs * shape[0], arrays[7].size) <= 255
        and all(size & (size - 1) == 0 for size in (slabs, walks, shape[1], shape[2]))
        and devices * shape[0] * shape[1] * shape[2] <= 2**24
    )
    if not fits:
        return by_collectives(*arrays)

    def finish(new_bias, top):
        new_out, free_out = outputs(new_bias, top)
        return new_out.reshape(shape), free_out.reshape(shape)

    new_bias, top, bias, hills, flag = by_kernel(2, slabs, walks, arrays)
    return lax.cond(
        flag.reshape(()),
        lambda: finish(*by_full_kernel(shape[0], slabs, walks, bias, hills)),
        lambda: finish(new_bias, top),
    )


def solution(mesh):
    in_specs = (
        P("slab", "walk", None),
        P(("slab", "walk"), None, None),
        P(("slab", "walk"), None),
        P(("slab", "walk"), None),
        P(("slab", "walk"), None),
        P(("slab", "walk"), None),
        P(("slab", "walk")),
        P(),
    )
    out_specs = (P("slab", "walk", None), P("slab", "walk", None))
    return jax.shard_map(
        per_device, mesh=mesh, in_specs=in_specs, out_specs=out_specs, check_vma=False
    )
```
